1024 devices in a mesh: grp: 64 (over z, x), mem: 16 (over y, core).
Axes of the slice: x: 8, y: 8, z: 8, core: 2. Of those that a mesh axis runs over, the one named last changes fastest.
Arguments:
- state: float32 [3, 4096, 16, 128], P(None, ('grp', 'mem')), may hold values from -0.18 to 0.18
- direction: float32 [3, 4096, 16, 128], P(None, ('grp', 'mem')), may hold values from -0.6 to 0.6
- rhs: float32 [3, 4096, 16, 128], P(None, ('grp', 'mem')), may hold values from -6 to 6
- clamp: int32 [4096, 16], P(('grp', 'mem')), may hold values 0 or 1
- stiffness: float32 [1024, 4, 32], P(('grp', 'mem')), may hold values from 0.5 to 5
- coarse_owner: int32 [1024, 128], P(('grp', 'mem')), may hold values from 0 to 127, as said below
- coarse_inverse: float32 [1024, 2, 192, 192], P(('grp', 'mem')), may hold values from -0.006 to 0.006
Outputs:
- new_direction: float32 [3, 4096, 16, 128], P(None, ('grp', 'mem'))
- residual: float32 [3, 4096, 16, 128], P(None, ('grp', 'mem'))
- coarse_residual: float32 [3, 1024, 4, 32], P(None, ('grp', 'mem'))
The draws below stay inside these ranges and needn't reach their ends.
Inputs may be any that keep to these rules, and one draw needn't show every extreme that they name: `coarse_owner`: each layer's row is a permutation of 0 to 127.
All inputs are finite; a program needn't handle non-finite values. No bound on the sum of `clamp` on one device may be relied on, other than what follows from the above.
Results may differ from the reference program's by a relative error of at most 0.0003.
Values sent between devices are 32-bit elements; how exact they have to be, the bound alone decides.
No kernel may reach another device: no remote copies, remote signals or barrier semaphores. Data moves between devices by JAX's collectives and lax.ppermute only.
A program may use at most 32 MiB of HBM per device.

```python
import math
import jax
import jax.numpy as jnp
import numpy as np
from jax import lax

EY = 4
EZ = 32
VB = 64
LAYERS = 1024
NBLK = 2
N_GRP = 64


def draw_coarse_owner(key, part):
    row_keys = jax.random.split(key, LAYERS)
    return jax.vmap(lambda k: jax.random.permutation(k, EY * EZ))(row_keys).astype(jnp.int32)


def set_ends(values, rng, low, high):
    shape = values.shape
    index_at = [jax.random.randint(jax.random.fold_in(rng, axis), (), 0, shape[axis]) for axis in range(len(shape))]
    values = values.at[tuple(index_at)].set(low)
    longest = shape.index(max(shape))
    index_at[longest] = (index_at[longest] + 1) % shape[longest]
    return values.at[tuple(index_at)].set(high)


def shard_levels(stream_key, extent, shards, smallest, high):
    level = 1.0
    for position, shards_of in shards:
        steps = jax.random.uniform(jax.random.fold_in(jax.random.fold_in(stream_key, 6), position), (shards_of,), jnp.float32, smallest / len(shards), high / len(shards))
        level = level * jnp.repeat(jnp.exp(steps), extent[position] // shards_of).reshape((-1,) + (1,) * (len(extent) - 1 - position))
    return level


def centred(rng, extent, scale, reach, cuts=(), kind=jnp.bfloat16):
    values = jax.random.normal(rng, extent, jnp.float32) * scale
    if len(cuts) > 0:
        values = shard_levels(rng, extent, cuts, -0.22, 0.18) * values
    return jnp.clip(values, min=-reach, max=reach).astype(kind)


def setup_inputs(seed: int = 0) -> dict:
    seeds = jax.random.split(jax.random.key(seed), 8)
    state = centred(seeds[0], (3, 4 * LAYERS, 4 * EY, 4 * EZ), 0.03, 0.18, ((1, 1024),), jnp.float32)
    direction = centred(seeds[1], (3, 4 * LAYERS, 4 * EY, 4 * EZ), 0.1, 0.6, ((1, 1024),), jnp.float32)
    rhs = centred(seeds[2], (3, 4 * LAYERS, 4 * EY, 4 * EZ), 1.0, 6.0, ((1, 1024),), jnp.float32)
    clamp = set_ends((jax.random.randint(seeds[3], (4 * LAYERS, 4 * EY), 0, 4) < 1).astype(jnp.int32), jax.random.fold_in(seeds[3], 1), 0, 1)
    stiffness = jnp.clip(jnp.exp(math.log(5.0) - 2.3025851 * jax.random.uniform(seeds[4], (LAYERS, EY, EZ), jnp.float32) ** shard_levels(seeds[4], (LAYERS, EY, EZ), ((0, 1024),), -0.2, 0.2)), 0.5, 5.0)
    coarse_owner = draw_coarse_owner(jax.random.fold_in(seeds[7], 71), 0)
    coarse_inverse = centred(seeds[6], (LAYERS, NBLK, 3 * VB, 3 * VB), 0.001, 0.006, ((0, 1024),), jnp.float32)
    return {"state": state, "direction": direction, "rhs": rhs, "clamp": clamp, "stiffness": stiffness, "coarse_owner": coarse_owner, "coarse_inverse": coarse_inverse}


LAME_FIRST = 1.2
LAME_SHEAR = 0.8
HIGHEST = lax.Precision.HIGHEST

def gauss_rule():
    inner = np.sqrt(5.0 - 2.0 * np.sqrt(10.0 / 7.0)) / 3.0
    outer = np.sqrt(5.0 + 2.0 * np.sqrt(10.0 / 7.0)) / 3.0
    inner_weight = (322.0 + 13.0 * np.sqrt(70.0)) / 900.0
    outer_weight = (322.0 - 13.0 * np.sqrt(70.0)) / 900.0
    points = np.array([-outer, -inner, 0.0, inner, outer])
    weights = np.array([outer_weight, inner_weight, 128.0 / 225.0, inner_weight, outer_weight])
    return (points, weights)

def basis_tables():
    gll_points = np.array([-1.0, -np.sqrt(3.0 / 7.0), 0.0, np.sqrt(3.0 / 7.0), 1.0])
    gauss_points, gauss_weights = gauss_rule()
    values = np.zeros((5, 5))
    slopes = np.zeros((5, 5))
    for j in range(5):
        others = [gll_points[k] for k in range(5) if k != j]
        denominator = np.prod([gll_points[j] - o for o in others])
        for q in range(5):
            t = gauss_points[q]
            values[q, j] = np.prod([t - o for o in others]) / denominator
            total = 0.0
            for i in range(4):
                total += np.prod([t - others[k] for k in range(4) if k != i])
            slopes[q, j] = 2.0 * total / denominator
    return (gll_points, gauss_weights, values, slopes)

def banded(table, count):
    banded_matrix = np.zeros((5 * count, 4 * count + 1))
    for e in range(count):
        banded_matrix[5 * e:5 * e + 5, 4 * e:4 * e + 5] = table
    return banded_matrix

def restrictor(gll_points, count):
    result = np.zeros((count, 4 * count))
    for e in range(count):
        for j in range(4):
            result[e, 4 * e + j] += (1.0 - gll_points[j]) / 2.0
            if e + 1 < count:
                result[e + 1, 4 * e + j] += (1.0 + gll_points[j]) / 2.0
    return result

def operators(count_y, count_z):
    gll_points, gauss_weights, values, slopes = basis_tables()
    return (jnp.asarray(values, jnp.float32), jnp.asarray(slopes, jnp.float32), jnp.asarray(banded(values, count_y), jnp.float32), jnp.asarray(banded(slopes, count_y), jnp.float32), jnp.asarray(banded(values, count_z), jnp.float32), jnp.asarray(banded(slopes, count_z), jnp.float32))

def gradient(field, mats, low, high):
    basis_x, slope_x, basis_y, slope_y, basis_z, slope_z = mats
    basis_x = basis_x[:, low:high]
    slope_x = slope_x[:, low:high]
    along_b = jnp.einsum('cxyz,qz->cxyq', field, basis_z, precision=HIGHEST)
    along_d = jnp.einsum('cxyz,qz->cxyq', field, slope_z, precision=HIGHEST)
    plain_b = jnp.einsum('cxyq,py->cxpq', along_b, basis_y, precision=HIGHEST)
    sloped_b = jnp.einsum('cxyq,py->cxpq', along_b, slope_y, precision=HIGHEST)
    plain_d = jnp.einsum('cxyq,py->cxpq', along_d, basis_y, precision=HIGHEST)
    grad_x = jnp.einsum('cxpq,rx->crpq', plain_b, slope_x, precision=HIGHEST)
    grad_y = jnp.einsum('cxpq,rx->crpq', sloped_b, basis_x, precision=HIGHEST)
    grad_z = jnp.einsum('cxpq,rx->crpq', plain_d, basis_x, precision=HIGHEST)
    return (grad_x, grad_y, grad_z)

def divergence(fluxes, mats):
    basis_x, slope_x, basis_y, slope_y, basis_z, slope_z = mats
    part_x = jnp.einsum('crpq,rx->cxpq', fluxes[0], slope_x, precision=HIGHEST)
    part_y = jnp.einsum('crpq,rx->cxpq', fluxes[1], basis_x, precision=HIGHEST)
    part_z = jnp.einsum('crpq,rx->cxpq', fluxes[2], basis_x, precision=HIGHEST)
    side_b = jnp.einsum('cxpq,py->cxyq', part_x, basis_y, precision=HIGHEST) + jnp.einsum('cxpq,py->cxyq', part_y, slope_y, precision=HIGHEST)
    side_d = jnp.einsum('cxpq,py->cxyq', part_z, basis_y, precision=HIGHEST)
    return jnp.einsum('cxyq,qz->cxyz', side_b, basis_z, precision=HIGHEST) + jnp.einsum('cxyq,qz->cxyz', side_d, slope_z, precision=HIGHEST)

def state_terms(gradients):
    deform = [[gradients[a][c] + (1.0 if c == a else 0.0) for a in range(3)] for c in range(3)]
    strain = [[0.5 * (deform[0][a] * deform[0][b] + deform[1][a] * deform[1][b] + deform[2][a] * deform[2][b]) - (0.5 if a == b else 0.0) for b in range(3)] for a in range(3)]
    strain_trace = strain[0][0] + strain[1][1] + strain[2][2]
    stress = [[2.0 * LAME_SHEAR * strain[a][b] + (LAME_FIRST * strain_trace if a == b else 0.0) for b in range(3)] for a in range(3)]
    return (deform, stress)

def tangent_flux(gradients, deform, stress, weighting):
    change = [[gradients[a][c] for a in range(3)] for c in range(3)]
    cross_terms = [[deform[0][a] * change[0][b] + deform[1][a] * change[1][b] + deform[2][a] * change[2][b] for b in range(3)] for a in range(3)]
    strain_change = [[0.5 * (cross_terms[a][b] + cross_terms[b][a]) for b in range(3)] for a in range(3)]
    trace_change = strain_change[0][0] + strain_change[1][1] + strain_change[2][2]
    stress_change = [[2.0 * LAME_SHEAR * strain_change[a][b] + (LAME_FIRST * trace_change if a == b else 0.0) for b in range(3)] for a in range(3)]
    fluxes = []
    for a in range(3):
        rows_of = []
        for c in range(3):
            entry = change[c][0] * stress[0][a] + change[c][1] * stress[1][a] + change[c][2] * stress[2][a] + deform[c][0] * stress_change[0][a] + deform[c][1] * stress_change[1][a] + deform[c][2] * stress_change[2][a]
            rows_of.append(entry * weighting)
        fluxes.append(jnp.stack(rows_of))
    return fluxes

def quad_weighting(element_stiffness, gauss_weights):
    count_y, count_z = element_stiffness.shape
    spread = jnp.repeat(jnp.repeat(element_stiffness, 5, axis=0), 5, axis=1)
    weight_y = np.tile(gauss_weights, count_y)
    weight_z = np.tile(gauss_weights, count_z)
    quadrature = gauss_weights[:, None, None] * weight_y[None, :, None] * weight_z[None, None, :] / 8.0
    return spread[None] * jnp.asarray(quadrature, jnp.float32)

def reference(state, direction, rhs, clamp, stiffness, coarse_owner, coarse_inverse):
    layers, count_y, count_z = stiffness.shape
    mats = operators(count_y, count_z)
    gll_points, gauss_weights, values, slopes = basis_tables()
    low_hat = jnp.asarray((1.0 - gll_points[:4]) / 2.0, jnp.float32)
    high_hat = jnp.asarray((1.0 + gll_points[:4]) / 2.0, jnp.float32)
    hat_y = jnp.asarray(restrictor(gll_points, count_y), jnp.float32)
    hat_z = jnp.asarray(restrictor(gll_points, count_z), jnp.float32)
    bottom = (jnp.arange(4 * count_z) == 0).astype(jnp.float32)
    keep = 1.0 - clamp.astype(jnp.float32)[:, :, None] * bottom[None, None, :]
    padded_state = jnp.pad(state, ((0, 0), (0, 1), (0, 1), (0, 1)))

    def apply_all(field):
        padded_field = jnp.pad(keep * field, ((0, 0), (0, 1), (0, 1), (0, 1)))

        def one_layer(e):
            start = (4 * e).astype(jnp.int32)
            piece = lax.dynamic_slice_in_dim(padded_field, start, 5, 1)
            state_piece = lax.dynamic_slice_in_dim(padded_state, start, 5, 1)
            element_stiffness = lax.dynamic_index_in_dim(stiffness, e, 0, keepdims=False)
            terms = state_terms(gradient(state_piece, mats, 0, 5))
            fluxes = tangent_flux(gradient(piece, mats, 0, 5), terms[0], terms[1], quad_weighting(element_stiffness, gauss_weights))
            return divergence(fluxes, mats)[:, :, :-1, :-1]
        images = lax.map(one_layer, jnp.arange(layers, dtype=jnp.int32))
        carried = jnp.concatenate([jnp.zeros_like(images[:1, :, 4]), images[:-1, :, 4]], axis=0)
        own_part = images[:, :, :4].at[:, :, 0].add(carried)
        return own_part.transpose(1, 0, 2, 3, 4).reshape(3, 4 * layers, 4 * count_y, 4 * count_z)

    def restrict(field):
        grouped = field.reshape(3, layers, 4, 4 * count_y, 4 * count_z)
        coarse_terms = jnp.einsum('cejyz,vy,wz->cejvw', grouped, hat_y, hat_z, precision=HIGHEST)
        own_part = jnp.einsum('cejvw,j->cevw', coarse_terms, low_hat, precision=HIGHEST)
        onward = jnp.einsum('cejvw,j->cevw', coarse_terms, high_hat, precision=HIGHEST)
        return own_part + jnp.concatenate([jnp.zeros_like(onward[:, :1]), onward[:, :-1]], axis=1)
    image = apply_all(direction)
    first = rhs - keep * image - (1.0 - keep) * direction
    restricted = restrict(first)
    members = layers // N_GRP
    message = count_y * count_z // N_GRP
    per_layer = restricted.transpose(1, 0, 2, 3).reshape(layers, 3, count_y * count_z)
    outgoing = jax.vmap(lambda row, slots: jnp.zeros_like(row).at[:, slots].set(row))(per_layer, coarse_owner)
    gathered = outgoing.reshape(N_GRP, members, 3, N_GRP, message).transpose(3, 1, 2, 0, 4)
    gathered = gathered.reshape(layers, 3, count_y * count_z)
    blocks = coarse_inverse.shape[1]
    block_size = coarse_inverse.shape[2] // 3
    stacked = gathered.reshape(layers, 3, blocks, block_size).transpose(0, 2, 1, 3)
    stacked = stacked.reshape(layers, blocks, 3 * block_size)
    solved = jnp.einsum('lkij,lkj->lki', coarse_inverse, stacked, precision=HIGHEST)
    solved = solved.reshape(layers, blocks, 3, block_size).transpose(0, 2, 1, 3)
    solved = solved.reshape(layers, 3, count_y * count_z)
    returned = solved.reshape(N_GRP, members, 3, N_GRP, message).transpose(3, 1, 2, 0, 4)
    returned = returned.reshape(layers, 3, count_y * count_z)
    correction = jax.vmap(lambda row, slots: row[:, slots])(returned, coarse_owner)
    correction = correction.reshape(layers, 3, count_y, count_z)
    spread_own = jnp.einsum('lcvw,vy,wz->lcyz', correction, hat_y, hat_z, precision=HIGHEST)
    spread_right = jnp.concatenate([spread_own[1:], jnp.zeros_like(spread_own[:1])], axis=0)
    prolonged = low_hat[None, None, :, None, None] * spread_own[:, :, None] + high_hat[None, None, :, None, None] * spread_right[:, :, None]
    update = keep * prolonged.transpose(1, 0, 2, 3, 4).reshape(3, 4 * layers, 4 * count_y, 4 * count_z)
    new_direction = direction + update
    image_next = apply_all(new_direction)
    residual = rhs - keep * image_next - (1.0 - keep) * new_direction
    coarse_residual = restrict(residual)
    return (new_direction, residual, coarse_residual)
```

```python
import functools
import jax
import jax.numpy as jnp
import numpy as np
from jax import lax
from jax.experimental import pallas as pl
from jax.experimental.pallas import tpu as pltpu
from jax.sharding import PartitionSpec as P

F32 = jnp.float32
BF16 = jnp.bfloat16
HIGHEST = lax.Precision.HIGHEST
EY = 4
EZ = 32
ROWS = 112
LIVE = 104
WIDE = 256
NODES = 80


def basis_tables():
    gll = np.array([-1.0, -np.sqrt(3.0 / 7.0), 0.0, np.sqrt(3.0 / 7.0), 1.0])
    inner = np.sqrt(5.0 - 2.0 * np.sqrt(10.0 / 7.0)) / 3.0
    outer = np.sqrt(5.0 + 2.0 * np.sqrt(10.0 / 7.0)) / 3.0
    inner_weight = (322.0 + 13.0 * np.sqrt(70.0)) / 900.0
    outer_weight = (322.0 - 13.0 * np.sqrt(70.0)) / 900.0
    points = np.array([-outer, -inner, 0.0, inner, outer])
    weights = np.array([outer_weight, inner_weight, 128.0 / 225.0, inner_weight, outer_weight])
    values = np.zeros((5, 5))
    slopes = np.zeros((5, 5))
    for j in range(5):
        others = [gll[k] for k in range(5) if k != j]
        denominator = np.prod([gll[j] - o for o in others])
        for q in range(5):
            t = points[q]
            values[q, j] = np.prod([t - o for o in others]) / denominator
            total = 0.0
            for i in range(4):
                total += np.prod([t - others[k] for k in range(4) if k != i])
            slopes[q, j] = 2.0 * total / denominator
    return gll, weights, values, slopes


def banded(table, count):
    result = np.zeros((5 * count, 4 * count + 1))
    for e in range(count):
        result[5 * e : 5 * e + 5, 4 * e : 4 * e + 5] = table
    return result[:, :-1]


def restrictor(gll, count):
    result = np.zeros((count, 4 * count))
    for e in range(count):
        for j in range(4):
            result[e, 4 * e + j] += (1.0 - gll[j]) / 2.0
            if e + 1 < count:
                result[e + 1, 4 * e + j] += (1.0 + gll[j]) / 2.0
    return result


def halves(table):
    table = np.asarray(table, np.float32)
    high = table.astype(BF16)
    low = (table - high.astype(np.float32)).astype(BF16)
    return high, low


def stack_left(table):
    high, low = halves(table)
    return np.concatenate([high, high, low], axis=1)


def stack_right(table):
    high, low = halves(table)
    return np.concatenate([high, high, low], axis=0)


@functools.lru_cache(maxsize=None)
def constants():
    gll, weights, values, slopes = basis_tables()
    by, dy = banded(values, EY), banded(slopes, EY)
    bz, dz = banded(values, EZ), banded(slopes, EZ)
    along = np.zeros((4 * EZ, 2 * WIDE))
    along[:, : 5 * EZ] = bz.T
    along[:, WIDE : WIDE + 5 * EZ] = dz.T
    kinds = np.zeros((3, ROWS, NODES))
    for a, (bx, side) in enumerate(((slopes, by), (values, dy), (values, by))):
        kinds[a, :100] = np.kron(bx, side)
    low = (1.0 - gll[:4]) / 2.0
    high = (1.0 + gll[:4]) / 2.0
    hat_y, hat_z = restrictor(gll, EY), restrictor(gll, EZ)
    rest = np.zeros((16, NODES))
    rest[0:4, :64] = np.kron(low[None, :], hat_y)
    rest[4:8, :64] = np.kron(high[None, :], hat_y)
    rest[4:8, 64:] = hat_y
    fold = np.zeros((8, 24))
    for c in range(3):
        for part in range(2):
            for k in range(4):
                fold[part * 4 + c, c * 8 + part * 4 + k] = 1.0
    quad_y = np.zeros((ROWS, EY))
    for r in range(5):
        for p in range(20):
            quad_y[r * 20 + p, p // 5] = weights[r] * weights[p % 5] / 8.0
    quad_z = np.zeros((EZ, WIDE))
    for q in range(5 * EZ):
        quad_z[q // 5, q] = weights[q % 5]
    return dict(
        along=stack_right(along),
        grads=stack_left(kinds.reshape(3 * ROWS, NODES)),
        back_xy=stack_left(np.concatenate([kinds[0].T, kinds[1].T], axis=1)),
        back_z=stack_left(kinds[2].T),
        back_along=stack_right(along.T),
        rest=stack_left(rest),
        tables=np.concatenate(
            [
                np.tile(hat_z.T, (1, 4)),
                np.pad(fold, ((0, 0), (0, 104))),
                np.pad(rest[:8].T, ((0, 0), (0, 120))),
            ],
            axis=0,
        ).astype(np.float32),
        quad_y=np.asarray(quad_y, np.float32),
        quad_z=np.asarray(quad_z, np.float32),
    )


def split(x):
    high = x.astype(BF16)
    return high, (x - high.astype(F32)).astype(BF16)


def dot(a, b):
    return jnp.dot(a, b, preferred_element_type=F32)


def exact(a, b):
    return jnp.dot(a, b, preferred_element_type=F32, precision=HIGHEST)


def under(x):
    high, low = split(x)
    return jnp.concatenate([high, low, high], axis=0)


def beside(x):
    high, low = split(x)
    return jnp.concatenate([high, low, high], axis=1)


def near(x):
    return pltpu.with_memory_space_constraint(x, pltpu.VMEM)


def call(body, outs, *operands, scratch=()):
    vmem = pl.BlockSpec(memory_space=pltpu.VMEM)
    return pl.pallas_call(
        body,
        out_shape=[pltpu.VMEM(s, F32) for s in outs],
        in_specs=[vmem] * len(operands),
        out_specs=[vmem] * len(outs),
        scratch_shapes=list(scratch),
        compiler_params=pltpu.CompilerParams(vmem_limit_bytes=24 * 2**20),
    )(*[near(x) for x in operands])


def prepare_body(count, *refs):
    sources, refs = refs[:count], refs[count:]
    message, keep_rows, rows, weighting = refs[:4]
    targets, done = refs[4:-1], refs[-1]
    copies = [
        pltpu.make_async_copy(source, target, done.at[i])
        for i, (source, target) in enumerate(zip(sources, targets))
    ]
    for copy in copies:
        copy.start()
    state, direction = targets[0], targets[1]
    clamp, owner, inverse, stiffness, quad_y, quad_z = targets[-6:]
    for i in (0, 1, count - 6, count - 5):
        copies[i].wait()
    eye = lax.broadcasted_iota(jnp.int32, (16, 16), 0) == lax.broadcasted_iota(
        jnp.int32, (16, 16), 1
    )
    lane = lax.broadcasted_iota(jnp.int32, (16, 128), 1)
    for x in range(4):
        row = clamp[x : x + 1, :].astype(F32)
        column = jnp.sum(jnp.where(eye, row, 0.0), axis=1, keepdims=True)
        keep = jnp.where(lane == 0, 1.0 - column, 1.0)
        keep_rows[x * 16 : (x + 1) * 16, :] = keep
        if x == 0:
            message[96:112, :] = keep
            message[112:120, :] = jnp.broadcast_to(owner[...].astype(F32), (8, 128))
            for c in range(3):
                message[c * 16 : (c + 1) * 16, :] = keep * direction[c, 0]
                message[48 + c * 16 : 48 + (c + 1) * 16, :] = state[c, 0]
    for i in range(count - 4, count):
        copies[i].wait()
    row = lax.broadcasted_iota(jnp.int32, (64, 64), 0)
    column = lax.broadcasted_iota(jnp.int32, (64, 64), 1)
    order = (column == (row % 32) * 2 + row // 32).astype(F32)
    for b in range(2):
        for c in range(3):
            sorted_rows = exact(order, inverse[b, c * 64 : (c + 1) * 64, :])
            for q in range(2):
                part = sorted_rows[q * 32 : (q + 1) * 32]
                padded = jnp.concatenate([part, jnp.zeros((32, 64), F32)], axis=1)
                for h in range(2):
                    first = b * 32 * 12 + (q * 3 + c) * 2 + h
                    rows[pl.ds(first, 32, stride=12), :] = padded[:, h * 128 : (h + 1) * 128]
    weighting[...] = exact(exact(quad_y[...], stiffness[...]), quad_z[...])
    for i in range(2, count - 6):
        copies[i].wait()


def prepare(kept, used):
    operands = list(kept) + list(used)
    far = pl.BlockSpec(memory_space=pltpu.HBM)
    vmem = pl.BlockSpec(memory_space=pltpu.VMEM)
    made = [(120, 128), (64, 128), (768, 128), (ROWS, WIDE)]
    outs = [pltpu.VMEM(s, F32) for s in made] + [pltpu.VMEM(x.shape, x.dtype) for x in kept]
    return pl.pallas_call(
        functools.partial(prepare_body, len(operands)),
        out_shape=outs,
        in_specs=[far] * len(operands),
        out_specs=[vmem] * len(outs),
        scratch_shapes=[pltpu.VMEM(x.shape, x.dtype) for x in used]
        + [pltpu.SemaphoreType.DMA((len(operands),))],
        compiler_params=pltpu.CompilerParams(vmem_limit_bytes=24 * 2**20),
    )(*[pltpu.with_memory_space_constraint(x, pltpu.HBM) for x in operands])


def gradients(fields, along, grads, refs):
    lines = jnp.concatenate([f for field in fields for f in field], axis=0)
    flat = dot(beside(lines), along[...])
    for i, ref in enumerate(refs):
        parts = [flat[(3 * i + c) * NODES : (3 * i + c + 1) * NODES] for c in range(3)]
        plain = jnp.concatenate([p[:, :WIDE] for p in parts], axis=1)
        sloped = jnp.concatenate([p[:, WIDE:] for p in parts], axis=1)
        ref[0 : 2 * ROWS, :] = dot(grads[0 : 2 * ROWS, :], under(plain))
        ref[2 * ROWS :, :] = dot(grads[2 * ROWS :, :], under(sloped))


def physics(state_grad, grad, weighting, flux):
    pairs = ((0, 0), (1, 1), (2, 2), (0, 1), (0, 2), (1, 2))
    for start in range(0, LIVE, 8):
        here = slice(start, start + 8)
        w = weighting[here, :]

        def piece(ref, c, a):
            return ref[a * ROWS + start : a * ROWS + start + 8, c * WIDE : (c + 1) * WIDE]

        deform = [
            [piece(state_grad, c, a) + (1.0 if a == c else 0.0) for a in range(3)]
            for c in range(3)
        ]
        change = [[piece(grad, c, a) for a in range(3)] for c in range(3)]
        square = {
            (a, b): deform[0][a] * deform[0][b]
            + deform[1][a] * deform[1][b]
            + deform[2][a] * deform[2][b]
            for a, b in pairs
        }
        shift = 0.6 * (square[0, 0] + square[1, 1] + square[2, 2] - 3.0)
        held = {
            (a, b): w * (0.8 * (square[a, b] - 1.0) + shift) if a == b else (0.8 * w) * square[a, b]
            for a, b in pairs
        }
        cross = [
            [
                deform[0][a] * change[0][b] + deform[1][a] * change[1][b] + deform[2][a] * change[2][b]
                for b in range(3)
            ]
            for a in range(3)
        ]
        trace = (1.2 * w) * (cross[0][0] + cross[1][1] + cross[2][2])
        moved = {}
        for a, b in pairs:
            if a == b:
                moved[a, b] = (1.6 * w) * cross[a][b] + trace
            else:
                moved[a, b] = (0.8 * w) * (cross[a][b] + cross[b][a])
        for a in range(3):
            for c in range(3):
                entry = None
                for b in range(3):
                    key = (min(a, b), max(a, b))
                    term = change[c][b] * held[key] + deform[c][b] * moved[key]
                    entry = term if entry is None else entry + term
                flux[a * ROWS + start : a * ROWS + start + 8, c * WIDE : (c + 1) * WIDE] = entry
    for a in range(3):
        flux[a * ROWS + LIVE : (a + 1) * ROWS, :] = jnp.zeros((ROWS - LIVE, 3 * WIDE), F32)


def images(flux, back_xy, back_z, back_along):
    side_b = dot(back_xy[...], under(flux[0 : 2 * ROWS, :]))
    side_d = dot(back_z[...], under(flux[2 * ROWS :, :]))
    lines = jnp.concatenate(
        [
            jnp.concatenate(
                [side_b[:, c * WIDE : (c + 1) * WIDE], side_d[:, c * WIDE : (c + 1) * WIDE]], axis=1
            )
            for c in range(3)
        ],
        axis=0,
    )
    return dot(beside(lines), back_along[...])


def coarse_rows(extended, rest):
    levels = dot(rest[...], under(jnp.concatenate(extended, axis=1)))
    return jnp.concatenate([levels[:8, c * 128 : (c + 1) * 128] for c in range(3)], axis=0)


def own_rows(ref, c):
    return ref[c].reshape(64, 128)


def first_body(
    state, direction, rhs, keep_rows, halo, weighting, along, grads, back_xy, back_z, back_along,
    rest, tables, owner, state_grad, sums, grad, flux,
):
    keep = keep_rows[...]
    fields = [
        [jnp.concatenate([own_rows(state, c), halo[48 + c * 16 : 64 + c * 16, :]], axis=0) for c in range(3)],
        [
            jnp.concatenate([keep * own_rows(direction, c), halo[c * 16 : 16 + c * 16, :]], axis=0)
            for c in range(3)
        ],
    ]
    gradients(fields, along, grads, (state_grad, grad))
    physics(state_grad, grad, weighting, flux)
    image = images(flux, back_xy, back_z, back_along)
    keep_right = halo[96:112, :]
    extended = []
    for c in range(3):
        part = image[c * NODES : (c + 1) * NODES]
        own = own_rows(rhs, c) - keep * part[:64] - (1.0 - keep) * own_rows(direction, c)
        extended.append(jnp.concatenate([own, -keep_right * part[64:]], axis=0))
    levels = exact(coarse_rows(extended, rest), tables[0:128, :])
    row = lax.broadcasted_iota(jnp.int32, (24, 128), 0)
    lane = lax.broadcasted_iota(jnp.int32, (24, 128), 1)
    levels = jnp.where(lane // EZ == row % EY, levels, 0.0)
    levels = exact(tables[128:136, 0:24], levels)
    sums[0:4, :] = placed(levels, owner[...])[0:4]
    sums[4:8, :] = placed(levels, halo[112:113, :].astype(jnp.int32))[4:8]


def slots(owner):
    place = (owner % 2) * 64 + owner // 2
    return (lax.broadcasted_iota(jnp.int32, (128, 128), 0) == place).astype(BF16)


def placed(rows, owner):
    where = slots(owner)
    nt = (((1,), (1,)), ((), ()))
    return sum(lax.dot_general(part, where, nt, preferred_element_type=F32) for part in split(rows))


def solve_body(gathered, rows, owner, correction):
    tn = (((0,), (0,)), ((), ()))
    values = gathered[...]
    row = lax.broadcasted_iota(jnp.int32, (128, 256), 0)
    lane = lax.broadcasted_iota(jnp.int32, (128, 256), 1)
    match = (row // 4 == lane % 64 // 2) & (row % 4 == lane // 64) & (lane < 192)
    need = None
    for q in range(2):
        pick = (match & (lane % 2 == q)).astype(BF16)
        for part in split(values[:, q * 64 : (q + 1) * 64]):
            term = lax.dot_general(part, pick, tn, preferred_element_type=F32)
            need = term if need is None else need + term
    products = []
    for k in range(6):
        product = None
        for h in range(2):
            term = rows[pl.ds(2 * k + h, 64, stride=12), :] * need[:, h * 128 : (h + 1) * 128]
            product = term if product is None else product + term
        products.append(product)
    ones = jnp.ones((128, 128), BF16)
    sums = sum(dot(part, ones) for part in split(jnp.concatenate(products, axis=0)))
    lane = lax.broadcasted_iota(jnp.int32, (64, 128), 1)
    stacked = []
    for q in range(2):
        first, second, third = [sums[(q * 3 + c) * 64 : (q * 3 + c + 1) * 64] for c in range(3)]
        stacked.append(jnp.where(lane == 0, first, jnp.where(lane == 1, second, third)))
    stacked = jnp.concatenate(stacked, axis=0)[:, 0:8]
    where = slots(owner[...])
    correction[...] = sum(
        lax.dot_general(part, where, tn, preferred_element_type=F32) for part in split(stacked)
    )


def second_body(
    correction, right, state_grad, direction, rhs, keep_rows, halo, weighting, along, grads,
    back_xy, back_z, back_along, rest, tables, new, partial, message, own_coarse, grad, flux,
):
    keep = keep_rows[...]
    keep_right = halo[96:112, :]
    rows = jnp.concatenate(
        [
            jnp.broadcast_to(ref[c : c + 1, :], (4, 128))
            for c in range(3)
            for ref in (correction, right)
        ],
        axis=0,
    )
    row = lax.broadcasted_iota(jnp.int32, (24, 128), 0)
    lane = lax.broadcasted_iota(jnp.int32, (24, 128), 1)
    levels = lax.dot_general(
        jnp.where(lane // EZ == row % EY, rows, 0.0), tables[0:128, :], (((1,), (1,)), ((), ())),
        preferred_element_type=F32, precision=HIGHEST,
    )
    levels = jnp.concatenate([levels[c * 8 : (c + 1) * 8] for c in range(3)], axis=1)
    update = exact(tables[136:216, 0:8], levels)
    field = []
    fresh = []
    for c in range(3):
        piece = update[:, c * 128 : (c + 1) * 128]
        own = own_rows(direction, c) + keep * piece[:64]
        new[c] = own.reshape(4, 16, 128)
        fresh.append(own)
        field.append(
            jnp.concatenate(
                [keep * own, halo[c * 16 : 16 + c * 16, :] + keep_right * piece[64:]], axis=0
            )
        )
    gradients([field], along, grads, (grad,))
    physics(state_grad, grad, weighting, flux)
    image = images(flux, back_xy, back_z, back_along)
    extended = []
    for c in range(3):
        part = image[c * NODES : (c + 1) * NODES]
        own = own_rows(rhs, c) - keep * part[:64] - (1.0 - keep) * fresh[c]
        last = -keep_right * part[64:]
        partial[c] = own.reshape(4, 16, 128)
        message[c * 16 : (c + 1) * 16, :] = last
        extended.append(jnp.concatenate([own, last], axis=0))
    levels = exact(coarse_rows(extended, rest), tables[0:128, :])
    message[48:72, :] = levels
    for c in range(3):
        own_coarse[c] = levels[c * 8 : c * 8 + 4, :EZ]


def finish_body(partial, arrived, own_coarse, residual, coarse):
    for c in range(3):
        residual[c, 0] = partial[c, 0] + arrived[c * 16 : (c + 1) * 16, :]
        residual[c, 1:4] = partial[c, 1:4]
        coarse[c] = own_coarse[c] + arrived[52 + c * 8 : 56 + c * 8, :EZ]


def finish(partial, arrived, own_coarse):
    vmem = pl.BlockSpec(memory_space=pltpu.VMEM)
    return pl.pallas_call(
        finish_body,
        out_shape=[
            jax.ShapeDtypeStruct((3, 4, 16, 128), F32),
            jax.ShapeDtypeStruct((3, EY, EZ), F32),
        ],
        in_specs=[vmem] * 3,
        out_specs=[vmem] * 2,
        compiler_params=pltpu.CompilerParams(vmem_limit_bytes=24 * 2**20),
    )(near(partial), near(arrived), near(own_coarse))


def shifted(block, distance):
    axes = ("grp", "mem")
    count = lax.axis_size(axes)
    route = [(i - distance, i) for i in range(count) if 0 <= i - distance < count]
    return lax.ppermute(block, axes, route)


def shards(state, direction, rhs, clamp, stiffness, coarse_owner, coarse_inverse):
    k = constants()
    names = ("along", "grads", "back_xy", "back_z", "back_along", "rest", "tables")
    kept = [state, direction, rhs] + [jnp.asarray(k[name]) for name in names] + [coarse_owner]
    used = [
        clamp, coarse_owner, coarse_inverse[0], stiffness[0],
        jnp.asarray(k["quad_y"]), jnp.asarray(k["quad_z"]),
    ]
    message, keep_rows, rows, weighting, state, direction, rhs, *shared, owner = prepare(kept, used)
    halo = shifted(message, -1)
    rows = lax.all_to_all(
        rows.reshape(192, 4, 128), "grp", split_axis=0, concat_axis=0, tiled=True
    ).reshape(768, 128)
    big = (3 * ROWS, 3 * WIDE)
    scratch = (pltpu.VMEM(big, F32), pltpu.VMEM(big, F32))
    state_grad, sums = call(
        first_body,
        [big, (8, 128)],
        state, direction, rhs, keep_rows, halo, weighting, *shared, owner,
        scratch=scratch,
    )
    arrived = shifted(sums, 1)
    total = jnp.broadcast_to((sums[0:4] + arrived[4:8])[None], (32, 4, 128)).reshape(128, 128)
    total, rows = lax.optimization_barrier((total, rows))
    sides = [list(range(32)), list(range(32, 64))]
    gathered = lax.all_to_all(
        total, "grp", split_axis=0, concat_axis=0, tiled=True, axis_index_groups=sides
    )
    (correction,) = call(solve_body, [(8, 128)], gathered, rows, owner)
    right = shifted(correction, -1)
    field = (3, 4, 16, 128)
    new, partial, last, own_coarse = call(
        second_body,
        [field, field, (72, 128), (3, EY, EZ)],
        correction, right, state_grad, direction, rhs, keep_rows, halo, weighting, *shared,
        scratch=scratch,
    )
    residual, coarse = finish(partial, shifted(last, 1), own_coarse)
    return new, residual, coarse[:, None]


def solution(mesh):
    along = ("grp", "mem")
    field = P(None, along, None, None)
    in_specs = (
        field, field, field, P(along, None), P(along, None, None), P(along, None),
        P(along, None, None, None),
    )
    return jax.shard_map(
        shards, mesh=mesh, in_specs=in_specs, out_specs=(field, field, field), check_vma=False
    )
```

```python
import functools
import jax
import jax.numpy as jnp
import numpy as np
from jax import lax
from jax.experimental import pallas as pl
from jax.experimental.pallas import tpu as pltpu
from jax.sharding import PartitionSpec as P

F32 = jnp.float32
BF16 = jnp.bfloat16
HIGHEST = lax.Precision.HIGHEST
EY = 4
EZ = 32
ROWS = 112
LIVE = 104
WIDE = 256
NODES = 80


def basis_tables():
    gll = np.array([-1.0, -np.sqrt(3.0 / 7.0), 0.0, np.sqrt(3.0 / 7.0), 1.0])
    inner = np.sqrt(5.0 - 2.0 * np.sqrt(10.0 / 7.0)) / 3.0
    outer = np.sqrt(5.0 + 2.0 * np.sqrt(10.0 / 7.0)) / 3.0
    inner_weight = (322.0 + 13.0 * np.sqrt(70.0)) / 900.0
    outer_weight = (322.0 - 13.0 * np.sqrt(70.0)) / 900.0
    points = np.array([-outer, -inner, 0.0, inner, outer])
    weights = np.array([outer_weight, inner_weight, 128.0 / 225.0, inner_weight, outer_weight])
    values = np.zeros((5, 5))
    slopes = np.zeros((5, 5))
    for j in range(5):
        others = [gll[k] for k in range(5) if k != j]
        denominator = np.prod([gll[j] - o for o in others])
        for q in range(5):
            t = points[q]
            values[q, j] = np.prod([t - o for o in others]) / denominator
            total = 0.0
            for i in range(4):
                total += np.prod([t - others[k] for k in range(4) if k != i])
            slopes[q, j] = 2.0 * total / denominator
    return gll, weights, values, slopes


def banded(table, count):
    result = np.zeros((5 * count, 4 * count + 1))
    for e in range(count):
        result[5 * e : 5 * e + 5, 4 * e : 4 * e + 5] = table
    return result[:, :-1]


def restrictor(gll, count):
    result = np.zeros((count, 4 * count))
    for e in range(count):
        for j in range(4):
            result[e, 4 * e + j] += (1.0 - gll[j]) / 2.0
            if e + 1 < count:
                result[e + 1, 4 * e + j] += (1.0 + gll[j]) / 2.0
    return result


def halves(table):
    table = np.asarray(table, np.float32)
    high = table.astype(BF16)
    low = (table - high.astype(np.float32)).astype(BF16)
    return high, low


def stack_left(table):
    high, low = halves(table)
    return np.concatenate([high, high, low], axis=1)


def stack_right(table):
    high, low = halves(table)
    return np.concatenate([high, high, low], axis=0)


@functools.lru_cache(maxsize=None)
def constants():
    gll, weights, values, slopes = basis_tables()
    by, dy = banded(values, EY), banded(slopes, EY)
    bz, dz = banded(values, EZ), banded(slopes, EZ)
    along = np.zeros((4 * EZ, 2 * WIDE))
    along[:, : 5 * EZ] = bz.T
    along[:, WIDE : WIDE + 5 * EZ] = dz.T
    kinds = np.zeros((3, ROWS, NODES))
    for a, (bx, side) in enumerate(((slopes, by), (values, dy), (values, by))):
        kinds[a, :100] = np.kron(bx, side)
    low = (1.0 - gll[:4]) / 2.0
    high = (1.0 + gll[:4]) / 2.0
    hat_y, hat_z = restrictor(gll, EY), restrictor(gll, EZ)
    rest = np.zeros((16, NODES))
    rest[0:4, :64] = np.kron(low[None, :], hat_y)
    rest[4:8, :64] = np.kron(high[None, :], hat_y)
    rest[4:8, 64:] = hat_y
    fold = np.zeros((8, 24))
    for c in range(3):
        for part in range(2):
            for k in range(4):
                fold[part * 4 + c, c * 8 + part * 4 + k] = 1.0
    quad_y = np.zeros((ROWS, EY))
    for r in range(5):
        for p in range(20):
            quad_y[r * 20 + p, p // 5] = weights[r] * weights[p % 5] / 8.0
    quad_z = np.zeros((EZ, WIDE))
    for q in range(5 * EZ):
        quad_z[q // 5, q] = weights[q % 5]
    return dict(
        along=stack_right(along),
        grads=stack_left(kinds.reshape(3 * ROWS, NODES)),
        back_xy=stack_left(np.concatenate([kinds[0].T, kinds[1].T], axis=1)),
        back_z=stack_left(kinds[2].T),
        back_along=stack_right(along.T),
        rest=stack_left(rest),
        tables=np.concatenate(
            [
                np.tile(hat_z.T, (1, 4)),
                np.pad(fold, ((0, 0), (0, 104))),
                np.pad(rest[:8].T, ((0, 0), (0, 120))),
            ],
            axis=0,
        ).astype(np.float32),
        quad_y=np.asarray(quad_y, np.float32),
        quad_z=np.asarray(quad_z, np.float32),
    )


def split(x):
    high = x.astype(BF16)
    return high, (x - high.astype(F32)).astype(BF16)


def dot(a, b):
    return jnp.dot(a, b, preferred_element_type=F32)


def exact(a, b):
    return jnp.dot(a, b, preferred_element_type=F32, precision=HIGHEST)


def under(x):
    high, low = split(x)
    return jnp.concatenate([high, low, high], axis=0)


def beside(x):
    high, low = split(x)
    return jnp.concatenate([high, low, high], axis=1)


def near(x):
    return pltpu.with_memory_space_constraint(x, pltpu.VMEM)


def call(body, outs, *operands, scratch=(), cost=None):
    vmem = pl.BlockSpec(memory_space=pltpu.VMEM)
    return pl.pallas_call(
        body,
        out_shape=[pltpu.VMEM(s, F32) for s in outs],
        in_specs=[vmem] * len(operands),
        out_specs=[vmem] * len(outs),
        scratch_shapes=list(scratch),
        cost_estimate=cost,
        compiler_params=pltpu.CompilerParams(vmem_limit_bytes=24 * 2**20),
    )(*[near(x) for x in operands])


def prepare_body(count, *refs):
    sources, refs = refs[:count], refs[count:]
    message, keep_rows, rows, weighting = refs[:4]
    targets, (halves_of, done) = refs[4:-2], refs[-2:]
    copies = [
        pltpu.make_async_copy(source, target, done.at[i])
        for i, (source, target) in enumerate(zip(sources, targets))
    ]
    for copy in copies:
        copy.start()
    state, direction = targets[0], targets[1]
    clamp, owner, inverse, stiffness, quad_y, quad_z = targets[-6:]
    for i in (0, 1, count - 6, count - 5):
        copies[i].wait()
    eye = lax.broadcasted_iota(jnp.int32, (16, 16), 0) == lax.broadcasted_iota(
        jnp.int32, (16, 16), 1
    )
    lane = lax.broadcasted_iota(jnp.int32, (16, 128), 1)
    for x in range(4):
        row = clamp[x : x + 1, :].astype(F32)
        column = jnp.sum(jnp.where(eye, row, 0.0), axis=1, keepdims=True)
        keep = jnp.where(lane == 0, 1.0 - column, 1.0)
        keep_rows[x * 16 : (x + 1) * 16, :] = keep
        if x == 0:
            message[96:112, :] = keep
            message[112:120, :] = jnp.broadcast_to(owner[...].astype(F32), (8, 128))
            for c in range(3):
                message[c * 16 : (c + 1) * 16, :] = keep * direction[c, 0]
                message[48 + c * 16 : 48 + (c + 1) * 16, :] = state[c, 0]
    for i in range(count - 4, count):
        copies[i].wait()
    halves_of[0] = inverse[:, 0:128]
    halves_of[1] = jnp.concatenate([inverse[:, 128:192], jnp.zeros((384, 64), F32)], axis=1)
    for b in range(2):
        for c in range(3):
            for q in range(2):
                source = pl.ds(b * 192 + c * 64 + q, 32, stride=2)
                first = b * 32 * 12 + (q * 3 + c) * 2
                for h in range(2):
                    rows[pl.ds(first + h, 32, stride=12), :] = halves_of[h, source, :]
    weighting[...] = exact(exact(quad_y[...], stiffness[...]), quad_z[...])
    for i in range(2, count - 6):
        copies[i].wait()


def prepare(kept, used):
    operands = list(kept) + list(used)
    far = pl.BlockSpec(memory_space=pltpu.HBM)
    vmem = pl.BlockSpec(memory_space=pltpu.VMEM)
    made = [(120, 128), (64, 128), (768, 128), (ROWS, WIDE)]
    outs = [pltpu.VMEM(s, F32) for s in made] + [pltpu.VMEM(x.shape, x.dtype) for x in kept]
    return pl.pallas_call(
        functools.partial(prepare_body, len(operands)),
        out_shape=outs,
        in_specs=[far] * len(operands),
        out_specs=[vmem] * len(outs),
        scratch_shapes=[pltpu.VMEM(x.shape, x.dtype) for x in used]
        + [pltpu.VMEM((2, 384, 128), F32)]
        + [pltpu.SemaphoreType.DMA((len(operands),))],
        compiler_params=pltpu.CompilerParams(vmem_limit_bytes=24 * 2**20),
    )(*[pltpu.with_memory_space_constraint(x, pltpu.HBM) for x in operands])


def gradients(fields, along, grads, refs):
    lines = jnp.concatenate([f for field in fields for f in field], axis=0)
    flat = dot(beside(lines), along[...])
    for i, ref in enumerate(refs):
        parts = [flat[(3 * i + c) * NODES : (3 * i + c + 1) * NODES] for c in range(3)]
        plain = jnp.concatenate([p[:, :WIDE] for p in parts], axis=1)
        sloped = jnp.concatenate([p[:, WIDE:] for p in parts], axis=1)
        ref[0 : 2 * ROWS, :] = dot(grads[0 : 2 * ROWS, :], under(plain))
        ref[2 * ROWS :, :] = dot(grads[2 * ROWS :, :], under(sloped))


def physics(state_grad, grad, weighting, flux):
    pairs = ((0, 0), (1, 1), (2, 2), (0, 1), (0, 2), (1, 2))
    for start in range(0, LIVE, 8):
        here = slice(start, start + 8)
        w = weighting[here, :]

        def piece(ref, c, a):
            return ref[a * ROWS + start : a * ROWS + start + 8, c * WIDE : (c + 1) * WIDE]

        deform = [
            [piece(state_grad, c, a) + (1.0 if a == c else 0.0) for a in range(3)]
            for c in range(3)
        ]
        change = [[piece(grad, c, a) for a in range(3)] for c in range(3)]
        square = {
            (a, b): deform[0][a] * deform[0][b]
            + deform[1][a] * deform[1][b]
            + deform[2][a] * deform[2][b]
            for a, b in pairs
        }
        shift = 0.6 * (square[0, 0] + square[1, 1] + square[2, 2] - 3.0)
        held = {
            (a, b): w * (0.8 * (square[a, b] - 1.0) + shift) if a == b else (0.8 * w) * square[a, b]
            for a, b in pairs
        }
        cross = [
            [
                deform[0][a] * change[0][b] + deform[1][a] * change[1][b] + deform[2][a] * change[2][b]
                for b in range(3)
            ]
            for a in range(3)
        ]
        trace = (1.2 * w) * (cross[0][0] + cross[1][1] + cross[2][2])
        moved = {}
        for a, b in pairs:
            if a == b:
                moved[a, b] = (1.6 * w) * cross[a][b] + trace
            else:
                moved[a, b] = (0.8 * w) * (cross[a][b] + cross[b][a])
        for a in range(3):
            for c in range(3):
                entry = None
                for b in range(3):
                    key = (min(a, b), max(a, b))
                    term = change[c][b] * held[key] + deform[c][b] * moved[key]
                    entry = term if entry is None else entry + term
                flux[a * ROWS + start : a * ROWS + start + 8, c * WIDE : (c + 1) * WIDE] = entry
    for a in range(3):
        flux[a * ROWS + LIVE : (a + 1) * ROWS, :] = jnp.zeros((ROWS - LIVE, 3 * WIDE), F32)


def images(flux, back_xy, back_z, back_along):
    side_b = dot(back_xy[...], under(flux[0 : 2 * ROWS, :]))
    side_d = dot(back_z[...], under(flux[2 * ROWS :, :]))
    lines = jnp.concatenate(
        [
            jnp.concatenate(
                [side_b[:, c * WIDE : (c + 1) * WIDE], side_d[:, c * WIDE : (c + 1) * WIDE]], axis=1
            )
            for c in range(3)
        ],
        axis=0,
    )
    return dot(beside(lines), back_along[...])


def coarse_rows(extended, rest):
    levels = dot(rest[...], under(jnp.concatenate(extended, axis=1)))
    return jnp.concatenate([levels[:8, c * 128 : (c + 1) * 128] for c in range(3)], axis=0)


def own_rows(ref, c):
    return ref[c].reshape(64, 128)


def first_body(
    state, direction, rhs, keep_rows, halo, weighting, along, grads, back_xy, back_z, back_along,
    rest, tables, owner, state_grad, sums, grad, flux,
):
    keep = keep_rows[...]
    fields = [
        [jnp.concatenate([own_rows(state, c), halo[48 + c * 16 : 64 + c * 16, :]], axis=0) for c in range(3)],
        [
            jnp.concatenate([keep * own_rows(direction, c), halo[c * 16 : 16 + c * 16, :]], axis=0)
            for c in range(3)
        ],
    ]
    gradients(fields, along, grads, (state_grad, grad))
    physics(state_grad, grad, weighting, flux)
    image = images(flux, back_xy, back_z, back_along)
    keep_right = halo[96:112, :]
    extended = []
    for c in range(3):
        part = image[c * NODES : (c + 1) * NODES]
        own = own_rows(rhs, c) - keep * part[:64] - (1.0 - keep) * own_rows(direction, c)
        extended.append(jnp.concatenate([own, -keep_right * part[64:]], axis=0))
    levels = exact(coarse_rows(extended, rest), tables[0:128, :])
    row = lax.broadcasted_iota(jnp.int32, (24, 128), 0)
    lane = lax.broadcasted_iota(jnp.int32, (24, 128), 1)
    levels = jnp.where(lane // EZ == row % EY, levels, 0.0)
    levels = exact(tables[128:136, 0:24], levels)
    sums[0:4, :] = placed(levels, owner[...])[0:4]
    sums[4:8, :] = placed(levels, halo[112:113, :].astype(jnp.int32))[4:8]


def slots(owner):
    place = (owner % 2) * 64 + owner // 2
    return (lax.broadcasted_iota(jnp.int32, (128, 128), 0) == place).astype(BF16)


def placed(rows, owner):
    where = slots(owner)
    nt = (((1,), (1,)), ((), ()))
    return sum(lax.dot_general(part, where, nt, preferred_element_type=F32) for part in split(rows))


def solve_body(gathered, rows, owner, correction):
    tn = (((0,), (0,)), ((), ()))
    values = gathered[...]
    row = lax.broadcasted_iota(jnp.int32, (128, 256), 0)
    lane = lax.broadcasted_iota(jnp.int32, (128, 256), 1)
    match = (row // 4 == lane % 64 // 2) & (row % 4 == lane // 64) & (lane < 192)
    need = None
    for q in range(2):
        pick = (match & (lane % 2 == q)).astype(BF16)
        for part in split(values[:, q * 64 : (q + 1) * 64]):
            term = lax.dot_general(part, pick, tn, preferred_element_type=F32)
            need = term if need is None else need + term
    products = []
    for k in range(6):
        product = None
        for h in range(2):
            term = rows[pl.ds(2 * k + h, 64, stride=12), :] * need[:, h * 128 : (h + 1) * 128]
            product = term if product is None else product + term
        products.append(product)
    ones = jnp.ones((128, 128), BF16)
    sums = sum(dot(part, ones) for part in split(jnp.concatenate(products, axis=0)))
    lane = lax.broadcasted_iota(jnp.int32, (64, 128), 1)
    stacked = []
    for q in range(2):
        first, second, third = [sums[(q * 3 + c) * 64 : (q * 3 + c + 1) * 64] for c in range(3)]
        stacked.append(jnp.where(lane == 0, first, jnp.where(lane == 1, second, third)))
    stacked = jnp.concatenate(stacked, axis=0)[:, 0:8]
    where = slots(owner[...])
    correction[...] = sum(
        lax.dot_general(part, where, tn, preferred_element_type=F32) for part in split(stacked)
    )


def second_body(
    correction, right, state_grad, direction, rhs, keep_rows, halo, weighting, along, grads,
    back_xy, back_z, back_along, rest, tables, new, partial, message, own_coarse, grad, flux,
):
    keep = keep_rows[...]
    keep_right = halo[96:112, :]
    rows = jnp.concatenate(
        [
            jnp.broadcast_to(ref[c : c + 1, :], (4, 128))
            for c in range(3)
            for ref in (correction, right)
        ],
        axis=0,
    )
    row = lax.broadcasted_iota(jnp.int32, (24, 128), 0)
    lane = lax.broadcasted_iota(jnp.int32, (24, 128), 1)
    levels = lax.dot_general(
        jnp.where(lane // EZ == row % EY, rows, 0.0), tables[0:128, :], (((1,), (1,)), ((), ())),
        preferred_element_type=F32, precision=HIGHEST,
    )
    levels = jnp.concatenate([levels[c * 8 : (c + 1) * 8] for c in range(3)], axis=1)
    update = exact(tables[136:216, 0:8], levels)
    field = []
    fresh = []
    for c in range(3):
        piece = update[:, c * 128 : (c + 1) * 128]
        own = own_rows(direction, c) + keep * piece[:64]
        new[c] = own.reshape(4, 16, 128)
        fresh.append(own)
        field.append(
            jnp.concatenate(
                [keep * own, halo[c * 16 : 16 + c * 16, :] + keep_right * piece[64:]], axis=0
            )
        )
    gradients([field], along, grads, (grad,))
    physics(state_grad, grad, weighting, flux)
    image = images(flux, back_xy, back_z, back_along)
    extended = []
    for c in range(3):
        part = image[c * NODES : (c + 1) * NODES]
        own = own_rows(rhs, c) - keep * part[:64] - (1.0 - keep) * fresh[c]
        last = -keep_right * part[64:]
        partial[c] = own.reshape(4, 16, 128)
        message[c * 16 : (c + 1) * 16, :] = last
        extended.append(jnp.concatenate([own, last], axis=0))
    levels = exact(coarse_rows(extended, rest), tables[0:128, :])
    message[48:72, :] = levels
    for c in range(3):
        own_coarse[c] = levels[c * 8 : c * 8 + 4, :EZ]


def finish_body(partial, arrived, own_coarse, residual, coarse):
    for c in range(3):
        residual[c, 0] = partial[c, 0] + arrived[c * 16 : (c + 1) * 16, :]
        residual[c, 1:4] = partial[c, 1:4]
        coarse[c] = own_coarse[c] + arrived[52 + c * 8 : 56 + c * 8, :EZ]


def finish(partial, arrived, own_coarse):
    vmem = pl.BlockSpec(memory_space=pltpu.VMEM)
    return pl.pallas_call(
        finish_body,
        out_shape=[
            jax.ShapeDtypeStruct((3, 4, 16, 128), F32),
            jax.ShapeDtypeStruct((3, EY, EZ), F32),
        ],
        in_specs=[vmem] * 3,
        out_specs=[vmem] * 2,
        compiler_params=pltpu.CompilerParams(vmem_limit_bytes=24 * 2**20),
    )(near(partial), near(arrived), near(own_coarse))


def shifted(block, distance):
    axes = ("grp", "mem")
    count = lax.axis_size(axes)
    route = [(i - distance, i) for i in range(count) if 0 <= i - distance < count]
    return lax.ppermute(block, axes, route)


def shards(state, direction, rhs, clamp, stiffness, coarse_owner, coarse_inverse):
    k = constants()
    names = ("along", "grads", "back_xy", "back_z", "back_along", "rest", "tables")
    kept = [state, direction, rhs] + [jnp.asarray(k[name]) for name in names] + [coarse_owner]
    inverse = coarse_inverse.reshape(384, 192)
    used = [
        clamp, coarse_owner, inverse, stiffness[0],
        jnp.asarray(k["quad_y"]), jnp.asarray(k["quad_z"]),
    ]
    message, keep_rows, rows, weighting, state, direction, rhs, *shared, owner = prepare(kept, used)
    halo = shifted(message, -1)
    rows = lax.all_to_all(
        rows.reshape(192, 4, 128), "grp", split_axis=0, concat_axis=0, tiled=True
    ).reshape(768, 128)
    big = (3 * ROWS, 3 * WIDE)
    scratch = (pltpu.VMEM(big, F32), pltpu.VMEM(big, F32))
    state_grad, sums = call(
        first_body,
        [big, (8, 128)],
        state, direction, rhs, keep_rows, halo, weighting, *shared, owner,
        scratch=scratch, cost=pl.CostEstimate(flops=20000000000, bytes_accessed=4 * 10**6, transcendentals=0),
    )
    arrived = shifted(sums, 1)
    total = jnp.broadcast_to((sums[0:4] + arrived[4:8])[None], (32, 4, 128)).reshape(128, 128)
    total, rows = lax.optimization_barrier((total, rows))
    sides = [list(range(32)), list(range(32, 64))]
    gathered = lax.all_to_all(
        total, "grp", split_axis=0, concat_axis=0, tiled=True, axis_index_groups=sides
    )
    (correction,) = call(solve_body, [(8, 128)], gathered, rows, owner)
    right = shifted(correction, -1)
    field = (3, 4, 16, 128)
    new, partial, last, own_coarse = call(
        second_body,
        [field, field, (72, 128), (3, EY, EZ)],
        correction, right, state_grad, direction, rhs, keep_rows, halo, weighting, *shared,
        scratch=scratch,
    )
    residual, coarse = finish(partial, shifted(last, 1), own_coarse)
    return new, residual, coarse[:, None]


def solution(mesh):
    along = ("grp", "mem")
    field = P(None, along, None, None)
    in_specs = (
        field, field, field, P(along, None), P(along, None, None), P(along, None),
        P(along, None, None, None),
    )
    return jax.shard_map(
        shards, mesh=mesh, in_specs=in_specs, out_specs=(field, field, field), check_vma=False
    )
```

```python
import functools
import jax
import jax.numpy as jnp
import numpy as np
from jax import lax
from jax.experimental import pallas as pl
from jax.experimental.pallas import tpu as pltpu
from jax.sharding import PartitionSpec as P

F32 = jnp.float32
BF16 = jnp.bfloat16
HIGHEST = lax.Precision.HIGHEST
EY = 4
EZ = 32
ROWS = 112
LIVE = 104
WIDE = 256
NODES = 80


def basis_tables():
    gll = np.array([-1.0, -np.sqrt(3.0 / 7.0), 0.0, np.sqrt(3.0 / 7.0), 1.0])
    inner = np.sqrt(5.0 - 2.0 * np.sqrt(10.0 / 7.0)) / 3.0
    outer = np.sqrt(5.0 + 2.0 * np.sqrt(10.0 / 7.0)) / 3.0
    inner_weight = (322.0 + 13.0 * np.sqrt(70.0)) / 900.0
    outer_weight = (322.0 - 13.0 * np.sqrt(70.0)) / 900.0
    points = np.array([-outer, -inner, 0.0, inner, outer])
    weights = np.array([outer_weight, inner_weight, 128.0 / 225.0, inner_weight, outer_weight])
    values = np.zeros((5, 5))
    slopes = np.zeros((5, 5))
    for j in range(5):
        others = [gll[k] for k in range(5) if k != j]
        denominator = np.prod([gll[j] - o for o in others])
        for q in range(5):
            t = points[q]
            values[q, j] = np.prod([t - o for o in others]) / denominator
            total = 0.0
            for i in range(4):
                total += np.prod([t - others[k] for k in range(4) if k != i])
            slopes[q, j] = 2.0 * total / denominator
    return gll, weights, values, slopes


def banded(table, count):
    result = np.zeros((5 * count, 4 * count + 1))
    for e in range(count):
        result[5 * e : 5 * e + 5, 4 * e : 4 * e + 5] = table
    return result[:, :-1]


def restrictor(gll, count):
    result = np.zeros((count, 4 * count))
    for e in range(count):
        for j in range(4):
            result[e, 4 * e + j] += (1.0 - gll[j]) / 2.0
            if e + 1 < count:
                result[e + 1, 4 * e + j] += (1.0 + gll[j]) / 2.0
    return result


def halves(table):
    table = np.asarray(table, np.float32)
    high = table.astype(BF16)
    low = (table - high.astype(np.float32)).astype(BF16)
    return high, low


def stack_left(table):
    high, low = halves(table)
    return np.concatenate([high, high, low], axis=1)


def stack_right(table):
    high, low = halves(table)
    return np.concatenate([high, high, low], axis=0)


@functools.lru_cache(maxsize=None)
def constants():
    gll, weights, values, slopes = basis_tables()
    by, dy = banded(values, EY), banded(slopes, EY)
    bz, dz = banded(values, EZ), banded(slopes, EZ)
    along = np.zeros((4 * EZ, 2 * WIDE))
    along[:, : 5 * EZ] = bz.T
    along[:, WIDE : WIDE + 5 * EZ] = dz.T
    kinds = np.zeros((3, ROWS, NODES))
    for a, (bx, side) in enumerate(((slopes, by), (values, dy), (values, by))):
        kinds[a, :100] = np.kron(bx, side)
    low = (1.0 - gll[:4]) / 2.0
    high = (1.0 + gll[:4]) / 2.0
    hat_y, hat_z = restrictor(gll, EY), restrictor(gll, EZ)
    rest = np.zeros((16, NODES))
    rest[0:4, :64] = np.kron(low[None, :], hat_y)
    rest[4:8, :64] = np.kron(high[None, :], hat_y)
    rest[4:8, 64:] = hat_y
    fold = np.zeros((8, 24))
    for c in range(3):
        for part in range(2):
            for k in range(4):
                fold[part * 4 + c, c * 8 + part * 4 + k] = 1.0
    quad_y = np.zeros((ROWS, EY))
    for r in range(5):
        for p in range(20):
            quad_y[r * 20 + p, p // 5] = weights[r] * weights[p % 5] / 8.0
    quad_z = np.zeros((EZ, WIDE))
    for q in range(5 * EZ):
        quad_z[q // 5, q] = weights[q % 5]
    return dict(
        along=stack_right(along),
        grads=stack_left(kinds.reshape(3 * ROWS, NODES)),
        back_xy=stack_left(np.concatenate([kinds[0].T, kinds[1].T], axis=1)),
        back_z=stack_left(kinds[2].T),
        back_along=stack_right(along.T),
        rest=stack_left(rest),
        tables=np.concatenate(
            [
                np.tile(hat_z.T, (1, 4)),
                np.pad(fold, ((0, 0), (0, 104))),
                np.pad(rest[:8].T, ((0, 0), (0, 120))),
            ],
            axis=0,
        ).astype(np.float32),
        quad_y=np.asarray(quad_y, np.float32),
        quad_z=np.asarray(quad_z, np.float32),
    )


def split(x):
    high = x.astype(BF16)
    return high, (x - high.astype(F32)).astype(BF16)


def dot(a, b):
    return jnp.dot(a, b, preferred_element_type=F32)


def exact(a, b):
    return jnp.dot(a, b, preferred_element_type=F32, precision=HIGHEST)


def under(x):
    high, low = split(x)
    return jnp.concatenate([high, low, high], axis=0)


def beside(x):
    high, low = split(x)
    return jnp.concatenate([high, low, high], axis=1)


def near(x):
    return pltpu.with_memory_space_constraint(x, pltpu.VMEM)


def call(body, outs, *operands, scratch=(), cost=None):
    vmem = pl.BlockSpec(memory_space=pltpu.VMEM)
    return pl.pallas_call(
        body,
        out_shape=[pltpu.VMEM(s, F32) for s in outs],
        in_specs=[vmem] * len(operands),
        out_specs=[vmem] * len(outs),
        scratch_shapes=list(scratch),
        cost_estimate=cost,
        compiler_params=pltpu.CompilerParams(vmem_limit_bytes=24 * 2**20),
    )(*[near(x) for x in operands])


def prepare_body(count, *refs):
    sources, refs = refs[:count], refs[count:]
    message, keep_rows, rows, weighting = refs[:4]
    targets, (halves_of, done) = refs[4:-2], refs[-2:]
    copies = [
        pltpu.make_async_copy(source, target, done.at[i])
        for i, (source, target) in enumerate(zip(sources, targets))
    ]
    urgent = (0, 1, count - 6, count - 5, count - 4)
    for i in urgent + tuple(i for i in range(count) if i not in urgent):
        copies[i].start()
    state, direction = targets[0], targets[1]
    clamp, owner, inverse, stiffness, quad_y, quad_z = targets[-6:]
    for i in (0, 1, count - 6, count - 5):
        copies[i].wait()
    eye = lax.broadcasted_iota(jnp.int32, (16, 16), 0) == lax.broadcasted_iota(
        jnp.int32, (16, 16), 1
    )
    lane = lax.broadcasted_iota(jnp.int32, (16, 128), 1)
    for x in range(4):
        row = clamp[x : x + 1, :].astype(F32)
        column = jnp.sum(jnp.where(eye, row, 0.0), axis=1, keepdims=True)
        keep = jnp.where(lane == 0, 1.0 - column, 1.0)
        keep_rows[x * 16 : (x + 1) * 16, :] = keep
        if x == 0:
            message[96:112, :] = keep
            message[112:120, :] = jnp.broadcast_to(owner[...].astype(F32), (8, 128))
            for c in range(3):
                message[c * 16 : (c + 1) * 16, :] = keep * direction[c, 0]
                message[48 + c * 16 : 48 + (c + 1) * 16, :] = state[c, 0]
    for i in range(count - 4, count):
        copies[i].wait()
    halves_of[0] = inverse[:, 0:128]
    halves_of[1] = jnp.concatenate([inverse[:, 128:192]] * 2, axis=1)
    low = lax.broadcasted_iota(jnp.int32, (32, 128), 1) < 64
    for b in range(2):
        for c in range(3):
            first, second = [pl.ds(b * 192 + c * 64 + q, 32, stride=2) for q in range(2)]
            values = (
                halves_of[0, first, :],
                jnp.where(low, halves_of[1, first, :], halves_of[1, second, :]),
                halves_of[0, second, :],
            )
            for i in range(3):
                rows[pl.ds(b * 32 * 9 + c * 3 + i, 32, stride=9), :] = values[i]
    weighting[...] = exact(exact(quad_y[...], stiffness[...]), quad_z[...])
    for i in range(2, count - 6):
        copies[i].wait()


def prepare(kept, used):
    operands = list(kept) + list(used)
    far = pl.BlockSpec(memory_space=pltpu.HBM)
    vmem = pl.BlockSpec(memory_space=pltpu.VMEM)
    made = [(120, 128), (64, 128), (576, 128), (ROWS, WIDE)]
    outs = [pltpu.VMEM(s, F32) for s in made] + [pltpu.VMEM(x.shape, x.dtype) for x in kept]
    return pl.pallas_call(
        functools.partial(prepare_body, len(operands)),
        out_shape=outs,
        in_specs=[far] * len(operands),
        out_specs=[vmem] * len(outs),
        scratch_shapes=[pltpu.VMEM(x.shape, x.dtype) for x in used]
        + [pltpu.VMEM((2, 384, 128), F32)]
        + [pltpu.SemaphoreType.DMA((len(operands),))],
        compiler_params=pltpu.CompilerParams(vmem_limit_bytes=24 * 2**20),
    )(*[pltpu.with_memory_space_constraint(x, pltpu.HBM) for x in operands])


def gradients(fields, along, grads, refs):
    lines = jnp.concatenate([f for field in fields for f in field], axis=0)
    flat = dot(beside(lines), along[...])
    for i, ref in enumerate(refs):
        parts = [flat[(3 * i + c) * NODES : (3 * i + c + 1) * NODES] for c in range(3)]
        plain = jnp.concatenate([p[:, :WIDE] for p in parts], axis=1)
        sloped = jnp.concatenate([p[:, WIDE:] for p in parts], axis=1)
        ref[0 : 2 * ROWS, :] = dot(grads[0 : 2 * ROWS, :], under(plain))
        ref[2 * ROWS :, :] = dot(grads[2 * ROWS :, :], under(sloped))


def physics(state_grad, grad, weighting, flux):
    pairs = ((0, 0), (1, 1), (2, 2), (0, 1), (0, 2), (1, 2))
    for start in range(0, LIVE, 8):
        here = slice(start, start + 8)
        w = weighting[here, :]

        def piece(ref, c, a):
            return ref[a * ROWS + start : a * ROWS + start + 8, c * WIDE : (c + 1) * WIDE]

        deform = [
            [piece(state_grad, c, a) + (1.0 if a == c else 0.0) for a in range(3)]
            for c in range(3)
        ]
        change = [[piece(grad, c, a) for a in range(3)] for c in range(3)]
        square = {
            (a, b): deform[0][a] * deform[0][b]
            + deform[1][a] * deform[1][b]
            + deform[2][a] * deform[2][b]
            for a, b in pairs
        }
        shift = 0.6 * (square[0, 0] + square[1, 1] + square[2, 2] - 3.0)
        held = {
            (a, b): w * (0.8 * (square[a, b] - 1.0) + shift) if a == b else (0.8 * w) * square[a, b]
            for a, b in pairs
        }
        cross = [
            [
                deform[0][a] * change[0][b] + deform[1][a] * change[1][b] + deform[2][a] * change[2][b]
                for b in range(3)
            ]
            for a in range(3)
        ]
        trace = (1.2 * w) * (cross[0][0] + cross[1][1] + cross[2][2])
        moved = {}
        for a, b in pairs:
            if a == b:
                moved[a, b] = (1.6 * w) * cross[a][b] + trace
            else:
                moved[a, b] = (0.8 * w) * (cross[a][b] + cross[b][a])
        for a in range(3):
            for c in range(3):
                entry = None
                for b in range(3):
                    key = (min(a, b), max(a, b))
                    term = change[c][b] * held[key] + deform[c][b] * moved[key]
                    entry = term if entry is None else entry + term
                flux[a * ROWS + start : a * ROWS + start + 8, c * WIDE : (c + 1) * WIDE] = entry
    for a in range(3):
        flux[a * ROWS + LIVE : (a + 1) * ROWS, :] = jnp.zeros((ROWS - LIVE, 3 * WIDE), F32)


def images(flux, back_xy, back_z, back_along):
    side_b = dot(back_xy[...], under(flux[0 : 2 * ROWS, :]))
    side_d = dot(back_z[...], under(flux[2 * ROWS :, :]))
    lines = jnp.concatenate(
        [
            jnp.concatenate(
                [side_b[:, c * WIDE : (c + 1) * WIDE], side_d[:, c * WIDE : (c + 1) * WIDE]], axis=1
            )
            for c in range(3)
        ],
        axis=0,
    )
    return dot(beside(lines), back_along[...])


def coarse_rows(extended, rest):
    levels = dot(rest[...], under(jnp.concatenate(extended, axis=1)))
    return jnp.concatenate([levels[:8, c * 128 : (c + 1) * 128] for c in range(3)], axis=0)


def own_rows(ref, c):
    return ref[c].reshape(64, 128)


def first_body(
    state, direction, rhs, keep_rows, halo, weighting, along, grads, back_xy, back_z, back_along,
    rest, tables, owner, state_grad, sums, grad, flux,
):
    keep = keep_rows[...]
    fields = [
        [jnp.concatenate([own_rows(state, c), halo[48 + c * 16 : 64 + c * 16, :]], axis=0) for c in range(3)],
        [
            jnp.concatenate([keep * own_rows(direction, c), halo[c * 16 : 16 + c * 16, :]], axis=0)
            for c in range(3)
        ],
    ]
    gradients(fields, along, grads, (state_grad, grad))
    physics(state_grad, grad, weighting, flux)
    image = images(flux, back_xy, back_z, back_along)
    keep_right = halo[96:112, :]
    extended = []
    for c in range(3):
        part = image[c * NODES : (c + 1) * NODES]
        own = own_rows(rhs, c) - keep * part[:64] - (1.0 - keep) * own_rows(direction, c)
        extended.append(jnp.concatenate([own, -keep_right * part[64:]], axis=0))
    levels = exact(coarse_rows(extended, rest), tables[0:128, :])
    row = lax.broadcasted_iota(jnp.int32, (24, 128), 0)
    lane = lax.broadcasted_iota(jnp.int32, (24, 128), 1)
    levels = jnp.where(lane // EZ == row % EY, levels, 0.0)
    levels = exact(tables[128:136, 0:24], levels)
    sums[0:4, :] = placed(levels, owner[...])[0:4]
    sums[4:8, :] = placed(levels, halo[112:113, :].astype(jnp.int32))[4:8]


def slots(owner):
    place = (owner % 2) * 64 + owner // 2
    return (lax.broadcasted_iota(jnp.int32, (128, 128), 0) == place).astype(BF16)


def placed(rows, owner):
    where = slots(owner)
    nt = (((1,), (1,)), ((), ()))
    return sum(lax.dot_general(part, where, nt, preferred_element_type=F32) for part in split(rows))


def solve_body(gathered, rows, owner, correction):
    tn = (((0,), (0,)), ((), ()))
    values = gathered[...]
    row = lax.broadcasted_iota(jnp.int32, (256, 256), 0)
    lane = lax.broadcasted_iota(jnp.int32, (256, 256), 1)
    side = lax.axis_index("grp") // 32
    holder = row // 8
    target = jnp.where(row % 8 < 4, holder, holder + 1 - jnp.where(holder % 8 == 7, 8 * side, 0))
    column = jnp.where(lane < 192, lane, lane - 64)
    match = (target == column % 64 // 2) & (row % 4 == column // 64)
    need = None
    for q in range(2):
        pick = (match & (column % 2 == q)).astype(BF16)
        for part in split(values[:, q * 64 : (q + 1) * 64]):
            term = lax.dot_general(part, pick, tn, preferred_element_type=F32)
            need = term if need is None else need + term
    low = lax.broadcasted_iota(jnp.int32, (64, 128), 1) < 64
    inner, outer = need[:, 0:128], need[:, 128:256]
    products = [[], []]
    for c in range(3):
        shared = rows[pl.ds(c * 3 + 1, 64, stride=9), :] * outer
        for q in range(2):
            own = rows[pl.ds(c * 3 + 2 * q, 64, stride=9), :] * inner
            products[q].append(own + jnp.where(low == (q == 0), shared, 0.0))
    products = products[0] + products[1]
    ones = jnp.ones((128, 128), BF16)
    sums = sum(dot(part, ones) for part in split(jnp.concatenate(products, axis=0)))
    lane = lax.broadcasted_iota(jnp.int32, (64, 128), 1)
    stacked = []
    for q in range(2):
        first, second, third = [sums[(q * 3 + c) * 64 : (q * 3 + c + 1) * 64] for c in range(3)]
        stacked.append(jnp.where(lane == 0, first, jnp.where(lane == 1, second, third)))
    stacked = jnp.concatenate(stacked, axis=0)[:, 0:8]
    where = slots(owner[...])
    correction[...] = sum(
        lax.dot_general(part, where, tn, preferred_element_type=F32) for part in split(stacked)
    )


def second_body(
    correction, right, state_grad, direction, rhs, keep_rows, halo, weighting, along, grads,
    back_xy, back_z, back_along, rest, tables, new, partial, message, own_coarse, grad, flux,
):
    keep = keep_rows[...]
    keep_right = halo[96:112, :]
    rows = jnp.concatenate(
        [
            jnp.broadcast_to(ref[c : c + 1, :], (4, 128))
            for c in range(3)
            for ref in (correction, right)
        ],
        axis=0,
    )
    row = lax.broadcasted_iota(jnp.int32, (24, 128), 0)
    lane = lax.broadcasted_iota(jnp.int32, (24, 128), 1)
    levels = lax.dot_general(
        jnp.where(lane // EZ == row % EY, rows, 0.0), tables[0:128, :], (((1,), (1,)), ((), ())),
        preferred_element_type=F32, precision=HIGHEST,
    )
    levels = jnp.concatenate([levels[c * 8 : (c + 1) * 8] for c in range(3)], axis=1)
    update = exact(tables[136:216, 0:8], levels)
    field = []
    fresh = []
    for c in range(3):
        piece = update[:, c * 128 : (c + 1) * 128]
        own = own_rows(direction, c) + keep * piece[:64]
        new[c] = own.reshape(4, 16, 128)
        fresh.append(own)
        field.append(
            jnp.concatenate(
                [keep * own, halo[c * 16 : 16 + c * 16, :] + keep_right * piece[64:]], axis=0
            )
        )
    gradients([field], along, grads, (grad,))
    physics(state_grad, grad, weighting, flux)
    image = images(flux, back_xy, back_z, back_along)
    extended = []
    for c in range(3):
        part = image[c * NODES : (c + 1) * NODES]
        own = own_rows(rhs, c) - keep * part[:64] - (1.0 - keep) * fresh[c]
        last = -keep_right * part[64:]
        partial[c] = own.reshape(4, 16, 128)
        message[c * 16 : (c + 1) * 16, :] = last
        extended.append(jnp.concatenate([own, last], axis=0))
    levels = exact(coarse_rows(extended, rest), tables[0:128, :])
    message[48:72, :] = levels
    for c in range(3):
        own_coarse[c] = levels[c * 8 : c * 8 + 4, :EZ]


def finish_body(partial, arrived, own_coarse, residual, coarse):
    for c in range(3):
        residual[c, 0] = partial[c, 0] + arrived[c * 16 : (c + 1) * 16, :]
        residual[c, 1:4] = partial[c, 1:4]
        coarse[c] = own_coarse[c] + arrived[52 + c * 8 : 56 + c * 8, :EZ]


def finish(partial, arrived, own_coarse):
    vmem = pl.BlockSpec(memory_space=pltpu.VMEM)
    return pl.pallas_call(
        finish_body,
        out_shape=[
            jax.ShapeDtypeStruct((3, 4, 16, 128), F32),
            jax.ShapeDtypeStruct((3, EY, EZ), F32),
        ],
        in_specs=[vmem] * 3,
        out_specs=[vmem] * 2,
        compiler_params=pltpu.CompilerParams(vmem_limit_bytes=24 * 2**20),
    )(near(partial), near(arrived), near(own_coarse))


def shifted(block, distance):
    axes = ("grp", "mem")
    count = lax.axis_size(axes)
    route = [(i - distance, i) for i in range(count) if 0 <= i - distance < count]
    return lax.ppermute(block, axes, route)


def ring():
    groups, members = lax.axis_size("grp"), lax.axis_size("mem")
    route = []
    for g in range(groups):
        route += [(g * members + m, g * members + m + 1) for m in range(members - 1)]
        last = g >= groups // 2 - 1 and g % 8 == 7
        to = g + 8 if last else g
        if to < groups:
            route.append((g * members + members - 1, to * members))
    return route


def shards(state, direction, rhs, clamp, stiffness, coarse_owner, coarse_inverse):
    k = constants()
    names = ("along", "grads", "back_xy", "back_z", "back_along", "rest", "tables")
    kept = [state, direction, rhs] + [jnp.asarray(k[name]) for name in names] + [coarse_owner]
    inverse = coarse_inverse.reshape(384, 192)
    used = [
        clamp, coarse_owner, inverse, stiffness[0],
        jnp.asarray(k["quad_y"]), jnp.asarray(k["quad_z"]),
    ]
    message, keep_rows, rows, weighting, state, direction, rhs, *shared, owner = prepare(kept, used)
    halo = shifted(message, -1)
    rows = lax.all_to_all(
        rows.reshape(576, 1, 128), "grp", split_axis=0, concat_axis=0, tiled=True
    ).reshape(576, 128)
    big = (3 * ROWS, 3 * WIDE)
    scratch = (pltpu.VMEM(big, F32), pltpu.VMEM(big, F32))
    state_grad, sums = call(
        first_body,
        [big, (8, 128)],
        state, direction, rhs, keep_rows, halo, weighting, *shared, owner,
        scratch=scratch, cost=pl.CostEstimate(flops=20000000000, bytes_accessed=4 * 10**6, transcendentals=0),
    )
    arrived = lax.ppermute(sums, ("grp", "mem"), ring())[4:8]
    wraps = lax.axis_index("mem") == 0
    total = jnp.concatenate(
        [sums[0:4] + jnp.where(wraps, 0.0, arrived), jnp.where(wraps, arrived, 0.0)], axis=0
    )
    total = jnp.broadcast_to(total[None], (32, 8, 128)).reshape(256, 128)
    total, rows = lax.optimization_barrier((total, rows))
    sides = [list(range(32)), list(range(32, 64))]
    gathered = lax.all_to_all(
        total, "grp", split_axis=0, concat_axis=0, tiled=True, axis_index_groups=sides
    )
    (correction,) = call(solve_body, [(8, 128)], gathered, rows, owner)
    right = shifted(correction, -1)
    field = (3, 4, 16, 128)
    new, partial, last, own_coarse = call(
        second_body,
        [field, field, (72, 128), (3, EY, EZ)],
        correction, right, state_grad, direction, rhs, keep_rows, halo, weighting, *shared,
        scratch=scratch,
    )
    residual, coarse = finish(partial, shifted(last, 1), own_coarse)
    return new, residual, coarse[:, None]


def solution(mesh):
    along = ("grp", "mem")
    field = P(None, along, None, None)
    in_specs = (
        field, field, field, P(along, None), P(along, None, None), P(along, None),
        P(along, None, None, None),
    )
    return jax.shard_map(
        shards, mesh=mesh, in_specs=in_specs, out_specs=(field, field, field), check_vma=False
    )
```

```python
import functools
import jax
import jax.numpy as jnp
import numpy as np
from jax import lax
from jax.experimental import pallas as pl
from jax.experimental.pallas import tpu as pltpu
from jax.sharding import PartitionSpec as P

F32 = jnp.float32
BF16 = jnp.bfloat16
HIGHEST = lax.Precision.HIGHEST
EY = 4
EZ = 32
ROWS = 112
LIVE = 104
WIDE = 256
NODES = 80


def basis_tables():
    gll = np.array([-1.0, -np.sqrt(3.0 / 7.0), 0.0, np.sqrt(3.0 / 7.0), 1.0])
    inner = np.sqrt(5.0 - 2.0 * np.sqrt(10.0 / 7.0)) / 3.0
    outer = np.sqrt(5.0 + 2.0 * np.sqrt(10.0 / 7.0)) / 3.0
    inner_weight = (322.0 + 13.0 * np.sqrt(70.0)) / 900.0
    outer_weight = (322.0 - 13.0 * np.sqrt(70.0)) / 900.0
    points = np.array([-outer, -inner, 0.0, inner, outer])
    weights = np.array([outer_weight, inner_weight, 128.0 / 225.0, inner_weight, outer_weight])
    values = np.zeros((5, 5))
    slopes = np.zeros((5, 5))
    for j in range(5):
        others = [gll[k] for k in range(5) if k != j]
        denominator = np.prod([gll[j] - o for o in others])
        for q in range(5):
            t = points[q]
            values[q, j] = np.prod([t - o for o in others]) / denominator
            total = 0.0
            for i in range(4):
                total += np.prod([t - others[k] for k in range(4) if k != i])
            slopes[q, j] = 2.0 * total / denominator
    return gll, weights, values, slopes


def banded(table, count):
    result = np.zeros((5 * count, 4 * count + 1))
    for e in range(count):
        result[5 * e : 5 * e + 5, 4 * e : 4 * e + 5] = table
    return result[:, :-1]


def restrictor(gll, count):
    result = np.zeros((count, 4 * count))
    for e in range(count):
        for j in range(4):
            result[e, 4 * e + j] += (1.0 - gll[j]) / 2.0
            if e + 1 < count:
                result[e + 1, 4 * e + j] += (1.0 + gll[j]) / 2.0
    return result


def halves(table):
    table = np.asarray(table, np.float32)
    high = table.astype(BF16)
    low = (table - high.astype(np.float32)).astype(BF16)
    return high, low


def stack_left(table):
    high, low = halves(table)
    return np.concatenate([high, high, low], axis=1)


def stack_right(table):
    high, low = halves(table)
    return np.concatenate([high, high, low], axis=0)


@functools.lru_cache(maxsize=None)
def constants():
    gll, weights, values, slopes = basis_tables()
    by, dy = banded(values, EY), banded(slopes, EY)
    bz, dz = banded(values, EZ), banded(slopes, EZ)
    along = np.zeros((4 * EZ, 2 * WIDE))
    along[:, : 5 * EZ] = bz.T
    along[:, WIDE : WIDE + 5 * EZ] = dz.T
    kinds = np.zeros((3, ROWS, NODES))
    for a, (bx, side) in enumerate(((slopes, by), (values, dy), (values, by))):
        kinds[a, :100] = np.kron(bx, side)
    low = (1.0 - gll[:4]) / 2.0
    high = (1.0 + gll[:4]) / 2.0
    hat_y, hat_z = restrictor(gll, EY), restrictor(gll, EZ)
    rest = np.zeros((16, NODES))
    rest[0:4, :64] = np.kron(low[None, :], hat_y)
    rest[4:8, :64] = np.kron(high[None, :], hat_y)
    rest[4:8, 64:] = hat_y
    fold = np.zeros((8, 24))
    for c in range(3):
        for part in range(2):
            for k in range(4):
                fold[part * 4 + c, c * 8 + part * 4 + k] = 1.0
    quad_y = np.zeros((ROWS, EY))
    for r in range(5):
        for p in range(20):
            quad_y[r * 20 + p, p // 5] = weights[r] * weights[p % 5] / 8.0
    quad_z = np.zeros((EZ, WIDE))
    for q in range(5 * EZ):
        quad_z[q // 5, q] = weights[q % 5]
    return dict(
        along=stack_right(along),
        grads=stack_left(kinds.reshape(3 * ROWS, NODES)),
        back_xy=stack_left(np.concatenate([kinds[0].T, kinds[1].T], axis=1)),
        back_z=stack_left(kinds[2].T),
        back_along=stack_right(along.T),
        rest=stack_left(rest),
        tables=np.concatenate(
            [
                np.tile(hat_z.T, (1, 4)),
                np.pad(fold, ((0, 0), (0, 104))),
                np.pad(rest[:8].T, ((0, 0), (0, 120))),
            ],
            axis=0,
        ).astype(np.float32),
        quad_y=np.asarray(quad_y, np.float32),
        quad_z=np.asarray(quad_z, np.float32),
    )


def split(x):
    high = x.astype(BF16)
    return high, (x - high.astype(F32)).astype(BF16)


def dot(a, b):
    return jnp.dot(a, b, preferred_element_type=F32)


def exact(a, b):
    return jnp.dot(a, b, preferred_element_type=F32, precision=HIGHEST)


def under(x):
    high, low = split(x)
    return jnp.concatenate([high, low, high], axis=0)


def beside(x):
    high, low = split(x)
    return jnp.concatenate([high, low, high], axis=1)


def near(x):
    return pltpu.with_memory_space_constraint(x, pltpu.VMEM)


def call(body, outs, *operands, scratch=()):
    vmem = pl.BlockSpec(memory_space=pltpu.VMEM)
    return pl.pallas_call(
        body,
        out_shape=[pltpu.VMEM(s, F32) for s in outs],
        in_specs=[vmem] * len(operands),
        out_specs=[vmem] * len(outs),
        scratch_shapes=list(scratch),
        compiler_params=pltpu.CompilerParams(vmem_limit_bytes=24 * 2**20),
    )(*[near(x) for x in operands])


def loads(pairs, done):
    copies = [
        pltpu.make_async_copy(source, target, done.at[i])
        for i, (source, target) in enumerate(pairs)
    ]
    for copy in copies:
        copy.start()
    return copies


def prepare_body(
    state_in, direction_in, clamp_in, owner_in, inverse_in, message, keep_rows, rows, state,
    direction, owner, clamp, inverse, halves_of, done,
):
    copies = loads(
        (
            (inverse_in, inverse),
            (inverse_in.at[:, 0:128], halves_of.at[0]),
            (clamp_in, clamp),
            (owner_in, owner),
            (direction_in, direction),
            (state_in, state),
        ),
        done,
    )
    for copy in copies[2:]:
        copy.wait()
    eye = lax.broadcasted_iota(jnp.int32, (16, 16), 0) == lax.broadcasted_iota(
        jnp.int32, (16, 16), 1
    )
    lane = lax.broadcasted_iota(jnp.int32, (16, 128), 1)
    for x in range(4):
        row = clamp[x : x + 1, :].astype(F32)
        column = jnp.sum(jnp.where(eye, row, 0.0), axis=1, keepdims=True)
        keep = jnp.where(lane == 0, 1.0 - column, 1.0)
        keep_rows[x * 16 : (x + 1) * 16, :] = keep
        if x == 0:
            message[96:112, :] = keep
            message[112:120, :] = jnp.broadcast_to(owner[...].astype(F32), (8, 128))
            for c in range(3):
                message[c * 16 : (c + 1) * 16, :] = keep * direction[c, 0]
                message[48 + c * 16 : 48 + (c + 1) * 16, :] = state[c, 0]
    for copy in copies[:2]:
        copy.wait()
    halves_of[1] = jnp.concatenate([inverse[:, 128:192]] * 2, axis=1)
    low = lax.broadcasted_iota(jnp.int32, (32, 128), 1) < 64
    for b in range(2):
        for c in range(3):
            first, second = [pl.ds(b * 192 + c * 64 + q, 32, stride=2) for q in range(2)]
            values = (
                halves_of[0, first, :],
                jnp.where(low, halves_of[1, first, :], halves_of[1, second, :]),
                halves_of[0, second, :],
            )
            for i in range(3):
                rows[pl.ds(b * 32 * 9 + c * 3 + i, 32, stride=9), :] = values[i]


def prepare(state, direction, clamp, owner, inverse):
    operands = (state, direction, clamp, owner, inverse)
    far = pl.BlockSpec(memory_space=pltpu.HBM)
    vmem = pl.BlockSpec(memory_space=pltpu.VMEM)
    outs = [pltpu.VMEM(s, F32) for s in ((120, 128), (64, 128), (576, 128))] + [
        pltpu.VMEM(x.shape, x.dtype) for x in (state, direction, owner)
    ]
    return pl.pallas_call(
        prepare_body,
        out_shape=outs,
        in_specs=[far] * len(operands),
        out_specs=[vmem] * len(outs),
        scratch_shapes=[
            pltpu.VMEM(clamp.shape, clamp.dtype),
            pltpu.VMEM(inverse.shape, F32),
            pltpu.VMEM((2, 384, 128), F32),
            pltpu.SemaphoreType.DMA((6,)),
        ],
        compiler_params=pltpu.CompilerParams(vmem_limit_bytes=24 * 2**20),
    )(*[pltpu.with_memory_space_constraint(x, pltpu.HBM) for x in operands])


def gradients(fields, along, grads, refs):
    lines = jnp.concatenate([f for field in fields for f in field], axis=0)
    flat = dot(beside(lines), along[...])
    for i, ref in enumerate(refs):
        parts = [flat[(3 * i + c) * NODES : (3 * i + c + 1) * NODES] for c in range(3)]
        plain = jnp.concatenate([p[:, :WIDE] for p in parts], axis=1)
        sloped = jnp.concatenate([p[:, WIDE:] for p in parts], axis=1)
        ref[0 : 2 * ROWS, :] = dot(grads[0 : 2 * ROWS, :], under(plain))
        ref[2 * ROWS :, :] = dot(grads[2 * ROWS :, :], under(sloped))


def physics(state_grad, grad, weighting, flux):
    pairs = ((0, 0), (1, 1), (2, 2), (0, 1), (0, 2), (1, 2))
    for start in range(0, LIVE, 8):
        here = slice(start, start + 8)
        w = weighting[here, :]

        def piece(ref, c, a):
            return ref[a * ROWS + start : a * ROWS + start + 8, c * WIDE : (c + 1) * WIDE]

        deform = [
            [piece(state_grad, c, a) + (1.0 if a == c else 0.0) for a in range(3)]
            for c in range(3)
        ]
        change = [[piece(grad, c, a) for a in range(3)] for c in range(3)]
        square = {
            (a, b): deform[0][a] * deform[0][b]
            + deform[1][a] * deform[1][b]
            + deform[2][a] * deform[2][b]
            for a, b in pairs
        }
        shift = 0.6 * (square[0, 0] + square[1, 1] + square[2, 2] - 3.0)
        held = {
            (a, b): w * (0.8 * (square[a, b] - 1.0) + shift) if a == b else (0.8 * w) * square[a, b]
            for a, b in pairs
        }
        cross = [
            [
                deform[0][a] * change[0][b] + deform[1][a] * change[1][b] + deform[2][a] * change[2][b]
                for b in range(3)
            ]
            for a in range(3)
        ]
        trace = (1.2 * w) * (cross[0][0] + cross[1][1] + cross[2][2])
        moved = {}
        for a, b in pairs:
            if a == b:
                moved[a, b] = (1.6 * w) * cross[a][b] + trace
            else:
                moved[a, b] = (0.8 * w) * (cross[a][b] + cross[b][a])
        for a in range(3):
            for c in range(3):
                entry = None
                for b in range(3):
                    key = (min(a, b), max(a, b))
                    term = change[c][b] * held[key] + deform[c][b] * moved[key]
                    entry = term if entry is None else entry + term
                flux[a * ROWS + start : a * ROWS + start + 8, c * WIDE : (c + 1) * WIDE] = entry
    for a in range(3):
        flux[a * ROWS + LIVE : (a + 1) * ROWS, :] = jnp.zeros((ROWS - LIVE, 3 * WIDE), F32)


def images(flux, back_xy, back_z, back_along):
    side_b = dot(back_xy[...], under(flux[0 : 2 * ROWS, :]))
    side_d = dot(back_z[...], under(flux[2 * ROWS :, :]))
    lines = jnp.concatenate(
        [
            jnp.concatenate(
                [side_b[:, c * WIDE : (c + 1) * WIDE], side_d[:, c * WIDE : (c + 1) * WIDE]], axis=1
            )
            for c in range(3)
        ],
        axis=0,
    )
    return dot(beside(lines), back_along[...])


def coarse_rows(extended, rest):
    levels = dot(rest[...], under(jnp.concatenate(extended, axis=1)))
    return jnp.concatenate([levels[:8, c * 128 : (c + 1) * 128] for c in range(3)], axis=0)


def first_apply(ready, kept, used, scratch):
    far = pl.BlockSpec(memory_space=pltpu.HBM)
    vmem = pl.BlockSpec(memory_space=pltpu.VMEM)
    made = [(3 * ROWS, 3 * WIDE), (8, 128), (ROWS, WIDE)]
    outs = [pltpu.VMEM(s, F32) for s in made] + [pltpu.VMEM(x.shape, x.dtype) for x in kept]
    return pl.pallas_call(
        first_body,
        out_shape=outs,
        in_specs=[vmem] * len(ready) + [far] * (len(kept) + len(used)),
        out_specs=[vmem] * len(outs),
        scratch_shapes=[pltpu.VMEM(x.shape, x.dtype) for x in used]
        + scratch
        + [pltpu.SemaphoreType.DMA((len(kept) + len(used),))],
        cost_estimate=pl.CostEstimate(flops=2 * 10**10, bytes_accessed=4 * 10**6, transcendentals=0),
        compiler_params=pltpu.CompilerParams(vmem_limit_bytes=24 * 2**20),
    )(
        *[near(x) for x in ready],
        *[pltpu.with_memory_space_constraint(x, pltpu.HBM) for x in kept + used],
    )


def own_rows(ref, c):
    return ref[c].reshape(64, 128)


def first_body(
    state, direction, keep_rows, halo, owner, rhs_in, along_in, grads_in, xy_in, z_in, back_in,
    rest_in, tables_in, stiffness_in, quad_y_in, quad_z_in, state_grad, sums, weighting, rhs, along,
    grads, back_xy, back_z, back_along, rest, tables, stiffness, quad_y, quad_z, grad, flux, done,
):
    copies = loads(
        (
            (along_in, along),
            (grads_in, grads),
            (stiffness_in, stiffness),
            (quad_y_in, quad_y),
            (quad_z_in, quad_z),
            (xy_in, back_xy),
            (z_in, back_z),
            (back_in, back_along),
            (rhs_in, rhs),
            (rest_in, rest),
            (tables_in, tables),
        ),
        done,
    )
    keep = keep_rows[...]
    fields = [
        [jnp.concatenate([own_rows(state, c), halo[48 + c * 16 : 64 + c * 16, :]], axis=0) for c in range(3)],
        [
            jnp.concatenate([keep * own_rows(direction, c), halo[c * 16 : 16 + c * 16, :]], axis=0)
            for c in range(3)
        ],
    ]
    for copy in copies[:5]:
        copy.wait()
    weighting[...] = exact(exact(quad_y[...], stiffness[...]), quad_z[...])
    gradients(fields, along, grads, (state_grad, grad))
    for copy in copies[5:]:
        copy.wait()
    physics(state_grad, grad, weighting, flux)
    image = images(flux, back_xy, back_z, back_along)
    keep_right = halo[96:112, :]
    extended = []
    for c in range(3):
        part = image[c * NODES : (c + 1) * NODES]
        own = own_rows(rhs, c) - keep * part[:64] - (1.0 - keep) * own_rows(direction, c)
        extended.append(jnp.concatenate([own, -keep_right * part[64:]], axis=0))
    levels = exact(coarse_rows(extended, rest), tables[0:128, :])
    row = lax.broadcasted_iota(jnp.int32, (24, 128), 0)
    lane = lax.broadcasted_iota(jnp.int32, (24, 128), 1)
    levels = jnp.where(lane // EZ == row % EY, levels, 0.0)
    levels = exact(tables[128:136, 0:24], levels)
    sums[0:4, :] = placed(levels, owner[...])[0:4]
    sums[4:8, :] = placed(levels, halo[112:113, :].astype(jnp.int32))[4:8]


def slots(owner):
    place = (owner % 2) * 64 + owner // 2
    return (lax.broadcasted_iota(jnp.int32, (128, 128), 0) == place).astype(BF16)


def placed(rows, owner):
    where = slots(owner)
    nt = (((1,), (1,)), ((), ()))
    return sum(lax.dot_general(part, where, nt, preferred_element_type=F32) for part in split(rows))


def solve_body(gathered, rows, owner, correction):
    tn = (((0,), (0,)), ((), ()))
    values = gathered[...]
    row = lax.broadcasted_iota(jnp.int32, (256, 256), 0)
    lane = lax.broadcasted_iota(jnp.int32, (256, 256), 1)
    side = lax.axis_index("grp") // 32
    holder = row // 8
    target = jnp.where(row % 8 < 4, holder, holder + 1 - jnp.where(holder % 8 == 7, 8 * side, 0))
    column = jnp.where(lane < 192, lane, lane - 64)
    match = (target == column % 64 // 2) & (row % 4 == column // 64)
    need = None
    for q in range(2):
        pick = (match & (column % 2 == q)).astype(BF16)
        for part in split(values[:, q * 64 : (q + 1) * 64]):
            term = lax.dot_general(part, pick, tn, preferred_element_type=F32)
            need = term if need is None else need + term
    low = lax.broadcasted_iota(jnp.int32, (64, 128), 1) < 64
    inner, outer = need[:, 0:128], need[:, 128:256]
    products = [[], []]
    for c in range(3):
        shared = rows[pl.ds(c * 3 + 1, 64, stride=9), :] * outer
        for q in range(2):
            own = rows[pl.ds(c * 3 + 2 * q, 64, stride=9), :] * inner
            products[q].append(own + jnp.where(low == (q == 0), shared, 0.0))
    products = products[0] + products[1]
    ones = jnp.ones((128, 128), BF16)
    sums = sum(dot(part, ones) for part in split(jnp.concatenate(products, axis=0)))
    lane = lax.broadcasted_iota(jnp.int32, (64, 128), 1)
    stacked = []
    for q in range(2):
        first, second, third = [sums[(q * 3 + c) * 64 : (q * 3 + c + 1) * 64] for c in range(3)]
        stacked.append(jnp.where(lane == 0, first, jnp.where(lane == 1, second, third)))
    stacked = jnp.concatenate(stacked, axis=0)[:, 0:8]
    where = slots(owner[...])
    correction[...] = sum(
        lax.dot_general(part, where, tn, preferred_element_type=F32) for part in split(stacked)
    )


def second_body(
    correction, right, state_grad, direction, rhs, keep_rows, halo, weighting, along, grads,
    back_xy, back_z, back_along, rest, tables, new, partial, message, own_coarse, grad, flux,
):
    keep = keep_rows[...]
    keep_right = halo[96:112, :]
    rows = jnp.concatenate(
        [
            jnp.broadcast_to(ref[c : c + 1, :], (4, 128))
            for c in range(3)
            for ref in (correction, right)
        ],
        axis=0,
    )
    row = lax.broadcasted_iota(jnp.int32, (24, 128), 0)
    lane = lax.broadcasted_iota(jnp.int32, (24, 128), 1)
    levels = lax.dot_general(
        jnp.where(lane // EZ == row % EY, rows, 0.0), tables[0:128, :], (((1,), (1,)), ((), ())),
        preferred_element_type=F32, precision=HIGHEST,
    )
    levels = jnp.concatenate([levels[c * 8 : (c + 1) * 8] for c in range(3)], axis=1)
    update = exact(tables[136:216, 0:8], levels)
    field = []
    fresh = []
    for c in range(3):
        piece = update[:, c * 128 : (c + 1) * 128]
        own = own_rows(direction, c) + keep * piece[:64]
        new[c] = own.reshape(4, 16, 128)
        fresh.append(own)
        field.append(
            jnp.concatenate(
                [keep * own, halo[c * 16 : 16 + c * 16, :] + keep_right * piece[64:]], axis=0
            )
        )
    gradients([field], along, grads, (grad,))
    physics(state_grad, grad, weighting, flux)
    image = images(flux, back_xy, back_z, back_along)
    extended = []
    for c in range(3):
        part = image[c * NODES : (c + 1) * NODES]
        own = own_rows(rhs, c) - keep * part[:64] - (1.0 - keep) * fresh[c]
        last = -keep_right * part[64:]
        partial[c] = own.reshape(4, 16, 128)
        message[c * 16 : (c + 1) * 16, :] = last
        extended.append(jnp.concatenate([own, last], axis=0))
    levels = exact(coarse_rows(extended, rest), tables[0:128, :])
    message[48:72, :] = levels
    for c in range(3):
        own_coarse[c] = levels[c * 8 : c * 8 + 4, :EZ]


def finish_body(partial, arrived, own_coarse, residual, coarse):
    for c in range(3):
        residual[c, 0] = partial[c, 0] + arrived[c * 16 : (c + 1) * 16, :]
        residual[c, 1:4] = partial[c, 1:4]
        coarse[c] = own_coarse[c] + arrived[52 + c * 8 : 56 + c * 8, :EZ]


def finish(partial, arrived, own_coarse):
    vmem = pl.BlockSpec(memory_space=pltpu.VMEM)
    return pl.pallas_call(
        finish_body,
        out_shape=[
            jax.ShapeDtypeStruct((3, 4, 16, 128), F32),
            jax.ShapeDtypeStruct((3, EY, EZ), F32),
        ],
        in_specs=[vmem] * 3,
        out_specs=[vmem] * 2,
        compiler_params=pltpu.CompilerParams(vmem_limit_bytes=24 * 2**20),
    )(near(partial), near(arrived), near(own_coarse))


def shifted(block, distance):
    axes = ("grp", "mem")
    count = lax.axis_size(axes)
    route = [(i - distance, i) for i in range(count) if 0 <= i - distance < count]
    return lax.ppermute(block, axes, route)


def ring():
    groups, members = lax.axis_size("grp"), lax.axis_size("mem")
    route = []
    for g in range(groups):
        route += [(g * members + m, g * members + m + 1) for m in range(members - 1)]
        last = g >= groups // 2 - 1 and g % 8 == 7
        to = g + 8 if last else g
        if to < groups:
            route.append((g * members + members - 1, to * members))
    return route


def shards(state, direction, rhs, clamp, stiffness, coarse_owner, coarse_inverse):
    k = constants()
    names = ("along", "grads", "back_xy", "back_z", "back_along", "rest", "tables")
    message, keep_rows, rows, state, direction, owner = prepare(
        state, direction, clamp, coarse_owner, coarse_inverse.reshape(384, 192)
    )
    halo = shifted(message, -1)
    rows = lax.all_to_all(
        rows.reshape(576, 1, 128), "grp", split_axis=0, concat_axis=0, tiled=True
    ).reshape(576, 128)
    scratch = [pltpu.VMEM((3 * ROWS, 3 * WIDE), F32)] * 2
    state_grad, sums, weighting, rhs, *shared = first_apply(
        (state, direction, keep_rows, halo, owner),
        (rhs, *[jnp.asarray(k[name]) for name in names]),
        (stiffness[0], jnp.asarray(k["quad_y"]), jnp.asarray(k["quad_z"])),
        scratch,
    )
    arrived = lax.ppermute(sums, ("grp", "mem"), ring())[4:8]
    wraps = lax.axis_index("mem") == 0
    total = jnp.concatenate(
        [sums[0:4] + jnp.where(wraps, 0.0, arrived), jnp.where(wraps, arrived, 0.0)], axis=0
    )
    total = jnp.broadcast_to(total[None], (32, 8, 128)).reshape(256, 128)
    total, rows = lax.optimization_barrier((total, rows))
    sides = [list(range(32)), list(range(32, 64))]
    gathered = lax.all_to_all(
        total, "grp", split_axis=0, concat_axis=0, tiled=True, axis_index_groups=sides
    )
    (correction,) = call(solve_body, [(8, 128)], gathered, rows, owner)
    right = shifted(correction, -1)
    field = (3, 4, 16, 128)
    new, partial, last, own_coarse = call(
        second_body,
        [field, field, (72, 128), (3, EY, EZ)],
        correction, right, state_grad, direction, rhs, keep_rows, halo, weighting, *shared,
        scratch=scratch,
    )
    residual, coarse = finish(partial, shifted(last, 1), own_coarse)
    return new, residual, coarse[:, None]


def solution(mesh):
    along = ("grp", "mem")
    field = P(None, along, None, None)
    in_specs = (
        field, field, field, P(along, None), P(along, None, None), P(along, None),
        P(along, None, None, None),
    )
    return jax.shard_map(
        shards, mesh=mesh, in_specs=in_specs, out_specs=(field, field, field), check_vma=False
    )
```

```python
import functools
import jax
import jax.numpy as jnp
import numpy as np
from jax import lax
from jax.experimental import pallas as pl
from jax.experimental.pallas import tpu as pltpu
from jax.sharding import PartitionSpec as P

F32 = jnp.float32
BF16 = jnp.bfloat16
HIGHEST = lax.Precision.HIGHEST
EY = 4
EZ = 32
ROWS = 112
LIVE = 104
WIDE = 256
NODES = 80


def basis_tables():
    gll = np.array([-1.0, -np.sqrt(3.0 / 7.0), 0.0, np.sqrt(3.0 / 7.0), 1.0])
    inner = np.sqrt(5.0 - 2.0 * np.sqrt(10.0 / 7.0)) / 3.0
    outer = np.sqrt(5.0 + 2.0 * np.sqrt(10.0 / 7.0)) / 3.0
    inner_weight = (322.0 + 13.0 * np.sqrt(70.0)) / 900.0
    outer_weight = (322.0 - 13.0 * np.sqrt(70.0)) / 900.0
    points = np.array([-outer, -inner, 0.0, inner, outer])
    weights = np.array([outer_weight, inner_weight, 128.0 / 225.0, inner_weight, outer_weight])
    values = np.zeros((5, 5))
    slopes = np.zeros((5, 5))
    for j in range(5):
        others = [gll[k] for k in range(5) if k != j]
        denominator = np.prod([gll[j] - o for o in others])
        for q in range(5):
            t = points[q]
            values[q, j] = np.prod([t - o for o in others]) / denominator
            total = 0.0
            for i in range(4):
                total += np.prod([t - others[k] for k in range(4) if k != i])
            slopes[q, j] = 2.0 * total / denominator
    return gll, weights, values, slopes


def banded(table, count):
    result = np.zeros((5 * count, 4 * count + 1))
    for e in range(count):
        result[5 * e : 5 * e + 5, 4 * e : 4 * e + 5] = table
    return result[:, :-1]


def restrictor(gll, count):
    result = np.zeros((count, 4 * count))
    for e in range(count):
        for j in range(4):
            result[e, 4 * e + j] += (1.0 - gll[j]) / 2.0
            if e + 1 < count:
                result[e + 1, 4 * e + j] += (1.0 + gll[j]) / 2.0
    return result


def halves(table):
    table = np.asarray(table, np.float32)
    high = table.astype(BF16)
    low = (table - high.astype(np.float32)).astype(BF16)
    return high, low


def stack_left(table):
    high, low = halves(table)
    return np.concatenate([high, high, low], axis=1)


def stack_right(table):
    return np.concatenate(halves(table), axis=0)


@functools.lru_cache(maxsize=None)
def constants():
    gll, weights, values, slopes = basis_tables()
    by, dy = banded(values, EY), banded(slopes, EY)
    bz, dz = banded(values, EZ), banded(slopes, EZ)
    along = np.zeros((4 * EZ, 2 * WIDE))
    along[:, : 5 * EZ] = bz.T
    along[:, WIDE : WIDE + 5 * EZ] = dz.T
    kinds = np.zeros((3, ROWS, NODES))
    for a, (bx, side) in enumerate(((slopes, by), (values, dy), (values, by))):
        kinds[a, :100] = np.kron(bx, side)
    low = (1.0 - gll[:4]) / 2.0
    high = (1.0 + gll[:4]) / 2.0
    hat_y, hat_z = restrictor(gll, EY), restrictor(gll, EZ)
    rest = np.zeros((16, NODES))
    rest[0:4, :64] = np.kron(low[None, :], hat_y)
    rest[4:8, :64] = np.kron(high[None, :], hat_y)
    rest[4:8, 64:] = hat_y
    fold = np.zeros((8, 24))
    for c in range(3):
        for part in range(2):
            for k in range(4):
                fold[part * 4 + c, c * 8 + part * 4 + k] = 1.0
    quad_y = np.zeros((ROWS, EY))
    for r in range(5):
        for p in range(20):
            quad_y[r * 20 + p, p // 5] = weights[r] * weights[p % 5] / 8.0
    quad_z = np.zeros((EZ, WIDE))
    for q in range(5 * EZ):
        quad_z[q // 5, q] = weights[q % 5]
    return dict(
        along=stack_right(along),
        grads=stack_left(kinds.reshape(3 * ROWS, NODES)),
        back_xy=stack_left(np.concatenate([kinds[0].T, kinds[1].T], axis=1)),
        back_z=stack_left(kinds[2].T),
        back_along=stack_right(along.T),
        rest=stack_left(rest),
        hat_down=stack_right(np.tile(hat_z.T, (1, 4))),
        hat_up=stack_right(np.tile(hat_z, (4, 1))),
        fold=np.pad(np.concatenate([fold, fold], axis=1), ((0, 8), (0, 0))).astype(BF16),
        spread=stack_left(rest[:8].T),
        quad_y=np.asarray(quad_y, np.float32),
        quad_z=np.asarray(quad_z, np.float32),
    )


def split(x):
    high = x.astype(BF16)
    return high, (x - high.astype(F32)).astype(BF16)


def dot(a, b):
    return jnp.dot(a, b, preferred_element_type=F32)


def exact(a, b):
    return jnp.dot(a, b, preferred_element_type=F32, precision=HIGHEST)


def under(x):
    high, low = split(x)
    return jnp.concatenate([high, low, high], axis=0)


def beside(x):
    high, low = split(x)
    return jnp.concatenate([high, low, high], axis=1)


def near(x):
    return pltpu.with_memory_space_constraint(x, pltpu.VMEM)


def thrice(ref):
    half = ref.shape[0] // 2
    return jnp.concatenate([ref[0:half, :], ref[0:half, :], ref[half:, :]], axis=0)


def call(body, outs, *operands, scratch=(), cost=None):
    vmem = pl.BlockSpec(memory_space=pltpu.VMEM)
    return pl.pallas_call(
        body,
        out_shape=[pltpu.VMEM(s, F32) for s in outs],
        in_specs=[vmem] * len(operands),
        out_specs=[vmem] * len(outs),
        scratch_shapes=list(scratch),
        cost_estimate=cost,
        compiler_params=pltpu.CompilerParams(vmem_limit_bytes=24 * 2**20),
    )(*[near(x) for x in operands])


def prepare_body(count, *refs):
    sources, refs = refs[:count], refs[count:]
    message, keep_rows, rows, weighting = refs[:4]
    targets, (halves_of, done) = refs[4:-2], refs[-2:]
    copies = [
        pltpu.make_async_copy(source, target, done.at[i])
        for i, (source, target) in enumerate(zip(sources, targets))
    ]
    urgent = (0, 1, count - 6, count - 5, count - 4)
    for i in urgent + tuple(i for i in range(count) if i not in urgent):
        copies[i].start()
    state, direction = targets[0], targets[1]
    clamp, owner, inverse, stiffness, quad_y, quad_z = targets[-6:]
    for i in (0, 1, count - 6, count - 5):
        copies[i].wait()
    eye = lax.broadcasted_iota(jnp.int32, (16, 16), 0) == lax.broadcasted_iota(
        jnp.int32, (16, 16), 1
    )
    lane = lax.broadcasted_iota(jnp.int32, (16, 128), 1)
    for x in range(4):
        row = clamp[x : x + 1, :].astype(F32)
        column = jnp.sum(jnp.where(eye, row, 0.0), axis=1, keepdims=True)
        keep = jnp.where(lane == 0, 1.0 - column, 1.0)
        keep_rows[x * 16 : (x + 1) * 16, :] = keep
        if x == 0:
            message[96:112, :] = keep
            message[112:120, :] = jnp.broadcast_to(owner[...].astype(F32), (8, 128))
            for c in range(3):
                message[c * 16 : (c + 1) * 16, :] = keep * direction[c, 0]
                message[48 + c * 16 : 48 + (c + 1) * 16, :] = state[c, 0]
    for i in range(count - 4, count):
        copies[i].wait()
    halves_of[0] = inverse[:, 0:128]
    halves_of[1] = jnp.concatenate([inverse[:, 128:192]] * 2, axis=1)
    low = lax.broadcasted_iota(jnp.int32, (32, 128), 1) < 64
    for b in range(2):
        for c in range(3):
            first, second = [pl.ds(b * 192 + c * 64 + q, 32, stride=2) for q in range(2)]
            values = (
                halves_of[0, first, :],
                jnp.where(low, halves_of[1, first, :], halves_of[1, second, :]),
                halves_of[0, second, :],
            )
            for i in range(3):
                rows[pl.ds(b * 32 * 9 + c * 3 + i, 32, stride=9), :] = values[i]
    weighting[...] = exact(exact(quad_y[...], stiffness[...]), quad_z[...])
    for i in range(2, count - 6):
        copies[i].wait()


def prepare(kept, used):
    operands = list(kept) + list(used)
    far = pl.BlockSpec(memory_space=pltpu.HBM)
    vmem = pl.BlockSpec(memory_space=pltpu.VMEM)
    made = [(120, 128), (64, 128), (576, 128), (ROWS, WIDE)]
    outs = [pltpu.VMEM(s, F32) for s in made] + [pltpu.VMEM(x.shape, x.dtype) for x in kept]
    return pl.pallas_call(
        functools.partial(prepare_body, len(operands)),
        out_shape=outs,
        in_specs=[far] * len(operands),
        out_specs=[vmem] * len(outs),
        scratch_shapes=[pltpu.VMEM(x.shape, x.dtype) for x in used]
        + [pltpu.VMEM((2, 384, 128), F32)]
        + [pltpu.SemaphoreType.DMA((len(operands),))],
        compiler_params=pltpu.CompilerParams(vmem_limit_bytes=24 * 2**20),
    )(*[pltpu.with_memory_space_constraint(x, pltpu.HBM) for x in operands])


def gradients(fields, along, grads, refs):
    lines = jnp.concatenate([f for field in fields for f in field], axis=0)
    flat = dot(beside(lines), thrice(along))
    for i, ref in enumerate(refs):
        parts = [flat[(3 * i + c) * NODES : (3 * i + c + 1) * NODES] for c in range(3)]
        plain = jnp.concatenate([p[:, :WIDE] for p in parts], axis=1)
        sloped = jnp.concatenate([p[:, WIDE:] for p in parts], axis=1)
        ref[0 : 2 * ROWS, :] = dot(grads[0 : 2 * ROWS, :], under(plain))
        ref[2 * ROWS :, :] = dot(grads[2 * ROWS :, :], under(sloped))


def physics(state_grad, grad, weighting, stress, flux, fresh):
    pairs = ((0, 0), (1, 1), (2, 2), (0, 1), (0, 2), (1, 2))
    for start in range(0, LIVE, 8):
        here = slice(start, start + 8)
        w = weighting[here, :]

        def piece(ref, c, a):
            return ref[a * ROWS + start : a * ROWS + start + 8, c * WIDE : (c + 1) * WIDE]

        deform = [
            [piece(state_grad, c, a) + (1.0 if a == c else 0.0) for a in range(3)]
            for c in range(3)
        ]
        change = [[piece(grad, c, a) for a in range(3)] for c in range(3)]
        if fresh:
            square = {
                (a, b): deform[0][a] * deform[0][b]
                + deform[1][a] * deform[1][b]
                + deform[2][a] * deform[2][b]
                for a, b in pairs
            }
            shift = 0.6 * (square[0, 0] + square[1, 1] + square[2, 2] - 3.0)
            held = {
                (a, b): w * (0.8 * (square[a, b] - 1.0) + shift) if a == b else (0.8 * w) * square[a, b]
                for a, b in pairs
            }
            for i, pair in enumerate(pairs):
                stress[i, here, :] = held[pair]
        else:
            held = {pair: stress[i, here, :] for i, pair in enumerate(pairs)}
        cross = [
            [
                deform[0][a] * change[0][b] + deform[1][a] * change[1][b] + deform[2][a] * change[2][b]
                for b in range(3)
            ]
            for a in range(3)
        ]
        trace = (1.2 * w) * (cross[0][0] + cross[1][1] + cross[2][2])
        moved = {}
        for a, b in pairs:
            if a == b:
                moved[a, b] = (1.6 * w) * cross[a][b] + trace
            else:
                moved[a, b] = (0.8 * w) * (cross[a][b] + cross[b][a])
        for a in range(3):
            for c in range(3):
                entry = None
                for b in range(3):
                    key = (min(a, b), max(a, b))
                    term = change[c][b] * held[key] + deform[c][b] * moved[key]
                    entry = term if entry is None else entry + term
                flux[a * ROWS + start : a * ROWS + start + 8, c * WIDE : (c + 1) * WIDE] = entry
    for a in range(3):
        flux[a * ROWS + LIVE : (a + 1) * ROWS, :] = jnp.zeros((ROWS - LIVE, 3 * WIDE), F32)


def images(flux, back_xy, back_z, back_along):
    side_b = dot(back_xy[...], under(flux[0 : 2 * ROWS, :]))
    side_d = dot(back_z[...], under(flux[2 * ROWS :, :]))
    lines = jnp.concatenate(
        [
            jnp.concatenate(
                [side_b[:, c * WIDE : (c + 1) * WIDE], side_d[:, c * WIDE : (c + 1) * WIDE]], axis=1
            )
            for c in range(3)
        ],
        axis=0,
    )
    return dot(beside(lines), thrice(back_along))


def coarse_rows(extended, rest):
    levels = dot(rest[...], under(jnp.concatenate(extended, axis=1)))
    return jnp.concatenate([levels[:8, c * 128 : (c + 1) * 128] for c in range(3)], axis=0)


def own_rows(ref, c):
    return ref[c].reshape(64, 128)


def first_body(
    state, direction, rhs, keep_rows, halo, weighting, along, grads, back_xy, back_z, back_along,
    rest, hat_down, hat_up, fold, spread, owner, state_grad, stress, sums, grad, flux,
):
    keep = keep_rows[...]
    fields = [
        [jnp.concatenate([own_rows(state, c), halo[48 + c * 16 : 64 + c * 16, :]], axis=0) for c in range(3)],
        [
            jnp.concatenate([keep * own_rows(direction, c), halo[c * 16 : 16 + c * 16, :]], axis=0)
            for c in range(3)
        ],
    ]
    gradients(fields, along, grads, (state_grad, grad))
    physics(state_grad, grad, weighting, stress, flux, True)
    image = images(flux, back_xy, back_z, back_along)
    keep_right = halo[96:112, :]
    extended = []
    for c in range(3):
        part = image[c * NODES : (c + 1) * NODES]
        own = own_rows(rhs, c) - keep * part[:64] - (1.0 - keep) * own_rows(direction, c)
        extended.append(jnp.concatenate([own, -keep_right * part[64:]], axis=0))
    levels = dot(beside(coarse_rows(extended, rest)), thrice(hat_down))
    row = lax.broadcasted_iota(jnp.int32, (24, 128), 0)
    lane = lax.broadcasted_iota(jnp.int32, (24, 128), 1)
    levels = jnp.where(lane // EZ == row % EY, levels, 0.0)
    levels = dot(fold[...], jnp.concatenate(split(levels), axis=0))[0:8]
    sums[0:4, :] = placed(levels, owner[...])[0:4]
    sums[4:8, :] = placed(levels, halo[112:113, :].astype(jnp.int32))[4:8]


def slots(owner):
    place = (owner % 2) * 64 + owner // 2
    return (lax.broadcasted_iota(jnp.int32, (128, 128), 0) == place).astype(BF16)


def placed(rows, owner):
    where = slots(owner)
    nt = (((1,), (1,)), ((), ()))
    return sum(lax.dot_general(part, where, nt, preferred_element_type=F32) for part in split(rows))


def solve_body(gathered, rows, owner, correction):
    tn = (((0,), (0,)), ((), ()))
    values = gathered[...]
    row = lax.broadcasted_iota(jnp.int32, (256, 256), 0)
    lane = lax.broadcasted_iota(jnp.int32, (256, 256), 1)
    side = lax.axis_index("grp") // 32
    holder = row // 8
    target = jnp.where(row % 8 < 4, holder, holder + 1 - jnp.where(holder % 8 == 7, 8 * side, 0))
    column = jnp.where(lane < 192, lane, lane - 64)
    match = (target == column % 64 // 2) & (row % 4 == column // 64)
    need = None
    for q in range(2):
        pick = (match & (column % 2 == q)).astype(BF16)
        for part in split(values[:, q * 64 : (q + 1) * 64]):
            term = lax.dot_general(part, pick, tn, preferred_element_type=F32)
            need = term if need is None else need + term
    low = lax.broadcasted_iota(jnp.int32, (64, 128), 1) < 64
    inner, outer = need[:, 0:128], need[:, 128:256]
    products = [[], []]
    for c in range(3):
        shared = rows[pl.ds(c * 3 + 1, 64, stride=9), :] * outer
        for q in range(2):
            own = rows[pl.ds(c * 3 + 2 * q, 64, stride=9), :] * inner
            products[q].append(own + jnp.where(low == (q == 0), shared, 0.0))
    products = products[0] + products[1]
    ones = jnp.ones((128, 128), BF16)
    sums = sum(dot(part, ones) for part in split(jnp.concatenate(products, axis=0)))
    lane = lax.broadcasted_iota(jnp.int32, (64, 128), 1)
    stacked = []
    for q in range(2):
        first, second, third = [sums[(q * 3 + c) * 64 : (q * 3 + c + 1) * 64] for c in range(3)]
        stacked.append(jnp.where(lane == 0, first, jnp.where(lane == 1, second, third)))
    stacked = jnp.concatenate(stacked, axis=0)[:, 0:8]
    where = slots(owner[...])
    correction[...] = sum(
        lax.dot_general(part, where, tn, preferred_element_type=F32) for part in split(stacked)
    )


def second_body(
    correction, right, state_grad, stress, direction, rhs, keep_rows, halo, weighting, along, grads,
    back_xy, back_z, back_along, rest, hat_down, hat_up, fold, spread, new, partial, message,
    own_coarse, grad, flux,
):
    keep = keep_rows[...]
    keep_right = halo[96:112, :]
    rows = jnp.concatenate(
        [
            jnp.broadcast_to(ref[c : c + 1, :], (4, 128))
            for c in range(3)
            for ref in (correction, right)
        ],
        axis=0,
    )
    row = lax.broadcasted_iota(jnp.int32, (24, 128), 0)
    lane = lax.broadcasted_iota(jnp.int32, (24, 128), 1)
    levels = dot(beside(jnp.where(lane // EZ == row % EY, rows, 0.0)), thrice(hat_up))
    levels = jnp.concatenate([levels[c * 8 : (c + 1) * 8] for c in range(3)], axis=1)
    update = dot(spread[...], under(levels))
    field = []
    fresh = []
    for c in range(3):
        piece = update[:, c * 128 : (c + 1) * 128]
        own = own_rows(direction, c) + keep * piece[:64]
        new[c] = own.reshape(4, 16, 128)
        fresh.append(own)
        field.append(
            jnp.concatenate(
                [keep * own, halo[c * 16 : 16 + c * 16, :] + keep_right * piece[64:]], axis=0
            )
        )
    gradients([field], along, grads, (grad,))
    physics(state_grad, grad, weighting, stress, flux, False)
    image = images(flux, back_xy, back_z, back_along)
    extended = []
    for c in range(3):
        part = image[c * NODES : (c + 1) * NODES]
        own = own_rows(rhs, c) - keep * part[:64] - (1.0 - keep) * fresh[c]
        last = -keep_right * part[64:]
        partial[c] = own.reshape(4, 16, 128)
        message[c * 16 : (c + 1) * 16, :] = last
        extended.append(jnp.concatenate([own, last], axis=0))
    levels = dot(beside(coarse_rows(extended, rest)), thrice(hat_down))
    message[48:72, :] = levels
    for c in range(3):
        own_coarse[c] = levels[c * 8 : c * 8 + 4, :EZ]


def finish_body(partial, arrived, own_coarse, residual, coarse):
    for c in range(3):
        residual[c, 0] = partial[c, 0] + arrived[c * 16 : (c + 1) * 16, :]
        residual[c, 1:4] = partial[c, 1:4]
        coarse[c] = own_coarse[c] + arrived[52 + c * 8 : 56 + c * 8, :EZ]


def finish(partial, arrived, own_coarse):
    vmem = pl.BlockSpec(memory_space=pltpu.VMEM)
    return pl.pallas_call(
        finish_body,
        out_shape=[
            jax.ShapeDtypeStruct((3, 4, 16, 128), F32),
            jax.ShapeDtypeStruct((3, EY, EZ), F32),
        ],
        in_specs=[vmem] * 3,
        out_specs=[vmem] * 2,
        compiler_params=pltpu.CompilerParams(vmem_limit_bytes=24 * 2**20),
    )(near(partial), near(arrived), near(own_coarse))


def shifted(block, distance):
    axes = ("grp", "mem")
    count = lax.axis_size(axes)
    route = [(i - distance, i) for i in range(count) if 0 <= i - distance < count]
    return lax.ppermute(block, axes, route)


def ring():
    groups, members = lax.axis_size("grp"), lax.axis_size("mem")
    route = []
    for g in range(groups):
        route += [(g * members + m, g * members + m + 1) for m in range(members - 1)]
        last = g >= groups // 2 - 1 and g % 8 == 7
        to = g + 8 if last else g
        if to < groups:
            route.append((g * members + members - 1, to * members))
    return route


def shards(state, direction, rhs, clamp, stiffness, coarse_owner, coarse_inverse):
    k = constants()
    names = ("along", "grads", "back_xy", "back_z", "back_along", "rest", "hat_down", "hat_up", "fold", "spread")
    kept = [state, direction, rhs] + [jnp.asarray(k[name]) for name in names] + [coarse_owner]
    inverse = coarse_inverse.reshape(384, 192)
    used = [
        clamp, coarse_owner, inverse, stiffness[0],
        jnp.asarray(k["quad_y"]), jnp.asarray(k["quad_z"]),
    ]
    message, keep_rows, rows, weighting, state, direction, rhs, *shared, owner = prepare(kept, used)
    halo = shifted(message, -1)
    rows = lax.all_to_all(
        rows.reshape(576, 1, 128), "grp", split_axis=0, concat_axis=0, tiled=True
    ).reshape(576, 128)
    big = (3 * ROWS, 3 * WIDE)
    scratch = (pltpu.VMEM(big, F32), pltpu.VMEM(big, F32))
    state_grad, stress, sums = call(
        first_body,
        [big, (6, LIVE, WIDE), (8, 128)],
        state, direction, rhs, keep_rows, halo, weighting, *shared, owner,
        scratch=scratch, cost=pl.CostEstimate(flops=20000000000, bytes_accessed=4 * 10**6, transcendentals=0),
    )
    arrived = lax.ppermute(sums, ("grp", "mem"), ring())[4:8]
    wraps = lax.axis_index("mem") == 0
    total = jnp.concatenate(
        [sums[0:4] + jnp.where(wraps, 0.0, arrived), jnp.where(wraps, arrived, 0.0)], axis=0
    )
    total = jnp.broadcast_to(total[None], (32, 8, 128)).reshape(256, 128)
    total, rows = lax.optimization_barrier((total, rows))
    sides = [list(range(32)), list(range(32, 64))]
    gathered = lax.all_to_all(
        total, "grp", split_axis=0, concat_axis=0, tiled=True, axis_index_groups=sides
    )
    (correction,) = call(solve_body, [(8, 128)], gathered, rows, owner)
    right = shifted(correction, -1)
    field = (3, 4, 16, 128)
    new, partial, last, own_coarse = call(
        second_body,
        [field, field, (72, 128), (3, EY, EZ)],
        correction, right, state_grad, stress, direction, rhs, keep_rows, halo, weighting, *shared,
        scratch=scratch,
    )
    residual, coarse = finish(partial, shifted(last, 1), own_coarse)
    return new, residual, coarse[:, None]


def solution(mesh):
    along = ("grp", "mem")
    field = P(None, along, None, None)
    in_specs = (
        field, field, field, P(along, None), P(along, None, None), P(along, None),
        P(along, None, None, None),
    )
    return jax.shard_map(
        shards, mesh=mesh, in_specs=in_specs, out_specs=(field, field, field), check_vma=False
    )
```

```python
import functools
import jax
import jax.numpy as jnp
import numpy as np
from jax import lax
from jax.experimental import pallas as pl
from jax.experimental.pallas import tpu as pltpu
from jax.sharding import PartitionSpec as P

F32 = jnp.float32
BF16 = jnp.bfloat16
HIGHEST = lax.Precision.HIGHEST
EY = 4
EZ = 32
ROWS = 112
LIVE = 104
WIDE = 256
NODES = 80


def basis_tables():
    gll = np.array([-1.0, -np.sqrt(3.0 / 7.0), 0.0, np.sqrt(3.0 / 7.0), 1.0])
    inner = np.sqrt(5.0 - 2.0 * np.sqrt(10.0 / 7.0)) / 3.0
    outer = np.sqrt(5.0 + 2.0 * np.sqrt(10.0 / 7.0)) / 3.0
    inner_weight = (322.0 + 13.0 * np.sqrt(70.0)) / 900.0
    outer_weight = (322.0 - 13.0 * np.sqrt(70.0)) / 900.0
    points = np.array([-outer, -inner, 0.0, inner, outer])
    weights = np.array([outer_weight, inner_weight, 128.0 / 225.0, inner_weight, outer_weight])
    values = np.zeros((5, 5))
    slopes = np.zeros((5, 5))
    for j in range(5):
        others = [gll[k] for k in range(5) if k != j]
        denominator = np.prod([gll[j] - o for o in others])
        for q in range(5):
            t = points[q]
            values[q, j] = np.prod([t - o for o in others]) / denominator
            total = 0.0
            for i in range(4):
                total += np.prod([t - others[k] for k in range(4) if k != i])
            slopes[q, j] = 2.0 * total / denominator
    return gll, weights, values, slopes


def banded(table, count):
    result = np.zeros((5 * count, 4 * count + 1))
    for e in range(count):
        result[5 * e : 5 * e + 5, 4 * e : 4 * e + 5] = table
    return result[:, :-1]


def restrictor(gll, count):
    result = np.zeros((count, 4 * count))
    for e in range(count):
        for j in range(4):
            result[e, 4 * e + j] += (1.0 - gll[j]) / 2.0
            if e + 1 < count:
                result[e + 1, 4 * e + j] += (1.0 + gll[j]) / 2.0
    return result


def halves(table):
    table = np.asarray(table, np.float32)
    high = table.astype(BF16)
    low = (table - high.astype(np.float32)).astype(BF16)
    return high, low


def stack_left(table):
    high, low = halves(table)
    return np.concatenate([high, high, low], axis=1)


def stack_right(table):
    return np.concatenate(halves(table), axis=0)


@functools.lru_cache(maxsize=None)
def constants():
    gll, weights, values, slopes = basis_tables()
    by, dy = banded(values, EY), banded(slopes, EY)
    bz, dz = banded(values, EZ), banded(slopes, EZ)
    along = np.zeros((4 * EZ, 2 * WIDE))
    along[:, : 5 * EZ] = bz.T
    along[:, WIDE : WIDE + 5 * EZ] = dz.T
    kinds = np.zeros((3, ROWS, NODES))
    for a, (bx, side) in enumerate(((slopes, by), (values, dy), (values, by))):
        kinds[a, :100] = np.kron(bx, side)
    low = (1.0 - gll[:4]) / 2.0
    high = (1.0 + gll[:4]) / 2.0
    hat_y, hat_z = restrictor(gll, EY), restrictor(gll, EZ)
    rest = np.zeros((16, NODES))
    rest[0:4, :64] = np.kron(low[None, :], hat_y)
    rest[4:8, :64] = np.kron(high[None, :], hat_y)
    rest[4:8, 64:] = hat_y
    fold = np.zeros((8, 24))
    for c in range(3):
        for part in range(2):
            for k in range(4):
                fold[part * 4 + c, c * 8 + part * 4 + k] = 1.0
    quad_y = np.zeros((ROWS, EY))
    for r in range(5):
        for p in range(20):
            quad_y[r * 20 + p, p // 5] = weights[r] * weights[p % 5] / 8.0
    quad_z = np.zeros((EZ, WIDE))
    for q in range(5 * EZ):
        quad_z[q // 5, q] = weights[q % 5]
    return dict(
        along=stack_right(along),
        grads=stack_left(kinds.reshape(3 * ROWS, NODES)),
        back_xy=stack_left(np.concatenate([kinds[0].T, kinds[1].T], axis=1)),
        back_z=stack_left(kinds[2].T),
        back_along=stack_right(along.T),
        rest=stack_left(rest),
        hat_down=stack_right(np.tile(hat_z.T, (1, 4))),
        hat_up=stack_right(np.tile(hat_z, (4, 1))),
        fold=np.pad(np.concatenate([fold, fold], axis=1), ((0, 8), (0, 0))).astype(BF16),
        spread=stack_left(rest[:8].T),
        quad_y=np.asarray(quad_y, np.float32),
        quad_z=np.asarray(quad_z, np.float32),
    )


def split(x):
    high = x.astype(BF16)
    return high, (x - high.astype(F32)).astype(BF16)


def dot(a, b):
    return jnp.dot(a, b, preferred_element_type=F32)


def exact(a, b):
    return jnp.dot(a, b, preferred_element_type=F32, precision=HIGHEST)


def under(x):
    high, low = split(x)
    return jnp.concatenate([high, low, high], axis=0)


def beside(x):
    high, low = split(x)
    return jnp.concatenate([high, low, high], axis=1)


def near(x):
    return pltpu.with_memory_space_constraint(x, pltpu.VMEM)


def thrice(ref):
    half = ref.shape[0] // 2
    return jnp.concatenate([ref[0:half, :], ref[0:half, :], ref[half:, :]], axis=0)


def call(body, outs, *operands, scratch=(), cost=None):
    vmem = pl.BlockSpec(memory_space=pltpu.VMEM)
    return pl.pallas_call(
        body,
        out_shape=[pltpu.VMEM(s, F32) for s in outs],
        in_specs=[vmem] * len(operands),
        out_specs=[vmem] * len(outs),
        scratch_shapes=list(scratch),
        cost_estimate=cost,
        compiler_params=pltpu.CompilerParams(vmem_limit_bytes=24 * 2**20),
    )(*[near(x) for x in operands])


def prepare_body(count, *refs):
    sources, refs = refs[:count], refs[count:]
    message, keep_rows, rows, weighting = refs[:4]
    targets, (halves_of, sorted_rows, done) = refs[4:-3], refs[-3:]
    copies = [
        pltpu.make_async_copy(source, target, done.at[i])
        for i, (source, target) in enumerate(zip(sources, targets))
    ]
    writes = [
        pltpu.make_async_copy(part(sorted_rows, b), part(rows, b), done.at[count + b])
        for b in range(2)
    ]
    urgent = (count - 4, count - 6, count - 5, 1, 0)
    for i in urgent + tuple(i for i in range(count) if i not in urgent):
        copies[i].start()
    state, direction = targets[0], targets[1]
    clamp, owner, inverse, stiffness, quad_y, quad_z = targets[-6:]
    copies[count - 4].wait()
    halves_of[0] = inverse[:, 0:128]
    halves_of[1] = jnp.concatenate([inverse[:, 128:192]] * 2, axis=1)
    low = lax.broadcasted_iota(jnp.int32, (32, 128), 1) < 64
    for b in range(2):
        for c in range(3):
            first, second = [pl.ds(b * 192 + c * 64 + q, 32, stride=2) for q in range(2)]
            values = (
                halves_of[0, first, :],
                jnp.where(low, halves_of[1, first, :], halves_of[1, second, :]),
                halves_of[0, second, :],
            )
            for i in range(3):
                sorted_rows[pl.ds(b * 288 + c * 3 + i, 32, stride=9), :] = values[i]
        writes[b].start()
    for i in (0, 1, count - 6, count - 5):
        copies[i].wait()
    eye = lax.broadcasted_iota(jnp.int32, (16, 16), 0) == lax.broadcasted_iota(
        jnp.int32, (16, 16), 1
    )
    lane = lax.broadcasted_iota(jnp.int32, (16, 128), 1)
    for x in range(4):
        row = clamp[x : x + 1, :].astype(F32)
        column = jnp.sum(jnp.where(eye, row, 0.0), axis=1, keepdims=True)
        keep = jnp.where(lane == 0, 1.0 - column, 1.0)
        keep_rows[x * 16 : (x + 1) * 16, :] = keep
        if x == 0:
            message[96:112, :] = keep
            message[112:120, :] = jnp.broadcast_to(owner[...].astype(F32), (8, 128))
            for c in range(3):
                message[c * 16 : (c + 1) * 16, :] = keep * direction[c, 0]
                message[48 + c * 16 : 48 + (c + 1) * 16, :] = state[c, 0]
    for i in range(count - 3, count):
        copies[i].wait()
    weighting[...] = exact(exact(quad_y[...], stiffness[...]), quad_z[...])
    for i in range(2, count - 6):
        copies[i].wait()
    for write in writes:
        write.wait()


def part(ref, b):
    return ref.at[b * 288 : (b + 1) * 288]


def prepare(kept, used):
    operands = list(kept) + list(used)
    far = pl.BlockSpec(memory_space=pltpu.HBM)
    vmem = pl.BlockSpec(memory_space=pltpu.VMEM)
    made = [(120, 128), (64, 128), (576, 128), (ROWS, WIDE)]
    outs = [pltpu.VMEM(s, F32) for s in made] + [pltpu.VMEM(x.shape, x.dtype) for x in kept]
    outs[2] = jax.ShapeDtypeStruct(made[2], F32)
    return pl.pallas_call(
        functools.partial(prepare_body, len(operands)),
        out_shape=outs,
        in_specs=[far] * len(operands),
        out_specs=[vmem, vmem, far] + [vmem] * (len(outs) - 3),
        scratch_shapes=[pltpu.VMEM(x.shape, x.dtype) for x in used]
        + [pltpu.VMEM((2, 384, 128), F32), pltpu.VMEM((576, 128), F32)]
        + [pltpu.SemaphoreType.DMA((len(operands) + 2,))],
        compiler_params=pltpu.CompilerParams(vmem_limit_bytes=24 * 2**20),
    )(*[pltpu.with_memory_space_constraint(x, pltpu.HBM) for x in operands])


def gradients(fields, along, grads, refs):
    lines = jnp.concatenate([f for field in fields for f in field], axis=0)
    flat = dot(beside(lines), thrice(along))
    for i, ref in enumerate(refs):
        parts = [flat[(3 * i + c) * NODES : (3 * i + c + 1) * NODES] for c in range(3)]
        plain = jnp.concatenate([p[:, :WIDE] for p in parts], axis=1)
        sloped = jnp.concatenate([p[:, WIDE:] for p in parts], axis=1)
        ref[0 : 2 * ROWS, :] = dot(grads[0 : 2 * ROWS, :], under(plain))
        ref[2 * ROWS :, :] = dot(grads[2 * ROWS :, :], under(sloped))


def physics(state_grad, grad, weighting, stress, flux, fresh):
    pairs = ((0, 0), (1, 1), (2, 2), (0, 1), (0, 2), (1, 2))
    for start in range(0, LIVE, 8):
        here = slice(start, start + 8)
        w = weighting[here, :]

        def piece(ref, c, a):
            return ref[a * ROWS + start : a * ROWS + start + 8, c * WIDE : (c + 1) * WIDE]

        deform = [
            [piece(state_grad, c, a) + (1.0 if a == c else 0.0) for a in range(3)]
            for c in range(3)
        ]
        change = [[piece(grad, c, a) for a in range(3)] for c in range(3)]
        if fresh:
            square = {
                (a, b): deform[0][a] * deform[0][b]
                + deform[1][a] * deform[1][b]
                + deform[2][a] * deform[2][b]
                for a, b in pairs
            }
            shift = 0.6 * (square[0, 0] + square[1, 1] + square[2, 2] - 3.0)
            held = {
                (a, b): w * (0.8 * (square[a, b] - 1.0) + shift) if a == b else (0.8 * w) * square[a, b]
                for a, b in pairs
            }
            for i, pair in enumerate(pairs):
                stress[i, here, :] = held[pair]
        else:
            held = {pair: stress[i, here, :] for i, pair in enumerate(pairs)}
        cross = [
            [
                deform[0][a] * change[0][b] + deform[1][a] * change[1][b] + deform[2][a] * change[2][b]
                for b in range(3)
            ]
            for a in range(3)
        ]
        trace = (1.2 * w) * (cross[0][0] + cross[1][1] + cross[2][2])
        moved = {}
        for a, b in pairs:
            if a == b:
                moved[a, b] = (1.6 * w) * cross[a][b] + trace
            else:
                moved[a, b] = (0.8 * w) * (cross[a][b] + cross[b][a])
        for a in range(3):
            for c in range(3):
                entry = None
                for b in range(3):
                    key = (min(a, b), max(a, b))
                    term = change[c][b] * held[key] + deform[c][b] * moved[key]
                    entry = term if entry is None else entry + term
                flux[a * ROWS + start : a * ROWS + start + 8, c * WIDE : (c + 1) * WIDE] = entry
    for a in range(3):
        flux[a * ROWS + LIVE : (a + 1) * ROWS, :] = jnp.zeros((ROWS - LIVE, 3 * WIDE), F32)


def images(flux, back_xy, back_z, back_along):
    side_b = dot(back_xy[...], under(flux[0 : 2 * ROWS, :]))
    side_d = dot(back_z[...], under(flux[2 * ROWS :, :]))
    lines = jnp.concatenate(
        [
            jnp.concatenate(
                [side_b[:, c * WIDE : (c + 1) * WIDE], side_d[:, c * WIDE : (c + 1) * WIDE]], axis=1
            )
            for c in range(3)
        ],
        axis=0,
    )
    return dot(beside(lines), thrice(back_along))


def coarse_rows(extended, rest):
    levels = dot(rest[...], under(jnp.concatenate(extended, axis=1)))
    return jnp.concatenate([levels[:8, c * 128 : (c + 1) * 128] for c in range(3)], axis=0)


def own_rows(ref, c):
    return ref[c].reshape(64, 128)


def first_body(
    state, direction, rhs, keep_rows, halo, weighting, along, grads, back_xy, back_z, back_along,
    rest, hat_down, hat_up, fold, spread, owner, state_grad, stress, sums, grad, flux,
):
    keep = keep_rows[...]
    fields = [
        [jnp.concatenate([own_rows(state, c), halo[48 + c * 16 : 64 + c * 16, :]], axis=0) for c in range(3)],
        [
            jnp.concatenate([keep * own_rows(direction, c), halo[c * 16 : 16 + c * 16, :]], axis=0)
            for c in range(3)
        ],
    ]
    gradients(fields, along, grads, (state_grad, grad))
    physics(state_grad, grad, weighting, stress, flux, True)
    image = images(flux, back_xy, back_z, back_along)
    keep_right = halo[96:112, :]
    extended = []
    for c in range(3):
        part = image[c * NODES : (c + 1) * NODES]
        own = own_rows(rhs, c) - keep * part[:64] - (1.0 - keep) * own_rows(direction, c)
        extended.append(jnp.concatenate([own, -keep_right * part[64:]], axis=0))
    levels = dot(beside(coarse_rows(extended, rest)), thrice(hat_down))
    row = lax.broadcasted_iota(jnp.int32, (24, 128), 0)
    lane = lax.broadcasted_iota(jnp.int32, (24, 128), 1)
    levels = jnp.where(lane // EZ == row % EY, levels, 0.0)
    levels = dot(fold[...], jnp.concatenate(split(levels), axis=0))[0:8]
    sums[0:4, :] = placed(levels, owner[...])[0:4]
    sums[4:8, :] = placed(levels, halo[112:113, :].astype(jnp.int32))[4:8]


def slots(owner):
    place = (owner % 2) * 64 + owner // 2
    return (lax.broadcasted_iota(jnp.int32, (128, 128), 0) == place).astype(BF16)


def placed(rows, owner):
    where = slots(owner)
    nt = (((1,), (1,)), ((), ()))
    return sum(lax.dot_general(part, where, nt, preferred_element_type=F32) for part in split(rows))


def solve_body(gathered, rows, owner, correction):
    tn = (((0,), (0,)), ((), ()))
    values = gathered[...]
    row = lax.broadcasted_iota(jnp.int32, (256, 256), 0)
    lane = lax.broadcasted_iota(jnp.int32, (256, 256), 1)
    side = lax.axis_index("grp") // 32
    holder = row // 8
    target = jnp.where(row % 8 < 4, holder, holder + 1 - jnp.where(holder % 8 == 7, 8 * side, 0))
    column = jnp.where(lane < 192, lane, lane - 64)
    match = (target == column % 64 // 2) & (row % 4 == column // 64)
    need = None
    for q in range(2):
        pick = (match & (column % 2 == q)).astype(BF16)
        for part in split(values[:, q * 64 : (q + 1) * 64]):
            term = lax.dot_general(part, pick, tn, preferred_element_type=F32)
            need = term if need is None else need + term
    low = lax.broadcasted_iota(jnp.int32, (64, 128), 1) < 64
    inner, outer = need[:, 0:128], need[:, 128:256]
    products = [[], []]
    for c in range(3):
        shared = rows[pl.ds(c * 3 + 1, 64, stride=9), :] * outer
        for q in range(2):
            own = rows[pl.ds(c * 3 + 2 * q, 64, stride=9), :] * inner
            products[q].append(own + jnp.where(low == (q == 0), shared, 0.0))
    products = products[0] + products[1]
    ones = jnp.ones((128, 128), BF16)
    sums = sum(dot(part, ones) for part in split(jnp.concatenate(products, axis=0)))
    lane = lax.broadcasted_iota(jnp.int32, (64, 128), 1)
    stacked = []
    for q in range(2):
        first, second, third = [sums[(q * 3 + c) * 64 : (q * 3 + c + 1) * 64] for c in range(3)]
        stacked.append(jnp.where(lane == 0, first, jnp.where(lane == 1, second, third)))
    stacked = jnp.concatenate(stacked, axis=0)[:, 0:8]
    where = slots(owner[...])
    correction[...] = sum(
        lax.dot_general(part, where, tn, preferred_element_type=F32) for part in split(stacked)
    )


def second_body(
    correction, right, state_grad, stress, direction, rhs, keep_rows, halo, weighting, along, grads,
    back_xy, back_z, back_along, rest, hat_down, hat_up, fold, spread, new, partial, message,
    own_coarse, grad, flux,
):
    keep = keep_rows[...]
    keep_right = halo[96:112, :]
    rows = jnp.concatenate(
        [
            jnp.broadcast_to(ref[c : c + 1, :], (4, 128))
            for c in range(3)
            for ref in (correction, right)
        ],
        axis=0,
    )
    row = lax.broadcasted_iota(jnp.int32, (24, 128), 0)
    lane = lax.broadcasted_iota(jnp.int32, (24, 128), 1)
    levels = dot(beside(jnp.where(lane // EZ == row % EY, rows, 0.0)), thrice(hat_up))
    levels = jnp.concatenate([levels[c * 8 : (c + 1) * 8] for c in range(3)], axis=1)
    update = dot(spread[...], under(levels))
    field = []
    fresh = []
    for c in range(3):
        piece = update[:, c * 128 : (c + 1) * 128]
        own = own_rows(direction, c) + keep * piece[:64]
        new[c] = own.reshape(4, 16, 128)
        fresh.append(own)
        field.append(
            jnp.concatenate(
                [keep * own, halo[c * 16 : 16 + c * 16, :] + keep_right * piece[64:]], axis=0
            )
        )
    gradients([field], along, grads, (grad,))
    physics(state_grad, grad, weighting, stress, flux, False)
    image = images(flux, back_xy, back_z, back_along)
    extended = []
    for c in range(3):
        part = image[c * NODES : (c + 1) * NODES]
        own = own_rows(rhs, c) - keep * part[:64] - (1.0 - keep) * fresh[c]
        last = -keep_right * part[64:]
        partial[c] = own.reshape(4, 16, 128)
        message[c * 16 : (c + 1) * 16, :] = last
        extended.append(jnp.concatenate([own, last], axis=0))
    levels = dot(beside(coarse_rows(extended, rest)), thrice(hat_down))
    message[48:72, :] = levels
    for c in range(3):
        own_coarse[c] = levels[c * 8 : c * 8 + 4, :EZ]


def finish_body(partial, arrived, own_coarse, residual, coarse):
    for c in range(3):
        residual[c, 0] = partial[c, 0] + arrived[c * 16 : (c + 1) * 16, :]
        residual[c, 1:4] = partial[c, 1:4]
        coarse[c] = own_coarse[c] + arrived[52 + c * 8 : 56 + c * 8, :EZ]


def finish(partial, arrived, own_coarse):
    vmem = pl.BlockSpec(memory_space=pltpu.VMEM)
    return pl.pallas_call(
        finish_body,
        out_shape=[
            jax.ShapeDtypeStruct((3, 4, 16, 128), F32),
            jax.ShapeDtypeStruct((3, EY, EZ), F32),
        ],
        in_specs=[vmem] * 3,
        out_specs=[vmem] * 2,
        compiler_params=pltpu.CompilerParams(vmem_limit_bytes=24 * 2**20),
    )(near(partial), near(arrived), near(own_coarse))


def shifted(block, distance):
    axes = ("grp", "mem")
    count = lax.axis_size(axes)
    route = [(i - distance, i) for i in range(count) if 0 <= i - distance < count]
    return lax.ppermute(block, axes, route)


def ring():
    groups, members = lax.axis_size("grp"), lax.axis_size("mem")
    route = []
    for g in range(groups):
        route += [(g * members + m, g * members + m + 1) for m in range(members - 1)]
        last = g >= groups // 2 - 1 and g % 8 == 7
        to = g + 8 if last else g
        if to < groups:
            route.append((g * members + members - 1, to * members))
    return route


def shards(state, direction, rhs, clamp, stiffness, coarse_owner, coarse_inverse):
    k = constants()
    names = ("along", "grads", "back_xy", "back_z", "back_along", "rest", "hat_down", "hat_up", "fold", "spread")
    kept = [state, direction, rhs] + [jnp.asarray(k[name]) for name in names] + [coarse_owner]
    inverse = coarse_inverse.reshape(384, 192)
    used = [
        clamp, coarse_owner, inverse, stiffness[0],
        jnp.asarray(k["quad_y"]), jnp.asarray(k["quad_z"]),
    ]
    message, keep_rows, rows, weighting, state, direction, rhs, *shared, owner = prepare(kept, used)
    halo = shifted(message, -1)
    rows = lax.all_to_all(
        rows.reshape(576, 1, 128), "grp", split_axis=0, concat_axis=0, tiled=True
    ).reshape(576, 128)
    big = (3 * ROWS, 3 * WIDE)
    scratch = (pltpu.VMEM(big, F32), pltpu.VMEM(big, F32))
    state_grad, stress, sums = call(
        first_body,
        [big, (6, LIVE, WIDE), (8, 128)],
        state, direction, rhs, keep_rows, halo, weighting, *shared, owner,
        scratch=scratch, cost=pl.CostEstimate(flops=20000000000, bytes_accessed=4 * 10**6, transcendentals=0),
    )
    arrived = lax.ppermute(sums, ("grp", "mem"), ring())[4:8]
    wraps = lax.axis_index("mem") == 0
    total = jnp.concatenate(
        [sums[0:4] + jnp.where(wraps, 0.0, arrived), jnp.where(wraps, arrived, 0.0)], axis=0
    )
    total = jnp.broadcast_to(total[None], (32, 8, 128)).reshape(256, 128)
    total, rows = lax.optimization_barrier((total, rows))
    sides = [list(range(32)), list(range(32, 64))]
    gathered = lax.all_to_all(
        total, "grp", split_axis=0, concat_axis=0, tiled=True, axis_index_groups=sides
    )
    (correction,) = call(solve_body, [(8, 128)], gathered, rows, owner)
    right = shifted(correction, -1)
    field = (3, 4, 16, 128)
    new, partial, last, own_coarse = call(
        second_body,
        [field, field, (72, 128), (3, EY, EZ)],
        correction, right, state_grad, stress, direction, rhs, keep_rows, halo, weighting, *shared,
        scratch=scratch,
    )
    residual, coarse = finish(partial, shifted(last, 1), own_coarse)
    return new, residual, coarse[:, None]


def solution(mesh):
    along = ("grp", "mem")
    field = P(None, along, None, None)
    in_specs = (
        field, field, field, P(along, None), P(along, None, None), P(along, None),
        P(along, None, None, None),
    )
    return jax.shard_map(
        shards, mesh=mesh, in_specs=in_specs, out_specs=(field, field, field), check_vma=False
    )
```

```python
import functools
import jax
import jax.numpy as jnp
import numpy as np
from jax import lax
from jax.experimental import pallas as pl
from jax.experimental.pallas import tpu as pltpu
from jax.sharding import PartitionSpec as P

F32 = jnp.float32
BF16 = jnp.bfloat16
HIGHEST = lax.Precision.HIGHEST
EY = 4
EZ = 32
ROWS = 112
LIVE = 104
WIDE = 256
NODES = 80


def basis_tables():
    gll = np.array([-1.0, -np.sqrt(3.0 / 7.0), 0.0, np.sqrt(3.0 / 7.0), 1.0])
    inner = np.sqrt(5.0 - 2.0 * np.sqrt(10.0 / 7.0)) / 3.0
    outer = np.sqrt(5.0 + 2.0 * np.sqrt(10.0 / 7.0)) / 3.0
    inner_weight = (322.0 + 13.0 * np.sqrt(70.0)) / 900.0
    outer_weight = (322.0 - 13.0 * np.sqrt(70.0)) / 900.0
    points = np.array([-outer, -inner, 0.0, inner, outer])
    weights = np.array([outer_weight, inner_weight, 128.0 / 225.0, inner_weight, outer_weight])
    values = np.zeros((5, 5))
    slopes = np.zeros((5, 5))
    for j in range(5):
        others = [gll[k] for k in range(5) if k != j]
        denominator = np.prod([gll[j] - o for o in others])
        for q in range(5):
            t = points[q]
            values[q, j] = np.prod([t - o for o in others]) / denominator
            total = 0.0
            for i in range(4):
                total += np.prod([t - others[k] for k in range(4) if k != i])
            slopes[q, j] = 2.0 * total / denominator
    return gll, weights, values, slopes


def banded(table, count):
    result = np.zeros((5 * count, 4 * count + 1))
    for e in range(count):
        result[5 * e : 5 * e + 5, 4 * e : 4 * e + 5] = table
    return result[:, :-1]


def restrictor(gll, count):
    result = np.zeros((count, 4 * count))
    for e in range(count):
        for j in range(4):
            result[e, 4 * e + j] += (1.0 - gll[j]) / 2.0
            if e + 1 < count:
                result[e + 1, 4 * e + j] += (1.0 + gll[j]) / 2.0
    return result


def halves(table):
    table = np.asarray(table, np.float32)
    high = table.astype(BF16)
    low = (table - high.astype(np.float32)).astype(BF16)
    return high, low


def stack_left(table):
    high, low = halves(table)
    return np.concatenate([high, high, low], axis=1)


def stack_right(table):
    return np.concatenate(halves(table), axis=0)


@functools.lru_cache(maxsize=None)
def constants():
    gll, weights, values, slopes = basis_tables()
    by, dy = banded(values, EY), banded(slopes, EY)
    bz, dz = banded(values, EZ), banded(slopes, EZ)
    along = np.zeros((4 * EZ, 2 * WIDE))
    along[:, : 5 * EZ] = bz.T
    along[:, WIDE : WIDE + 5 * EZ] = dz.T
    kinds = np.zeros((3, ROWS, NODES))
    for a, (bx, side) in enumerate(((slopes, by), (values, dy), (values, by))):
        kinds[a, :100] = np.kron(bx, side)
    low = (1.0 - gll[:4]) / 2.0
    high = (1.0 + gll[:4]) / 2.0
    hat_y, hat_z = restrictor(gll, EY), restrictor(gll, EZ)
    rest = np.zeros((16, NODES))
    rest[0:4, :64] = np.kron(low[None, :], hat_y)
    rest[4:8, :64] = np.kron(high[None, :], hat_y)
    rest[4:8, 64:] = hat_y
    fold = np.zeros((8, 24))
    for c in range(3):
        for part in range(2):
            for k in range(4):
                fold[part * 4 + c, c * 8 + part * 4 + k] = 1.0
    quad_y = np.zeros((ROWS, EY))
    for r in range(5):
        for p in range(20):
            quad_y[r * 20 + p, p // 5] = weights[r] * weights[p % 5] / 8.0
    quad_z = np.zeros((EZ, WIDE))
    for q in range(5 * EZ):
        quad_z[q // 5, q] = weights[q % 5]
    return dict(
        along=stack_right(along),
        grads=stack_left(kinds.reshape(3 * ROWS, NODES)),
        back_xy=stack_left(np.concatenate([kinds[0].T, kinds[1].T], axis=1)),
        back_z=stack_left(kinds[2].T),
        back_along=stack_right(along.T),
        rest=stack_left(rest),
        hat_down=stack_right(np.tile(hat_z.T, (1, 4))),
        hat_up=stack_right(np.tile(hat_z, (4, 1))),
        fold=np.pad(np.concatenate([fold, fold], axis=1), ((0, 8), (0, 0))).astype(BF16),
        spread=stack_left(rest[:8].T),
        quad_y=np.asarray(quad_y, np.float32),
        quad_z=np.asarray(quad_z, np.float32),
    )


def split(x):
    high = x.astype(BF16)
    return high, (x - high.astype(F32)).astype(BF16)


def dot(a, b):
    return jnp.dot(a, b, preferred_element_type=F32)


def exact(a, b):
    return jnp.dot(a, b, preferred_element_type=F32, precision=HIGHEST)


def under(x):
    high, low = split(x)
    return jnp.concatenate([high, low, high], axis=0)


def beside(x):
    high, low = split(x)
    return jnp.concatenate([high, low, high], axis=1)


def near(x):
    return pltpu.with_memory_space_constraint(x, pltpu.VMEM)


def thrice(ref):
    half = ref.shape[0] // 2
    return jnp.concatenate([ref[0:half, :], ref[0:half, :], ref[half:, :]], axis=0)


def call(body, outs, *operands, scratch=(), cost=None):
    vmem = pl.BlockSpec(memory_space=pltpu.VMEM)
    return pl.pallas_call(
        body,
        out_shape=[pltpu.VMEM(s, F32) for s in outs],
        in_specs=[vmem] * len(operands),
        out_specs=[vmem] * len(outs),
        scratch_shapes=list(scratch),
        cost_estimate=cost,
        compiler_params=pltpu.CompilerParams(vmem_limit_bytes=24 * 2**20),
    )(*[near(x) for x in operands])


def prepare_body(count, *refs):
    sources, refs = refs[:count], refs[count:]
    message, keep_rows, rows, weighting = refs[:4]
    targets, (halves_of, sorted_rows, done) = refs[4:-3], refs[-3:]
    copies = [
        pltpu.make_async_copy(source, target, done.at[i])
        for i, (source, target) in enumerate(zip(sources, targets))
    ]
    writes = [
        pltpu.make_async_copy(part(sorted_rows, b), part(rows, b), done.at[count + b])
        for b in range(2)
    ]
    urgent = (count - 4, count - 6, count - 5, 1, 0)
    for i in urgent + tuple(i for i in range(count) if i not in urgent):
        copies[i].start()
    state, direction = targets[0], targets[1]
    clamp, owner, inverse, stiffness, quad_y, quad_z = targets[-6:]
    copies[count - 4].wait()
    halves_of[0] = inverse[:, 0:128]
    halves_of[1] = jnp.concatenate([inverse[:, 128:192]] * 2, axis=1)
    low = lax.broadcasted_iota(jnp.int32, (32, 128), 1) < 64
    for b in range(2):
        for c in range(3):
            first, second = [pl.ds(b * 192 + c * 64 + q, 32, stride=2) for q in range(2)]
            values = (
                halves_of[0, first, :],
                jnp.where(low, halves_of[1, first, :], halves_of[1, second, :]),
                halves_of[0, second, :],
            )
            for i in range(3):
                sorted_rows[pl.ds(b * 288 + c * 3 + i, 32, stride=9), :] = values[i]
        writes[b].start()
    for i in (0, 1, count - 6, count - 5):
        copies[i].wait()
    eye = lax.broadcasted_iota(jnp.int32, (16, 16), 0) == lax.broadcasted_iota(
        jnp.int32, (16, 16), 1
    )
    lane = lax.broadcasted_iota(jnp.int32, (16, 128), 1)
    for x in range(4):
        row = clamp[x : x + 1, :].astype(F32)
        column = jnp.sum(jnp.where(eye, row, 0.0), axis=1, keepdims=True)
        keep = jnp.where(lane == 0, 1.0 - column, 1.0)
        keep_rows[x * 16 : (x + 1) * 16, :] = keep
        if x == 0:
            message[96:112, :] = keep
            message[112:120, :] = jnp.broadcast_to(owner[...].astype(F32), (8, 128))
            for c in range(3):
                message[c * 16 : (c + 1) * 16, :] = keep * direction[c, 0]
                message[48 + c * 16 : 48 + (c + 1) * 16, :] = state[c, 0]
    for i in range(count - 3, count):
        copies[i].wait()
    weighting[...] = exact(exact(quad_y[...], stiffness[...]), quad_z[...])
    for i in range(2, count - 6):
        copies[i].wait()
    for write in writes:
        write.wait()


def part(ref, b):
    return ref.at[b * 288 : (b + 1) * 288]


def prepare(kept, used):
    operands = list(kept) + list(used)
    far = pl.BlockSpec(memory_space=pltpu.HBM)
    vmem = pl.BlockSpec(memory_space=pltpu.VMEM)
    made = [(120, 128), (64, 128), (576, 128), (ROWS, WIDE)]
    outs = [pltpu.VMEM(s, F32) for s in made] + [pltpu.VMEM(x.shape, x.dtype) for x in kept]
    outs[2] = jax.ShapeDtypeStruct(made[2], F32)
    return pl.pallas_call(
        functools.partial(prepare_body, len(operands)),
        out_shape=outs,
        in_specs=[far] * len(operands),
        out_specs=[vmem, vmem, far] + [vmem] * (len(outs) - 3),
        scratch_shapes=[pltpu.VMEM(x.shape, x.dtype) for x in used]
        + [pltpu.VMEM((2, 384, 128), F32), pltpu.VMEM((576, 128), F32)]
        + [pltpu.SemaphoreType.DMA((len(operands) + 2,))],
        compiler_params=pltpu.CompilerParams(vmem_limit_bytes=24 * 2**20),
    )(*[pltpu.with_memory_space_constraint(x, pltpu.HBM) for x in operands])


def gradients(fields, along, grads, refs):
    lines = jnp.concatenate([f for field in fields for f in field], axis=0)
    flat = dot(beside(lines), thrice(along))
    for i, ref in enumerate(refs):
        parts = [flat[(3 * i + c) * NODES : (3 * i + c + 1) * NODES] for c in range(3)]
        plain = jnp.concatenate([p[:, :WIDE] for p in parts], axis=1)
        sloped = jnp.concatenate([p[:, WIDE:] for p in parts], axis=1)
        ref[0 : 2 * ROWS, :] = dot(grads[0 : 2 * ROWS, :], under(plain))
        ref[2 * ROWS :, :] = dot(grads[2 * ROWS :, :], under(sloped))


def physics(state_grad, grad, weighting, stress, flux, fresh):
    pairs = ((0, 0), (1, 1), (2, 2), (0, 1), (0, 2), (1, 2))
    for start in range(0, LIVE, 8):
        here = slice(start, start + 8)
        w = weighting[here, :]

        def piece(ref, c, a):
            return ref[a * ROWS + start : a * ROWS + start + 8, c * WIDE : (c + 1) * WIDE]

        deform = [
            [piece(state_grad, c, a) + (1.0 if a == c else 0.0) for a in range(3)]
            for c in range(3)
        ]
        change = [[piece(grad, c, a) for a in range(3)] for c in range(3)]
        if fresh:
            square = {
                (a, b): deform[0][a] * deform[0][b]
                + deform[1][a] * deform[1][b]
                + deform[2][a] * deform[2][b]
                for a, b in pairs
            }
            shift = 0.6 * (square[0, 0] + square[1, 1] + square[2, 2] - 3.0)
            held = {
                (a, b): w * (0.8 * (square[a, b] - 1.0) + shift) if a == b else (0.8 * w) * square[a, b]
                for a, b in pairs
            }
            for i, pair in enumerate(pairs):
                stress[i, here, :] = held[pair]
        else:
            held = {pair: stress[i, here, :] for i, pair in enumerate(pairs)}
        cross = [
            [
                deform[0][a] * change[0][b] + deform[1][a] * change[1][b] + deform[2][a] * change[2][b]
                for b in range(3)
            ]
            for a in range(3)
        ]
        trace = (1.2 * w) * (cross[0][0] + cross[1][1] + cross[2][2])
        moved = {}
        for a, b in pairs:
            if a == b:
                moved[a, b] = (1.6 * w) * cross[a][b] + trace
            else:
                moved[a, b] = (0.8 * w) * (cross[a][b] + cross[b][a])
        for a in range(3):
            for c in range(3):
                entry = None
                for b in range(3):
                    key = (min(a, b), max(a, b))
                    term = change[c][b] * held[key] + deform[c][b] * moved[key]
                    entry = term if entry is None else entry + term
                flux[a * ROWS + start : a * ROWS + start + 8, c * WIDE : (c + 1) * WIDE] = entry
    for a in range(3):
        flux[a * ROWS + LIVE : (a + 1) * ROWS, :] = jnp.zeros((ROWS - LIVE, 3 * WIDE), F32)


def images(flux, back_xy, back_z, back_along):
    side_b = dot(back_xy[...], under(flux[0 : 2 * ROWS, :]))
    side_d = dot(back_z[...], under(flux[2 * ROWS :, :]))
    lines = jnp.concatenate(
        [
            jnp.concatenate(
                [side_b[:, c * WIDE : (c + 1) * WIDE], side_d[:, c * WIDE : (c + 1) * WIDE]], axis=1
            )
            for c in range(3)
        ],
        axis=0,
    )
    return dot(beside(lines), thrice(back_along))


def coarse_rows(extended, rest):
    levels = dot(rest[...], under(jnp.concatenate(extended, axis=1)))
    return jnp.concatenate([levels[:8, c * 128 : (c + 1) * 128] for c in range(3)], axis=0)


def own_rows(ref, c):
    return ref[c].reshape(64, 128)


def first_body(
    state, direction, rhs, keep_rows, halo, weighting, along, grads, back_xy, back_z, back_along,
    rest, hat_down, hat_up, fold, spread, owner, state_grad, stress, sums, grad, flux,
):
    keep = keep_rows[...]
    fields = [
        [jnp.concatenate([own_rows(state, c), halo[48 + c * 16 : 64 + c * 16, :]], axis=0) for c in range(3)],
        [
            jnp.concatenate([keep * own_rows(direction, c), halo[c * 16 : 16 + c * 16, :]], axis=0)
            for c in range(3)
        ],
    ]
    gradients(fields, along, grads, (state_grad, grad))
    physics(state_grad, grad, weighting, stress, flux, True)
    image = images(flux, back_xy, back_z, back_along)
    keep_right = halo[96:112, :]
    extended = []
    for c in range(3):
        part = image[c * NODES : (c + 1) * NODES]
        own = own_rows(rhs, c) - keep * part[:64] - (1.0 - keep) * own_rows(direction, c)
        extended.append(jnp.concatenate([own, -keep_right * part[64:]], axis=0))
    levels = dot(beside(coarse_rows(extended, rest)), thrice(hat_down))
    row = lax.broadcasted_iota(jnp.int32, (24, 128), 0)
    lane = lax.broadcasted_iota(jnp.int32, (24, 128), 1)
    levels = jnp.where(lane // EZ == row % EY, levels, 0.0)
    levels = dot(fold[...], jnp.concatenate(split(levels), axis=0))[0:8]
    sums[0:4, :] = placed(levels, owner[...])[0:4]
    sums[4:8, :] = placed(levels, halo[112:113, :].astype(jnp.int32))[4:8]


def slots(owner):
    place = (owner % 2) * 64 + owner // 2
    return (lax.broadcasted_iota(jnp.int32, (128, 128), 0) == place).astype(BF16)


def placed(rows, owner):
    where = slots(owner)
    nt = (((1,), (1,)), ((), ()))
    return sum(lax.dot_general(part, where, nt, preferred_element_type=F32) for part in split(rows))


def solve_body(gathered, rows, owner, correction):
    tn = (((0,), (0,)), ((), ()))
    values = gathered[...]
    row = lax.broadcasted_iota(jnp.int32, (192, 256), 0)
    lane = lax.broadcasted_iota(jnp.int32, (192, 256), 1)
    side = lax.axis_index("grp") // 32
    holder = (row * 171) >> 10
    place = row - 6 * holder
    target = jnp.where(place < 3, holder, holder + 1 - jnp.where(holder % 8 == 7, 8 * side, 0))
    column = jnp.where(lane < 192, lane, lane - 64)
    part = jnp.where(place < 3, place, place - 3)
    match = (target == column % 64 // 2) & (part == column // 64)
    need = None
    for q in range(2):
        pick = (match & (column % 2 == q)).astype(BF16)
        for part in split(values[:, q * 64 : (q + 1) * 64]):
            term = lax.dot_general(part, pick, tn, preferred_element_type=F32)
            need = term if need is None else need + term
    low = lax.broadcasted_iota(jnp.int32, (64, 128), 1) < 64
    inner, outer = need[:, 0:128], need[:, 128:256]
    products = [[], []]
    for c in range(3):
        shared = rows[pl.ds(c * 3 + 1, 64, stride=9), :] * outer
        for q in range(2):
            own = rows[pl.ds(c * 3 + 2 * q, 64, stride=9), :] * inner
            products[q].append(own + jnp.where(low == (q == 0), shared, 0.0))
    products = products[0] + products[1]
    ones = jnp.ones((128, 128), BF16)
    sums = sum(dot(part, ones) for part in split(jnp.concatenate(products, axis=0)))
    lane = lax.broadcasted_iota(jnp.int32, (64, 128), 1)
    stacked = []
    for q in range(2):
        first, second, third = [sums[(q * 3 + c) * 64 : (q * 3 + c + 1) * 64] for c in range(3)]
        stacked.append(jnp.where(lane == 0, first, jnp.where(lane == 1, second, third)))
    stacked = jnp.concatenate(stacked, axis=0)[:, 0:8]
    where = slots(owner[...])
    correction[...] = sum(
        lax.dot_general(part, where, tn, preferred_element_type=F32) for part in split(stacked)
    )


def second_body(
    correction, right, state_grad, stress, direction, rhs, keep_rows, halo, weighting, along, grads,
    back_xy, back_z, back_along, rest, hat_down, hat_up, fold, spread, new, partial, message,
    own_coarse, grad, flux,
):
    keep = keep_rows[...]
    keep_right = halo[96:112, :]
    rows = jnp.concatenate(
        [
            jnp.broadcast_to(ref[c : c + 1, :], (4, 128))
            for c in range(3)
            for ref in (correction, right)
        ],
        axis=0,
    )
    row = lax.broadcasted_iota(jnp.int32, (24, 128), 0)
    lane = lax.broadcasted_iota(jnp.int32, (24, 128), 1)
    levels = dot(beside(jnp.where(lane // EZ == row % EY, rows, 0.0)), thrice(hat_up))
    levels = jnp.concatenate([levels[c * 8 : (c + 1) * 8] for c in range(3)], axis=1)
    update = dot(spread[...], under(levels))
    field = []
    fresh = []
    for c in range(3):
        piece = update[:, c * 128 : (c + 1) * 128]
        own = own_rows(direction, c) + keep * piece[:64]
        new[c] = own.reshape(4, 16, 128)
        fresh.append(own)
        field.append(
            jnp.concatenate(
                [keep * own, halo[c * 16 : 16 + c * 16, :] + keep_right * piece[64:]], axis=0
            )
        )
    gradients([field], along, grads, (grad,))
    physics(state_grad, grad, weighting, stress, flux, False)
    image = images(flux, back_xy, back_z, back_along)
    extended = []
    for c in range(3):
        part = image[c * NODES : (c + 1) * NODES]
        own = own_rows(rhs, c) - keep * part[:64] - (1.0 - keep) * fresh[c]
        last = -keep_right * part[64:]
        partial[c] = own.reshape(4, 16, 128)
        message[c * 16 : (c + 1) * 16, :] = last
        extended.append(jnp.concatenate([own, last], axis=0))
    levels = dot(beside(coarse_rows(extended, rest)), thrice(hat_down))
    message[48:72, :] = levels
    for c in range(3):
        own_coarse[c] = levels[c * 8 : c * 8 + 4, :EZ]


def finish_body(partial, arrived, own_coarse, residual, coarse):
    for c in range(3):
        residual[c, 0] = partial[c, 0] + arrived[c * 16 : (c + 1) * 16, :]
        residual[c, 1:4] = partial[c, 1:4]
        coarse[c] = own_coarse[c] + arrived[52 + c * 8 : 56 + c * 8, :EZ]


def finish(partial, arrived, own_coarse):
    vmem = pl.BlockSpec(memory_space=pltpu.VMEM)
    return pl.pallas_call(
        finish_body,
        out_shape=[
            jax.ShapeDtypeStruct((3, 4, 16, 128), F32),
            jax.ShapeDtypeStruct((3, EY, EZ), F32),
        ],
        in_specs=[vmem] * 3,
        out_specs=[vmem] * 2,
        compiler_params=pltpu.CompilerParams(vmem_limit_bytes=24 * 2**20),
    )(near(partial), near(arrived), near(own_coarse))


def shifted(block, distance):
    axes = ("grp", "mem")
    count = lax.axis_size(axes)
    route = [(i - distance, i) for i in range(count) if 0 <= i - distance < count]
    return lax.ppermute(block, axes, route)


def ring():
    groups, members = lax.axis_size("grp"), lax.axis_size("mem")
    route = []
    for g in range(groups):
        route += [(g * members + m, g * members + m + 1) for m in range(members - 1)]
        last = g >= groups // 2 - 1 and g % 8 == 7
        to = g + 8 if last else g
        if to < groups:
            route.append((g * members + members - 1, to * members))
    return route


def shards(state, direction, rhs, clamp, stiffness, coarse_owner, coarse_inverse):
    k = constants()
    names = ("along", "grads", "back_xy", "back_z", "back_along", "rest", "hat_down", "hat_up", "fold", "spread")
    kept = [state, direction, rhs] + [jnp.asarray(k[name]) for name in names] + [coarse_owner]
    inverse = coarse_inverse.reshape(384, 192)
    used = [
        clamp, coarse_owner, inverse, stiffness[0],
        jnp.asarray(k["quad_y"]), jnp.asarray(k["quad_z"]),
    ]
    message, keep_rows, rows, weighting, state, direction, rhs, *shared, owner = prepare(kept, used)
    halo = shifted(message, -1)
    rows = lax.all_to_all(
        rows.reshape(576, 1, 128), "grp", split_axis=0, concat_axis=0, tiled=True
    ).reshape(576, 128)
    big = (3 * ROWS, 3 * WIDE)
    scratch = (pltpu.VMEM(big, F32), pltpu.VMEM(big, F32))
    state_grad, stress, sums = call(
        first_body,
        [big, (6, LIVE, WIDE), (8, 128)],
        state, direction, rhs, keep_rows, halo, weighting, *shared, owner,
        scratch=scratch, cost=pl.CostEstimate(flops=20000000000, bytes_accessed=4 * 10**6, transcendentals=0),
    )
    arrived = lax.ppermute(sums, ("grp", "mem"), ring())[4:7]
    wraps = lax.axis_index("mem") == 0
    total = jnp.concatenate(
        [sums[0:3] + jnp.where(wraps, 0.0, arrived), jnp.where(wraps, arrived, 0.0)], axis=0
    )
    total = jnp.broadcast_to(total[None, :, None], (32, 6, 1, 128)).reshape(192, 1, 128)
    total, rows = lax.optimization_barrier((total, rows))
    sides = [list(range(32)), list(range(32, 64))]
    gathered = lax.all_to_all(
        total, "grp", split_axis=0, concat_axis=0, tiled=True, axis_index_groups=sides
    ).reshape(192, 128)
    (correction,) = call(solve_body, [(8, 128)], gathered, rows, owner)
    right = shifted(correction, -1)
    field = (3, 4, 16, 128)
    new, partial, last, own_coarse = call(
        second_body,
        [field, field, (72, 128), (3, EY, EZ)],
        correction, right, state_grad, stress, direction, rhs, keep_rows, halo, weighting, *shared,
        scratch=scratch,
    )
    residual, coarse = finish(partial, shifted(last, 1), own_coarse)
    return new, residual, coarse[:, None]


def solution(mesh):
    along = ("grp", "mem")
    field = P(None, along, None, None)
    in_specs = (
        field, field, field, P(along, None), P(along, None, None), P(along, None),
        P(along, None, None, None),
    )
    return jax.shard_map(
        shards, mesh=mesh, in_specs=in_specs, out_specs=(field, field, field), check_vma=False
    )
```

```python
import functools
import jax
import jax.numpy as jnp
import numpy as np
from jax import lax
from jax.experimental import pallas as pl
from jax.experimental.pallas import tpu as pltpu
from jax.sharding import PartitionSpec as P

F32 = jnp.float32
BF16 = jnp.bfloat16
HIGHEST = lax.Precision.HIGHEST
EY = 4
EZ = 32
ROWS = 112
LIVE = 104
WIDE = 256
NODES = 80


def basis_tables():
    gll = np.array([-1.0, -np.sqrt(3.0 / 7.0), 0.0, np.sqrt(3.0 / 7.0), 1.0])
    inner = np.sqrt(5.0 - 2.0 * np.sqrt(10.0 / 7.0)) / 3.0
    outer = np.sqrt(5.0 + 2.0 * np.sqrt(10.0 / 7.0)) / 3.0
    inner_weight = (322.0 + 13.0 * np.sqrt(70.0)) / 900.0
    outer_weight = (322.0 - 13.0 * np.sqrt(70.0)) / 900.0
    points = np.array([-outer, -inner, 0.0, inner, outer])
    weights = np.array([outer_weight, inner_weight, 128.0 / 225.0, inner_weight, outer_weight])
    values = np.zeros((5, 5))
    slopes = np.zeros((5, 5))
    for j in range(5):
        others = [gll[k] for k in range(5) if k != j]
        denominator = np.prod([gll[j] - o for o in others])
        for q in range(5):
            t = points[q]
            values[q, j] = np.prod([t - o for o in others]) / denominator
            total = 0.0
            for i in range(4):
                total += np.prod([t - others[k] for k in range(4) if k != i])
            slopes[q, j] = 2.0 * total / denominator
    return gll, weights, values, slopes


def banded(table, count):
    result = np.zeros((5 * count, 4 * count + 1))
    for e in range(count):
        result[5 * e : 5 * e + 5, 4 * e : 4 * e + 5] = table
    return result[:, :-1]


def restrictor(gll, count):
    result = np.zeros((count, 4 * count))
    for e in range(count):
        for j in range(4):
            result[e, 4 * e + j] += (1.0 - gll[j]) / 2.0
            if e + 1 < count:
                result[e + 1, 4 * e + j] += (1.0 + gll[j]) / 2.0
    return result


def halves(table):
    table = np.asarray(table, np.float32)
    high = table.astype(BF16)
    low = (table - high.astype(np.float32)).astype(BF16)
    return high, low


def stack_left(table):
    high, low = halves(table)
    return np.concatenate([high, high, low], axis=1)


def stack_right(table):
    return np.concatenate(halves(table), axis=0)


@functools.lru_cache(maxsize=None)
def constants():
    gll, weights, values, slopes = basis_tables()
    by, dy = banded(values, EY), banded(slopes, EY)
    bz, dz = banded(values, EZ), banded(slopes, EZ)
    along = np.zeros((4 * EZ, 2 * WIDE))
    along[:, : 5 * EZ] = bz.T
    along[:, WIDE : WIDE + 5 * EZ] = dz.T
    kinds = np.zeros((3, ROWS, NODES))
    for a, (bx, side) in enumerate(((slopes, by), (values, dy), (values, by))):
        kinds[a, :100] = np.kron(bx, side)
    low = (1.0 - gll[:4]) / 2.0
    high = (1.0 + gll[:4]) / 2.0
    hat_y, hat_z = restrictor(gll, EY), restrictor(gll, EZ)
    rest = np.zeros((16, NODES))
    rest[0:4, :64] = np.kron(low[None, :], hat_y)
    rest[4:8, :64] = np.kron(high[None, :], hat_y)
    rest[4:8, 64:] = hat_y
    fold = np.zeros((8, 24))
    for c in range(3):
        for part in range(2):
            for k in range(4):
                fold[part * 4 + c, c * 8 + part * 4 + k] = 1.0
    quad_y = np.zeros((ROWS, EY))
    for r in range(5):
        for p in range(20):
            quad_y[r * 20 + p, p // 5] = weights[r] * weights[p % 5] / 8.0
    quad_z = np.zeros((EZ, WIDE))
    for q in range(5 * EZ):
        quad_z[q // 5, q] = weights[q % 5]
    return dict(
        along=stack_right(along),
        grads=stack_left(kinds.reshape(3 * ROWS, NODES)),
        back_xy=stack_left(np.concatenate([kinds[0].T, kinds[1].T], axis=1)),
        back_z=stack_left(kinds[2].T),
        back_along=stack_right(along.T),
        rest=stack_left(rest),
        hat_down=stack_right(np.tile(hat_z.T, (1, 4))),
        hat_up=stack_right(np.tile(hat_z, (4, 1))),
        fold=np.pad(np.concatenate([fold, fold], axis=1), ((0, 8), (0, 0))).astype(BF16),
        spread=stack_left(rest[:8].T),
        quad_y=np.asarray(quad_y, np.float32),
        quad_z=np.asarray(quad_z, np.float32),
    )


def split(x):
    high = x.astype(BF16)
    return high, (x - high.astype(F32)).astype(BF16)


def dot(a, b):
    return jnp.dot(a, b, preferred_element_type=F32)


def exact(a, b):
    return jnp.dot(a, b, preferred_element_type=F32, precision=HIGHEST)


def under(x):
    high, low = split(x)
    return jnp.concatenate([high, low, high], axis=0)


def beside(x):
    high, low = split(x)
    return jnp.concatenate([high, low, high], axis=1)


def near(x):
    return pltpu.with_memory_space_constraint(x, pltpu.VMEM)


def thrice(ref):
    half = ref.shape[0] // 2
    return jnp.concatenate([ref[0:half, :], ref[0:half, :], ref[half:, :]], axis=0)


def call(body, outs, *operands, scratch=(), cost=None):
    vmem = pl.BlockSpec(memory_space=pltpu.VMEM)
    return pl.pallas_call(
        body,
        out_shape=[pltpu.VMEM(s, F32) for s in outs],
        in_specs=[vmem] * len(operands),
        out_specs=[vmem] * len(outs),
        scratch_shapes=list(scratch),
        cost_estimate=cost,
        compiler_params=pltpu.CompilerParams(vmem_limit_bytes=24 * 2**20),
    )(*[near(x) for x in operands])


def prepare_body(count, *refs):
    sources, refs = refs[:count], refs[count:]
    message, keep_rows, rows, weighting = refs[:4]
    targets, (halves_of, sorted_rows, done) = refs[4:-3], refs[-3:]
    copies = [
        pltpu.make_async_copy(source, target, done.at[i])
        for i, (source, target) in enumerate(zip(sources, targets))
    ]
    writes = [
        pltpu.make_async_copy(part(sorted_rows, b), part(rows, b), done.at[count + b])
        for b in range(2)
    ]
    urgent = (count - 4, count - 6, count - 5, 1, 0)
    for i in urgent + tuple(i for i in range(count) if i not in urgent):
        copies[i].start()
    state, direction = targets[0], targets[1]
    clamp, owner, inverse, stiffness, quad_y, quad_z = targets[-6:]
    copies[count - 4].wait()
    halves_of[0] = inverse[:, 0:128]
    halves_of[1] = jnp.concatenate([inverse[:, 128:192]] * 2, axis=1)
    low = lax.broadcasted_iota(jnp.int32, (32, 128), 1) < 64
    for b in range(2):
        for c in range(3):
            first, second = [pl.ds(b * 192 + c * 64 + q, 32, stride=2) for q in range(2)]
            values = (
                halves_of[0, first, :],
                jnp.where(low, halves_of[1, first, :], halves_of[1, second, :]),
                halves_of[0, second, :],
            )
            for i in range(3):
                sorted_rows[pl.ds(b * 288 + c * 3 + i, 32, stride=9), :] = values[i]
        writes[b].start()
    for i in (0, 1, count - 6, count - 5):
        copies[i].wait()
    eye = lax.broadcasted_iota(jnp.int32, (16, 16), 0) == lax.broadcasted_iota(
        jnp.int32, (16, 16), 1
    )
    lane = lax.broadcasted_iota(jnp.int32, (16, 128), 1)
    for x in range(4):
        row = clamp[x : x + 1, :].astype(F32)
        column = jnp.sum(jnp.where(eye, row, 0.0), axis=1, keepdims=True)
        keep = jnp.where(lane == 0, 1.0 - column, 1.0)
        keep_rows[x * 16 : (x + 1) * 16, :] = keep
        if x == 0:
            message[96:112, :] = keep
            message[112:120, :] = jnp.broadcast_to(owner[...].astype(F32), (8, 128))
            for c in range(3):
                message[c * 16 : (c + 1) * 16, :] = keep * direction[c, 0]
                message[48 + c * 16 : 48 + (c + 1) * 16, :] = state[c, 0]
    for i in range(count - 3, count):
        copies[i].wait()
    weighting[...] = exact(exact(quad_y[...], stiffness[...]), quad_z[...])
    for i in range(2, count - 6):
        copies[i].wait()
    for write in writes:
        write.wait()


def part(ref, b):
    return ref.at[b * 288 : (b + 1) * 288]


def prepare(kept, used):
    operands = list(kept) + list(used)
    far = pl.BlockSpec(memory_space=pltpu.HBM)
    vmem = pl.BlockSpec(memory_space=pltpu.VMEM)
    made = [(120, 128), (64, 128), (576, 128), (ROWS, WIDE)]
    outs = [pltpu.VMEM(s, F32) for s in made] + [pltpu.VMEM(x.shape, x.dtype) for x in kept]
    outs[2] = jax.ShapeDtypeStruct(made[2], F32)
    return pl.pallas_call(
        functools.partial(prepare_body, len(operands)),
        out_shape=outs,
        in_specs=[far] * len(operands),
        out_specs=[vmem, vmem, far] + [vmem] * (len(outs) - 3),
        scratch_shapes=[pltpu.VMEM(x.shape, x.dtype) for x in used]
        + [pltpu.VMEM((2, 384, 128), F32), pltpu.VMEM((576, 128), F32)]
        + [pltpu.SemaphoreType.DMA((len(operands) + 2,))],
        compiler_params=pltpu.CompilerParams(vmem_limit_bytes=24 * 2**20),
    )(*[pltpu.with_memory_space_constraint(x, pltpu.HBM) for x in operands])


def gradients(fields, along, grads, refs):
    lines = jnp.concatenate([f for field in fields for f in field], axis=0)
    flat = dot(beside(lines), thrice(along))
    for i, ref in enumerate(refs):
        parts = [flat[(3 * i + c) * NODES : (3 * i + c + 1) * NODES] for c in range(3)]
        plain = jnp.concatenate([p[:, :WIDE] for p in parts], axis=1)
        sloped = jnp.concatenate([p[:, WIDE:] for p in parts], axis=1)
        ref[0 : 2 * ROWS, :] = dot(grads[0 : 2 * ROWS, :], under(plain))
        ref[2 * ROWS :, :] = dot(grads[2 * ROWS :, :], under(sloped))


def physics(state_grad, grad, weighting, stress, flux, fresh):
    pairs = ((0, 0), (1, 1), (2, 2), (0, 1), (0, 2), (1, 2))
    for start in range(0, LIVE, 8):
        here = slice(start, start + 8)
        w = weighting[here, :]

        def piece(ref, c, a):
            return ref[a * ROWS + start : a * ROWS + start + 8, c * WIDE : (c + 1) * WIDE]

        deform = [
            [piece(state_grad, c, a) + (1.0 if a == c else 0.0) for a in range(3)]
            for c in range(3)
        ]
        change = [[piece(grad, c, a) for a in range(3)] for c in range(3)]
        if fresh:
            square = {
                (a, b): deform[0][a] * deform[0][b]
                + deform[1][a] * deform[1][b]
                + deform[2][a] * deform[2][b]
                for a, b in pairs
            }
            shift = 0.6 * (square[0, 0] + square[1, 1] + square[2, 2] - 3.0)
            held = {
                (a, b): w * (0.8 * (square[a, b] - 1.0) + shift) if a == b else (0.8 * w) * square[a, b]
                for a, b in pairs
            }
            for i, pair in enumerate(pairs):
                stress[i, here, :] = held[pair]
        else:
            held = {pair: stress[i, here, :] for i, pair in enumerate(pairs)}
        cross = [
            [
                deform[0][a] * change[0][b] + deform[1][a] * change[1][b] + deform[2][a] * change[2][b]
                for b in range(3)
            ]
            for a in range(3)
        ]
        trace = (1.2 * w) * (cross[0][0] + cross[1][1] + cross[2][2])
        moved = {}
        for a, b in pairs:
            if a == b:
                moved[a, b] = (1.6 * w) * cross[a][b] + trace
            else:
                moved[a, b] = (0.8 * w) * (cross[a][b] + cross[b][a])
        for a in range(3):
            for c in range(3):
                entry = None
                for b in range(3):
                    key = (min(a, b), max(a, b))
                    term = change[c][b] * held[key] + deform[c][b] * moved[key]
                    entry = term if entry is None else entry + term
                flux[a * ROWS + start : a * ROWS + start + 8, c * WIDE : (c + 1) * WIDE] = entry
    for a in range(3):
        flux[a * ROWS + LIVE : (a + 1) * ROWS, :] = jnp.zeros((ROWS - LIVE, 3 * WIDE), F32)


def images(flux, back_xy, back_z, back_along):
    side_b = dot(back_xy[...], under(flux[0 : 2 * ROWS, :]))
    side_d = dot(back_z[...], under(flux[2 * ROWS :, :]))
    lines = jnp.concatenate(
        [
            jnp.concatenate(
                [side_b[:, c * WIDE : (c + 1) * WIDE], side_d[:, c * WIDE : (c + 1) * WIDE]], axis=1
            )
            for c in range(3)
        ],
        axis=0,
    )
    return dot(beside(lines), thrice(back_along))


def coarse_rows(extended, rest):
    levels = dot(rest[...], under(jnp.concatenate(extended, axis=1)))
    return jnp.concatenate([levels[:8, c * 128 : (c + 1) * 128] for c in range(3)], axis=0)


def own_rows(ref, c):
    return ref[c].reshape(64, 128)


def first_body(
    state, direction, rhs, keep_rows, halo, weighting, along, grads, back_xy, back_z, back_along,
    rest, hat_down, hat_up, fold, spread, owner, state_grad, stress, sums, grad, flux,
):
    keep = keep_rows[...]
    fields = [
        [jnp.concatenate([own_rows(state, c), halo[48 + c * 16 : 64 + c * 16, :]], axis=0) for c in range(3)],
        [
            jnp.concatenate([keep * own_rows(direction, c), halo[c * 16 : 16 + c * 16, :]], axis=0)
            for c in range(3)
        ],
    ]
    gradients(fields, along, grads, (state_grad, grad))
    physics(state_grad, grad, weighting, stress, flux, True)
    image = images(flux, back_xy, back_z, back_along)
    keep_right = halo[96:112, :]
    extended = []
    for c in range(3):
        part = image[c * NODES : (c + 1) * NODES]
        own = own_rows(rhs, c) - keep * part[:64] - (1.0 - keep) * own_rows(direction, c)
        extended.append(jnp.concatenate([own, -keep_right * part[64:]], axis=0))
    levels = dot(beside(coarse_rows(extended, rest)), thrice(hat_down))
    row = lax.broadcasted_iota(jnp.int32, (24, 128), 0)
    lane = lax.broadcasted_iota(jnp.int32, (24, 128), 1)
    levels = jnp.where(lane // EZ == row % EY, levels, 0.0)
    levels = dot(fold[...], jnp.concatenate(split(levels), axis=0))[0:8]
    sums[0:4, :] = placed(levels, owner[...])[0:4]
    sums[4:8, :] = placed(levels, halo[112:113, :].astype(jnp.int32))[4:8]


def slots(owner):
    place = (owner % 2) * 64 + owner // 2
    return (lax.broadcasted_iota(jnp.int32, (128, 128), 0) == place).astype(BF16)


def placed(rows, owner):
    where = slots(owner)
    nt = (((1,), (1,)), ((), ()))
    return sum(lax.dot_general(part, where, nt, preferred_element_type=F32) for part in split(rows))


def solve_body(gathered, rows, owner, correction):
    tn = (((0,), (0,)), ((), ()))
    values = gathered[...]
    row = lax.broadcasted_iota(jnp.int32, (128, 256), 0)
    lane = lax.broadcasted_iota(jnp.int32, (128, 256), 1)
    column = jnp.where(lane < 192, lane, lane - 64)
    match = (row // 4 == column % 64 // 2) & (row % 4 == column // 64)
    need = None
    for q in range(2):
        pick = (match & (column % 2 == q)).astype(BF16)
        for part in split(values[:, q * 64 : (q + 1) * 64]):
            term = lax.dot_general(part, pick, tn, preferred_element_type=F32)
            need = term if need is None else need + term
    low = lax.broadcasted_iota(jnp.int32, (64, 128), 1) < 64
    inner, outer = need[:, 0:128], need[:, 128:256]
    products = [[], []]
    for c in range(3):
        shared = rows[pl.ds(c * 3 + 1, 64, stride=9), :] * outer
        for q in range(2):
            own = rows[pl.ds(c * 3 + 2 * q, 64, stride=9), :] * inner
            products[q].append(own + jnp.where(low == (q == 0), shared, 0.0))
    products = products[0] + products[1]
    ones = jnp.ones((128, 128), BF16)
    sums = sum(dot(part, ones) for part in split(jnp.concatenate(products, axis=0)))
    lane = lax.broadcasted_iota(jnp.int32, (64, 128), 1)
    stacked = []
    for q in range(2):
        first, second, third = [sums[(q * 3 + c) * 64 : (q * 3 + c + 1) * 64] for c in range(3)]
        stacked.append(jnp.where(lane == 0, first, jnp.where(lane == 1, second, third)))
    stacked = jnp.concatenate(stacked, axis=0)[:, 0:8]
    where = slots(owner[...])
    correction[...] = sum(
        lax.dot_general(part, where, tn, preferred_element_type=F32) for part in split(stacked)
    )


def second_body(
    correction, right, state_grad, stress, direction, rhs, keep_rows, halo, weighting, along, grads,
    back_xy, back_z, back_along, rest, hat_down, hat_up, fold, spread, new, partial, message,
    own_coarse, grad, flux,
):
    keep = keep_rows[...]
    keep_right = halo[96:112, :]
    rows = jnp.concatenate(
        [
            jnp.broadcast_to(ref[c : c + 1, :], (4, 128))
            for c in range(3)
            for ref in (correction, right)
        ],
        axis=0,
    )
    row = lax.broadcasted_iota(jnp.int32, (24, 128), 0)
    lane = lax.broadcasted_iota(jnp.int32, (24, 128), 1)
    levels = dot(beside(jnp.where(lane // EZ == row % EY, rows, 0.0)), thrice(hat_up))
    levels = jnp.concatenate([levels[c * 8 : (c + 1) * 8] for c in range(3)], axis=1)
    update = dot(spread[...], under(levels))
    field = []
    fresh = []
    for c in range(3):
        piece = update[:, c * 128 : (c + 1) * 128]
        own = own_rows(direction, c) + keep * piece[:64]
        new[c] = own.reshape(4, 16, 128)
        fresh.append(own)
        field.append(
            jnp.concatenate(
                [keep * own, halo[c * 16 : 16 + c * 16, :] + keep_right * piece[64:]], axis=0
            )
        )
    gradients([field], along, grads, (grad,))
    physics(state_grad, grad, weighting, stress, flux, False)
    image = images(flux, back_xy, back_z, back_along)
    extended = []
    for c in range(3):
        part = image[c * NODES : (c + 1) * NODES]
        own = own_rows(rhs, c) - keep * part[:64] - (1.0 - keep) * fresh[c]
        last = -keep_right * part[64:]
        partial[c] = own.reshape(4, 16, 128)
        message[c * 16 : (c + 1) * 16, :] = last
        extended.append(jnp.concatenate([own, last], axis=0))
    levels = dot(beside(coarse_rows(extended, rest)), thrice(hat_down))
    message[48:72, :] = levels
    for c in range(3):
        own_coarse[c] = levels[c * 8 : c * 8 + 4, :EZ]


def finish_body(partial, arrived, own_coarse, residual, coarse):
    for c in range(3):
        residual[c, 0] = partial[c, 0] + arrived[c * 16 : (c + 1) * 16, :]
        residual[c, 1:4] = partial[c, 1:4]
        coarse[c] = own_coarse[c] + arrived[52 + c * 8 : 56 + c * 8, :EZ]


def finish(partial, arrived, own_coarse):
    vmem = pl.BlockSpec(memory_space=pltpu.VMEM)
    return pl.pallas_call(
        finish_body,
        out_shape=[
            jax.ShapeDtypeStruct((3, 4, 16, 128), F32),
            jax.ShapeDtypeStruct((3, EY, EZ), F32),
        ],
        in_specs=[vmem] * 3,
        out_specs=[vmem] * 2,
        compiler_params=pltpu.CompilerParams(vmem_limit_bytes=24 * 2**20),
    )(near(partial), near(arrived), near(own_coarse))


def shifted(block, distance):
    axes = ("grp", "mem")
    count = lax.axis_size(axes)
    route = [(i - distance, i) for i in range(count) if 0 <= i - distance < count]
    return lax.ppermute(block, axes, route)


def shards(state, direction, rhs, clamp, stiffness, coarse_owner, coarse_inverse):
    k = constants()
    names = ("along", "grads", "back_xy", "back_z", "back_along", "rest", "hat_down", "hat_up", "fold", "spread")
    kept = [state, direction, rhs] + [jnp.asarray(k[name]) for name in names] + [coarse_owner]
    inverse = coarse_inverse.reshape(384, 192)
    used = [
        clamp, coarse_owner, inverse, stiffness[0],
        jnp.asarray(k["quad_y"]), jnp.asarray(k["quad_z"]),
    ]
    message, keep_rows, rows, weighting, state, direction, rhs, *shared, owner = prepare(kept, used)
    halo = shifted(message, -1)
    rows = lax.all_to_all(
        rows.reshape(576, 1, 128), "grp", split_axis=0, concat_axis=0, tiled=True
    ).reshape(576, 128)
    big = (3 * ROWS, 3 * WIDE)
    scratch = (pltpu.VMEM(big, F32), pltpu.VMEM(big, F32))
    state_grad, stress, sums = call(
        first_body,
        [big, (6, LIVE, WIDE), (8, 128)],
        state, direction, rhs, keep_rows, halo, weighting, *shared, owner,
        scratch=scratch, cost=pl.CostEstimate(flops=20000000000, bytes_accessed=4 * 10**6, transcendentals=0),
    )
    total = sums[0:4] + shifted(sums, 1)[4:8]
    total = jnp.broadcast_to(total[None], (32, 4, 128)).reshape(128, 128)
    total, rows = lax.optimization_barrier((total, rows))
    sides = [list(range(32)), list(range(32, 64))]
    gathered = lax.all_to_all(
        total, "grp", split_axis=0, concat_axis=0, tiled=True, axis_index_groups=sides
    )
    (correction,) = call(solve_body, [(8, 128)], gathered, rows, owner)
    right = shifted(correction, -1)
    field = (3, 4, 16, 128)
    new, partial, last, own_coarse = call(
        second_body,
        [field, field, (72, 128), (3, EY, EZ)],
        correction, right, state_grad, stress, direction, rhs, keep_rows, halo, weighting, *shared,
        scratch=scratch,
    )
    residual, coarse = finish(partial, shifted(last, 1), own_coarse)
    return new, residual, coarse[:, None]


def solution(mesh):
    along = ("grp", "mem")
    field = P(None, along, None, None)
    in_specs = (
        field, field, field, P(along, None), P(along, None, None), P(along, None),
        P(along, None, None, None),
    )
    return jax.shard_map(
        shards, mesh=mesh, in_specs=in_specs, out_specs=(field, field, field), check_vma=False
    )
```

```python
import functools
import jax
import jax.numpy as jnp
import numpy as np
from jax import lax
from jax.experimental import pallas as pl
from jax.experimental.pallas import tpu as pltpu
from jax.sharding import PartitionSpec as P

F32 = jnp.float32
BF16 = jnp.bfloat16
HIGHEST = lax.Precision.HIGHEST
EY = 4
EZ = 32
ROWS = 112
LIVE = 104
WIDE = 256
NODES = 80


def basis_tables():
    gll = np.array([-1.0, -np.sqrt(3.0 / 7.0), 0.0, np.sqrt(3.0 / 7.0), 1.0])
    inner = np.sqrt(5.0 - 2.0 * np.sqrt(10.0 / 7.0)) / 3.0
    outer = np.sqrt(5.0 + 2.0 * np.sqrt(10.0 / 7.0)) / 3.0
    inner_weight = (322.0 + 13.0 * np.sqrt(70.0)) / 900.0
    outer_weight = (322.0 - 13.0 * np.sqrt(70.0)) / 900.0
    points = np.array([-outer, -inner, 0.0, inner, outer])
    weights = np.array([outer_weight, inner_weight, 128.0 / 225.0, inner_weight, outer_weight])
    values = np.zeros((5, 5))
    slopes = np.zeros((5, 5))
    for j in range(5):
        others = [gll[k] for k in range(5) if k != j]
        denominator = np.prod([gll[j] - o for o in others])
        for q in range(5):
            t = points[q]
            values[q, j] = np.prod([t - o for o in others]) / denominator
            total = 0.0
            for i in range(4):
                total += np.prod([t - others[k] for k in range(4) if k != i])
            slopes[q, j] = 2.0 * total / denominator
    return gll, weights, values, slopes


def banded(table, count):
    result = np.zeros((5 * count, 4 * count + 1))
    for e in range(count):
        result[5 * e : 5 * e + 5, 4 * e : 4 * e + 5] = table
    return result[:, :-1]


def restrictor(gll, count):
    result = np.zeros((count, 4 * count))
    for e in range(count):
        for j in range(4):
            result[e, 4 * e + j] += (1.0 - gll[j]) / 2.0
            if e + 1 < count:
                result[e + 1, 4 * e + j] += (1.0 + gll[j]) / 2.0
    return result


def halves(table):
    table = np.asarray(table, np.float32)
    high = table.astype(BF16)
    low = (table - high.astype(np.float32)).astype(BF16)
    return high, low


def stack_left(table):
    high, low = halves(table)
    return np.concatenate([high, high, low], axis=1)


def stack_right(table):
    return np.concatenate(halves(table), axis=0)


@functools.lru_cache(maxsize=None)
def constants():
    gll, weights, values, slopes = basis_tables()
    by, dy = banded(values, EY), banded(slopes, EY)
    bz, dz = banded(values, EZ), banded(slopes, EZ)
    along = np.zeros((4 * EZ, 2 * WIDE))
    along[:, : 5 * EZ] = bz.T
    along[:, WIDE : WIDE + 5 * EZ] = dz.T
    kinds = np.zeros((3, ROWS, NODES))
    for a, (bx, side) in enumerate(((slopes, by), (values, dy), (values, by))):
        kinds[a, :100] = np.kron(bx, side)
    low = (1.0 - gll[:4]) / 2.0
    high = (1.0 + gll[:4]) / 2.0
    hat_y, hat_z = restrictor(gll, EY), restrictor(gll, EZ)
    rest = np.zeros((16, NODES))
    rest[0:4, :64] = np.kron(low[None, :], hat_y)
    rest[4:8, :64] = np.kron(high[None, :], hat_y)
    rest[4:8, 64:] = hat_y
    fold = np.zeros((8, 24))
    for c in range(3):
        for part in range(2):
            for k in range(4):
                fold[part * 4 + c, c * 8 + part * 4 + k] = 1.0
    quad_y = np.zeros((ROWS, EY))
    for r in range(5):
        for p in range(20):
            quad_y[r * 20 + p, p // 5] = weights[r] * weights[p % 5] / 8.0
    quad_z = np.zeros((EZ, WIDE))
    for q in range(5 * EZ):
        quad_z[q // 5, q] = weights[q % 5]
    return dict(
        along=stack_right(along),
        grads=stack_left(kinds.reshape(3 * ROWS, NODES)),
        back_xy=stack_left(np.concatenate([kinds[0].T, kinds[1].T], axis=1)),
        back_z=stack_left(kinds[2].T),
        back_along=stack_right(along.T),
        rest=stack_left(rest),
        hat_down=stack_right(np.tile(hat_z.T, (1, 4))),
        hat_up=stack_right(np.tile(hat_z, (4, 1))),
        fold=np.pad(np.concatenate([fold, fold], axis=1), ((0, 8), (0, 0))).astype(BF16),
        spread=stack_left(rest[:8].T),
        quad_y=np.asarray(quad_y, np.float32),
        quad_z=np.asarray(quad_z, np.float32),
    )


def split(x):
    high = x.astype(BF16)
    return high, (x - high.astype(F32)).astype(BF16)


def dot(a, b):
    return jnp.dot(a, b, preferred_element_type=F32)


def exact(a, b):
    return jnp.dot(a, b, preferred_element_type=F32, precision=HIGHEST)


def under(x):
    high, low = split(x)
    return jnp.concatenate([high, low, high], axis=0)


def beside(x):
    high, low = split(x)
    return jnp.concatenate([high, low, high], axis=1)


def near(x):
    return pltpu.with_memory_space_constraint(x, pltpu.VMEM)


def thrice(ref):
    half = ref.shape[0] // 2
    return jnp.concatenate([ref[0:half, :], ref[0:half, :], ref[half:, :]], axis=0)


def call(body, outs, *operands, scratch=(), cost=None):
    vmem = pl.BlockSpec(memory_space=pltpu.VMEM)
    return pl.pallas_call(
        body,
        out_shape=[pltpu.VMEM(s, F32) for s in outs],
        in_specs=[vmem] * len(operands),
        out_specs=[vmem] * len(outs),
        scratch_shapes=list(scratch),
        cost_estimate=cost,
        compiler_params=pltpu.CompilerParams(vmem_limit_bytes=24 * 2**20),
    )(*[near(x) for x in operands])


def prepare_body(count, *refs):
    sources, refs = refs[:count], refs[count:]
    message, keep_rows, rows, weighting = refs[:4]
    targets, (halves_of, sorted_rows, done) = refs[4:-3], refs[-3:]
    copies = [
        pltpu.make_async_copy(source, target, done.at[i])
        for i, (source, target) in enumerate(zip(sources, targets))
    ]
    writes = [
        pltpu.make_async_copy(part(sorted_rows, b), part(rows, b), done.at[count + b])
        for b in range(2)
    ]
    urgent = (count - 4, count - 6, count - 5, 1, 0)
    for i in urgent + tuple(i for i in range(count) if i not in urgent):
        copies[i].start()
    state, direction = targets[0], targets[1]
    clamp, owner, inverse, stiffness, quad_y, quad_z = targets[-6:]
    copies[count - 4].wait()
    halves_of[0] = inverse[:, 0:128]
    halves_of[1] = jnp.concatenate([inverse[:, 128:192]] * 2, axis=1)
    low = lax.broadcasted_iota(jnp.int32, (32, 128), 1) < 64
    for b in range(2):
        for c in range(3):
            first, second = [pl.ds(b * 192 + c * 64 + q, 32, stride=2) for q in range(2)]
            values = (
                halves_of[0, first, :],
                jnp.where(low, halves_of[1, first, :], halves_of[1, second, :]),
                halves_of[0, second, :],
            )
            for i in range(3):
                sorted_rows[pl.ds(b * 288 + c * 3 + i, 32, stride=9), :] = values[i]
        writes[b].start()
    for i in (0, 1, count - 6, count - 5):
        copies[i].wait()
    eye = lax.broadcasted_iota(jnp.int32, (16, 16), 0) == lax.broadcasted_iota(
        jnp.int32, (16, 16), 1
    )
    lane = lax.broadcasted_iota(jnp.int32, (16, 128), 1)
    for x in range(4):
        row = clamp[x : x + 1, :].astype(F32)
        column = jnp.sum(jnp.where(eye, row, 0.0), axis=1, keepdims=True)
        keep = jnp.where(lane == 0, 1.0 - column, 1.0)
        keep_rows[x * 16 : (x + 1) * 16, :] = keep
        if x == 0:
            message[96:112, :] = keep
            message[112:120, :] = jnp.broadcast_to(owner[...].astype(F32), (8, 128))
            for c in range(3):
                message[c * 16 : (c + 1) * 16, :] = keep * direction[c, 0]
                message[48 + c * 16 : 48 + (c + 1) * 16, :] = state[c, 0]
    for i in range(count - 3, count):
        copies[i].wait()
    weighting[...] = exact(exact(quad_y[...], stiffness[...]), quad_z[...])
    for i in range(2, count - 6):
        copies[i].wait()
    for write in writes:
        write.wait()


def part(ref, b):
    return ref.at[b * 288 : (b + 1) * 288]


def prepare(kept, used):
    operands = list(kept) + list(used)
    far = pl.BlockSpec(memory_space=pltpu.HBM)
    vmem = pl.BlockSpec(memory_space=pltpu.VMEM)
    made = [(120, 128), (64, 128), (576, 128), (ROWS, WIDE)]
    outs = [pltpu.VMEM(s, F32) for s in made] + [pltpu.VMEM(x.shape, x.dtype) for x in kept]
    outs[2] = jax.ShapeDtypeStruct(made[2], F32)
    return pl.pallas_call(
        functools.partial(prepare_body, len(operands)),
        out_shape=outs,
        in_specs=[far] * len(operands),
        out_specs=[vmem, vmem, far] + [vmem] * (len(outs) - 3),
        scratch_shapes=[pltpu.VMEM(x.shape, x.dtype) for x in used]
        + [pltpu.VMEM((2, 384, 128), F32), pltpu.VMEM((576, 128), F32)]
        + [pltpu.SemaphoreType.DMA((len(operands) + 2,))],
        compiler_params=pltpu.CompilerParams(vmem_limit_bytes=24 * 2**20),
    )(*[pltpu.with_memory_space_constraint(x, pltpu.HBM) for x in operands])


def gradients(fields, along, grads, refs):
    lines = jnp.concatenate([f for field in fields for f in field], axis=0)
    flat = dot(beside(lines), thrice(along))
    for i, ref in enumerate(refs):
        parts = [flat[(3 * i + c) * NODES : (3 * i + c + 1) * NODES] for c in range(3)]
        plain = jnp.concatenate([p[:, :WIDE] for p in parts], axis=1)
        sloped = jnp.concatenate([p[:, WIDE:] for p in parts], axis=1)
        ref[0 : 2 * ROWS, :] = dot(grads[0 : 2 * ROWS, :], under(plain))
        ref[2 * ROWS :, :] = dot(grads[2 * ROWS :, :], under(sloped))


def physics(state_grad, grad, weighting, stress, flux, fresh):
    pairs = ((0, 0), (1, 1), (2, 2), (0, 1), (0, 2), (1, 2))
    for start in range(0, LIVE, 8):
        here = slice(start, start + 8)
        w = weighting[here, :]

        def piece(ref, c, a):
            return ref[a * ROWS + start : a * ROWS + start + 8, c * WIDE : (c + 1) * WIDE]

        deform = [
            [piece(state_grad, c, a) + (1.0 if a == c else 0.0) for a in range(3)]
            for c in range(3)
        ]
        change = [[piece(grad, c, a) for a in range(3)] for c in range(3)]
        if fresh:
            square = {
                (a, b): deform[0][a] * deform[0][b]
                + deform[1][a] * deform[1][b]
                + deform[2][a] * deform[2][b]
                for a, b in pairs
            }
            shift = 0.6 * (square[0, 0] + square[1, 1] + square[2, 2] - 3.0)
            held = {
                (a, b): w * (0.8 * (square[a, b] - 1.0) + shift) if a == b else (0.8 * w) * square[a, b]
                for a, b in pairs
            }
            for i, pair in enumerate(pairs):
                stress[i, here, :] = held[pair]
        else:
            held = {pair: stress[i, here, :] for i, pair in enumerate(pairs)}
        cross = [
            [
                deform[0][a] * change[0][b] + deform[1][a] * change[1][b] + deform[2][a] * change[2][b]
                for b in range(3)
            ]
            for a in range(3)
        ]
        trace = (1.2 * w) * (cross[0][0] + cross[1][1] + cross[2][2])
        moved = {}
        for a, b in pairs:
            if a == b:
                moved[a, b] = (1.6 * w) * cross[a][b] + trace
            else:
                moved[a, b] = (0.8 * w) * (cross[a][b] + cross[b][a])
        for a in range(3):
            for c in range(3):
                entry = None
                for b in range(3):
                    key = (min(a, b), max(a, b))
                    term = change[c][b] * held[key] + deform[c][b] * moved[key]
                    entry = term if entry is None else entry + term
                flux[a * ROWS + start : a * ROWS + start + 8, c * WIDE : (c + 1) * WIDE] = entry
    for a in range(3):
        flux[a * ROWS + LIVE : (a + 1) * ROWS, :] = jnp.zeros((ROWS - LIVE, 3 * WIDE), F32)


def images(flux, back_xy, back_z, back_along):
    side_b = dot(back_xy[...], under(flux[0 : 2 * ROWS, :]))
    side_d = dot(back_z[...], under(flux[2 * ROWS :, :]))
    lines = jnp.concatenate(
        [
            jnp.concatenate(
                [side_b[:, c * WIDE : (c + 1) * WIDE], side_d[:, c * WIDE : (c + 1) * WIDE]], axis=1
            )
            for c in range(3)
        ],
        axis=0,
    )
    return dot(beside(lines), thrice(back_along))


def coarse_rows(extended, rest):
    levels = dot(rest[...], under(jnp.concatenate(extended, axis=1)))
    return jnp.concatenate([levels[:8, c * 128 : (c + 1) * 128] for c in range(3)], axis=0)


def own_rows(ref, c):
    return ref[c].reshape(64, 128)


def first_body(
    state, direction, rhs, keep_rows, halo, weighting, along, grads, back_xy, back_z, back_along,
    rest, hat_down, hat_up, fold, spread, owner, state_grad, stress, sums, grad, flux,
):
    keep = keep_rows[...]
    fields = [
        [jnp.concatenate([own_rows(state, c), halo[48 + c * 16 : 64 + c * 16, :]], axis=0) for c in range(3)],
        [
            jnp.concatenate([keep * own_rows(direction, c), halo[c * 16 : 16 + c * 16, :]], axis=0)
            for c in range(3)
        ],
    ]
    gradients(fields, along, grads, (state_grad, grad))
    physics(state_grad, grad, weighting, stress, flux, True)
    image = images(flux, back_xy, back_z, back_along)
    keep_right = halo[96:112, :]
    extended = []
    for c in range(3):
        part = image[c * NODES : (c + 1) * NODES]
        own = own_rows(rhs, c) - keep * part[:64] - (1.0 - keep) * own_rows(direction, c)
        extended.append(jnp.concatenate([own, -keep_right * part[64:]], axis=0))
    levels = dot(beside(coarse_rows(extended, rest)), thrice(hat_down))
    row = lax.broadcasted_iota(jnp.int32, (24, 128), 0)
    lane = lax.broadcasted_iota(jnp.int32, (24, 128), 1)
    levels = jnp.where(lane // EZ == row % EY, levels, 0.0)
    levels = dot(fold[...], jnp.concatenate(split(levels), axis=0))[0:8]
    sums[0:4, :] = placed(levels, owner[...])[0:4]
    sums[4:8, :] = placed(levels, halo[112:113, :].astype(jnp.int32))[4:8]


def slots(owner):
    place = (owner % 2) * 64 + owner // 2
    return (lax.broadcasted_iota(jnp.int32, (128, 128), 0) == place).astype(BF16)


def placed(rows, owner):
    where = slots(owner)
    nt = (((1,), (1,)), ((), ()))
    return sum(lax.dot_general(part, where, nt, preferred_element_type=F32) for part in split(rows))


def solve_body(gathered, rows, owner, correction):
    tn = (((0,), (0,)), ((), ()))
    values = gathered[...]
    row = lax.broadcasted_iota(jnp.int32, (256, 256), 0)
    lane = lax.broadcasted_iota(jnp.int32, (256, 256), 1)
    side = lax.axis_index("grp") // 32
    holder = row // 8
    target = jnp.where(row % 8 < 4, holder, holder + 1 - jnp.where(holder % 8 == 7, 8 * side, 0))
    column = jnp.where(lane < 192, lane, lane - 64)
    match = (target == column % 64 // 2) & (row % 4 == column // 64)
    need = None
    for q in range(2):
        pick = (match & (column % 2 == q)).astype(BF16)
        for part in split(values[:, q * 64 : (q + 1) * 64]):
            term = lax.dot_general(part, pick, tn, preferred_element_type=F32)
            need = term if need is None else need + term
    low = lax.broadcasted_iota(jnp.int32, (64, 128), 1) < 64
    inner, outer = need[:, 0:128], need[:, 128:256]
    products = [[], []]
    for c in range(3):
        shared = rows[pl.ds(c * 3 + 1, 64, stride=9), :] * outer
        for q in range(2):
            own = rows[pl.ds(c * 3 + 2 * q, 64, stride=9), :] * inner
            products[q].append(own + jnp.where(low == (q == 0), shared, 0.0))
    products = products[0] + products[1]
    ones = jnp.ones((128, 128), BF16)
    sums = sum(dot(part, ones) for part in split(jnp.concatenate(products, axis=0)))
    lane = lax.broadcasted_iota(jnp.int32, (64, 128), 1)
    stacked = []
    for q in range(2):
        first, second, third = [sums[(q * 3 + c) * 64 : (q * 3 + c + 1) * 64] for c in range(3)]
        stacked.append(jnp.where(lane == 0, first, jnp.where(lane == 1, second, third)))
    stacked = jnp.concatenate(stacked, axis=0)[:, 0:8]
    where = slots(owner[...])
    correction[...] = sum(
        lax.dot_general(part, where, tn, preferred_element_type=F32) for part in split(stacked)
    )


def second_body(
    correction, right, state_grad, stress, direction, rhs, keep_rows, halo, weighting, along, grads,
    back_xy, back_z, back_along, rest, hat_down, hat_up, fold, spread, new, partial, message,
    own_coarse, grad, flux,
):
    keep = keep_rows[...]
    keep_right = halo[96:112, :]
    rows = jnp.concatenate(
        [
            jnp.broadcast_to(ref[c : c + 1, :], (4, 128))
            for c in range(3)
            for ref in (correction, right)
        ],
        axis=0,
    )
    row = lax.broadcasted_iota(jnp.int32, (24, 128), 0)
    lane = lax.broadcasted_iota(jnp.int32, (24, 128), 1)
    levels = dot(beside(jnp.where(lane // EZ == row % EY, rows, 0.0)), thrice(hat_up))
    levels = jnp.concatenate([levels[c * 8 : (c + 1) * 8] for c in range(3)], axis=1)
    update = dot(spread[...], under(levels))
    field = []
    fresh = []
    for c in range(3):
        piece = update[:, c * 128 : (c + 1) * 128]
        own = own_rows(direction, c) + keep * piece[:64]
        new[c] = own.reshape(4, 16, 128)
        fresh.append(own)
        field.append(
            jnp.concatenate(
                [keep * own, halo[c * 16 : 16 + c * 16, :] + keep_right * piece[64:]], axis=0
            )
        )
    gradients([field], along, grads, (grad,))
    physics(state_grad, grad, weighting, stress, flux, False)
    image = images(flux, back_xy, back_z, back_along)
    extended = []
    for c in range(3):
        part = image[c * NODES : (c + 1) * NODES]
        own = own_rows(rhs, c) - keep * part[:64] - (1.0 - keep) * fresh[c]
        last = -keep_right * part[64:]
        partial[c] = own.reshape(4, 16, 128)
        message[c * 16 : (c + 1) * 16, :] = last
        extended.append(jnp.concatenate([own, last], axis=0))
    levels = dot(beside(coarse_rows(extended, rest)), thrice(hat_down))
    message[48:72, :] = levels
    for c in range(3):
        own_coarse[c] = levels[c * 8 : c * 8 + 4, :EZ]


def finish_body(partial, arrived, own_coarse, residual, coarse):
    for c in range(3):
        residual[c, 0] = partial[c, 0] + arrived[c * 16 : (c + 1) * 16, :]
        residual[c, 1:4] = partial[c, 1:4]
        coarse[c] = own_coarse[c] + arrived[52 + c * 8 : 56 + c * 8, :EZ]


def finish(partial, arrived, own_coarse):
    vmem = pl.BlockSpec(memory_space=pltpu.VMEM)
    return pl.pallas_call(
        finish_body,
        out_shape=[
            jax.ShapeDtypeStruct((3, 4, 16, 128), F32),
            jax.ShapeDtypeStruct((3, EY, EZ), F32),
        ],
        in_specs=[vmem] * 3,
        out_specs=[vmem] * 2,
        compiler_params=pltpu.CompilerParams(vmem_limit_bytes=24 * 2**20),
    )(near(partial), near(arrived), near(own_coarse))


def shifted(block, distance):
    axes = ("grp", "mem")
    count = lax.axis_size(axes)
    route = [(i - distance, i) for i in range(count) if 0 <= i - distance < count]
    return lax.ppermute(block, axes, route)


def ring():
    groups, members = lax.axis_size("grp"), lax.axis_size("mem")
    route = []
    for g in range(groups):
        route += [(g * members + m, g * members + m + 1) for m in range(members - 1)]
        last = g >= groups // 2 - 1 and g % 8 == 7
        to = g + 8 if last else g
        if to < groups:
            route.append((g * members + members - 1, to * members))
    return route


def shards(state, direction, rhs, clamp, stiffness, coarse_owner, coarse_inverse):
    k = constants()
    names = ("along", "grads", "back_xy", "back_z", "back_along", "rest", "hat_down", "hat_up", "fold", "spread")
    kept = [state, direction, rhs] + [jnp.asarray(k[name]) for name in names] + [coarse_owner]
    inverse = coarse_inverse.reshape(384, 192)
    used = [
        clamp, coarse_owner, inverse, stiffness[0],
        jnp.asarray(k["quad_y"]), jnp.asarray(k["quad_z"]),
    ]
    message, keep_rows, rows, weighting, state, direction, rhs, *shared, owner = prepare(kept, used)
    halo = shifted(message, -1)
    rows = lax.all_to_all(
        rows.reshape(576, 1, 128), "grp", split_axis=0, concat_axis=0, tiled=True
    ).reshape(576, 128)
    big = (3 * ROWS, 3 * WIDE)
    scratch = (pltpu.VMEM(big, F32), pltpu.VMEM(big, F32))
    state_grad, stress, sums = call(
        first_body,
        [big, (6, LIVE, WIDE), (8, 128)],
        state, direction, rhs, keep_rows, halo, weighting, *shared, owner,
        scratch=scratch, cost=None,
    )
    arrived = lax.ppermute(sums, ("grp", "mem"), ring())[4:8]
    wraps = lax.axis_index("mem") == 0
    total = jnp.concatenate(
        [sums[0:4] + jnp.where(wraps, 0.0, arrived), jnp.where(wraps, arrived, 0.0)], axis=0
    )
    total = jnp.broadcast_to(total[None], (32, 8, 128)).reshape(256, 128)
    total, rows = lax.optimization_barrier((total, rows))
    sides = [list(range(32)), list(range(32, 64))]
    gathered = lax.all_to_all(
        total, "grp", split_axis=0, concat_axis=0, tiled=True, axis_index_groups=sides
    )
    (correction,) = call(solve_body, [(8, 128)], gathered, rows, owner)
    right = shifted(correction, -1)
    field = (3, 4, 16, 128)
    new, partial, last, own_coarse = call(
        second_body,
        [field, field, (72, 128), (3, EY, EZ)],
        correction, right, state_grad, stress, direction, rhs, keep_rows, halo, weighting, *shared,
        scratch=scratch,
    )
    residual, coarse = finish(partial, shifted(last, 1), own_coarse)
    return new, residual, coarse[:, None]


def solution(mesh):
    along = ("grp", "mem")
    field = P(None, along, None, None)
    in_specs = (
        field, field, field, P(along, None), P(along, None, None), P(along, None),
        P(along, None, None, None),
    )
    return jax.shard_map(
        shards, mesh=mesh, in_specs=in_specs, out_specs=(field, field, field), check_vma=False
    )
```
